32 devices in a mesh: fsdp: 2 (over x), ctx: 4 (over z), tp: 4 (over y, core).
Axes of the slice: x: 2, y: 2, z: 4, core: 2. Of those that a mesh axis runs over, the one named last changes fastest.
Arguments:
- tokens: bfloat16 [4, 1024, 2048], P('fsdp', 'ctx'), may hold values from -36 to 36
- cotangent: bfloat16 [4, 1024, 2048], P('fsdp', 'ctx'), may hold values from -9 to 9
- lengths: int32 [4, 2], P('fsdp'), may hold values from 1 to 768, 1024 in all within a row
- deal: int32 [4, 1024], P('fsdp'), may hold values from 0 to 1023, each once within a row
- att_proj: float32 [3, 2048, 2048], P(None, ('fsdp', 'ctx'), 'tp'), may hold values from -0.125 to 0.125
- attn_out: float32 [2048, 2048], P(('fsdp', 'ctx'), 'tp'), may hold values from -0.75 to 0.75
- ff_proj: float32 [2, 2048, 8192], P(None, ('fsdp', 'ctx'), 'tp'), may hold values from -0.125 to 0.125
- ff_out: float32 [2048, 8192], P(('fsdp', 'ctx'), 'tp'), may hold values from -0.0625 to 0.0625
- att_proj_first: float32 [3, 2048, 2048], P(None, ('fsdp', 'ctx'), 'tp')
- attn_out_first: float32 [2048, 2048], P(('fsdp', 'ctx'), 'tp')
- ff_proj_first: float32 [2, 2048, 8192], P(None, ('fsdp', 'ctx'), 'tp')
- ff_out_first: float32 [2048, 8192], P(('fsdp', 'ctx'), 'tp')
- att_proj_second: float32 [3, 2048, 2048], P(None, ('fsdp', 'ctx'), 'tp'), as said below
- attn_out_second: float32 [2048, 2048], P(('fsdp', 'ctx'), 'tp'), as said below
- ff_proj_second: float32 [2, 2048, 8192], P(None, ('fsdp', 'ctx'), 'tp'), as said below
- ff_out_second: float32 [2048, 8192], P(('fsdp', 'ctx'), 'tp'), as said below
Outputs:
- block_out: bfloat16 [4, 1024, 2048], P('fsdp', 'ctx')
- input_grad: float32 [4, 1024, 2048], P('fsdp', 'ctx')
- grad_norm: float32 [1], replicated
- att_proj_grad: float32 [3, 2048, 2048], P(None, ('fsdp', 'ctx'), 'tp')
- attn_out_grad: float32 [2048, 2048], P(('fsdp', 'ctx'), 'tp')
- ff_proj_grad: float32 [2, 2048, 8192], P(None, ('fsdp', 'ctx'), 'tp')
- ff_out_grad: float32 [2048, 8192], P(('fsdp', 'ctx'), 'tp')
- att_proj_first_new: float32 [3, 2048, 2048], P(None, ('fsdp', 'ctx'), 'tp')
- attn_out_first_new: float32 [2048, 2048], P(('fsdp', 'ctx'), 'tp')
- ff_proj_first_new: float32 [2, 2048, 8192], P(None, ('fsdp', 'ctx'), 'tp')
- ff_out_first_new: float32 [2048, 8192], P(('fsdp', 'ctx'), 'tp')
- att_proj_second_new: float32 [3, 2048, 2048], P(None, ('fsdp', 'ctx'), 'tp')
- attn_out_second_new: float32 [2048, 2048], P(('fsdp', 'ctx'), 'tp')
- ff_proj_second_new: float32 [2, 2048, 8192], P(None, ('fsdp', 'ctx'), 'tp')
- ff_out_second_new: float32 [2048, 8192], P(('fsdp', 'ctx'), 'tp')
- att_proj_new: float32 [3, 2048, 2048], P(None, ('fsdp', 'ctx'), 'tp')
- attn_out_new: float32 [2048, 2048], P(('fsdp', 'ctx'), 'tp')
- ff_proj_new: float32 [2, 2048, 8192], P(None, ('fsdp', 'ctx'), 'tp')
- ff_out_new: float32 [2048, 8192], P(('fsdp', 'ctx'), 'tp')
- att_proj_low: bfloat16 [3, 2048, 2048], P(None, ('fsdp', 'ctx'), 'tp')
- attn_out_low: bfloat16 [2048, 2048], P(('fsdp', 'ctx'), 'tp')
- ff_proj_low: bfloat16 [2, 2048, 8192], P(None, ('fsdp', 'ctx'), 'tp')
- ff_out_low: bfloat16 [2048, 8192], P(('fsdp', 'ctx'), 'tp')
The draws below stay inside these ranges and needn't reach their ends.
Inputs may be any that keep to these rules, and one draw needn't show every extreme that they name: `lengths`: each row sums to 1024 and no entry exceeds 768. `deal`: each row is a permutation of the positions of its pack. `att_proj_second`: every entry is positive. `attn_out_second`: every entry is positive. `ff_proj_second`: every entry is positive. `ff_out_second`: every entry is positive.
All inputs are finite; a program needn't handle non-finite values.
Results may differ from the reference program's by a relative error of at most 0.017.
Values may be sent and summed in bfloat16 or wider, within the bound.
A program may use at most 320 MiB of HBM per device.

```python
import math
import jax
import jax.numpy as jnp
import numpy as np
from jax import lax

D = 2048
HEADS = 16
HEAD_DIM = 128
FF = 8192
SEQS = 2
STEP = 10
PACK_LEN = 1024
LONGEST = 768
PACKS = 4


def grad_size(factor):
    return factor / math.sqrt(3.0 * D * D + 0.54 * D * FF)


def first_draw(key, dims, factor):
    return jax.random.truncated_normal(key, -3.0, 3.0, dims, jnp.float32) * (0.111 * grad_size(factor))


def second_draw(key, dims, factor):
    spread = jax.random.uniform(key, dims, jnp.float32, 0.0, math.log(4.0))
    return jnp.exp(spread) * (0.0526 * grad_size(factor) ** 2)


def draw_tokens(key, part):
    key_entry, key_rows = jax.random.split(key)
    column_place = jnp.arange(D, dtype=jnp.float32) / D
    entries = jax.random.truncated_normal(key_entry, -5.0, 5.0, (PACKS, PACK_LEN, D), jnp.float32)
    row_scale = jnp.exp(jax.random.uniform(key_rows, (PACKS, PACK_LEN, 1), jnp.float32, math.log(0.5), math.log(5.0)))
    column_scale = jnp.exp(math.log(2.0) * (column_place - 0.5))
    return (entries * row_scale * column_scale).astype(jnp.bfloat16)


def draw_cotangent(key, part):
    key_entry = jax.random.fold_in(key, 0)
    column_place = jnp.arange(D, dtype=jnp.float32) / D
    entries = jax.random.truncated_normal(key_entry, -5.0, 5.0, (PACKS, PACK_LEN, D), jnp.float32)
    column_scale = jnp.exp(math.log(2.0) * (column_place - 0.5))
    return (entries * column_scale).astype(jnp.bfloat16)


def draw_att_proj_first(key, part):
    return first_draw(key, (3, D, D), 1.0)


def draw_attn_out_first(key, part):
    return first_draw(key, (D, D), 0.15)


def draw_ff_proj_first(key, part):
    return first_draw(key, (2, D, FF), 0.3)


def draw_ff_out_first(key, part):
    return first_draw(key, (D, FF), 0.6)


def draw_att_proj_second(key, part):
    return second_draw(key, (3, D, D), 1.0)


def draw_attn_out_second(key, part):
    return second_draw(key, (D, D), 0.15)


def draw_ff_proj_second(key, part):
    return second_draw(key, (2, D, FF), 0.3)


def draw_ff_out_second(key, part):
    return second_draw(key, (D, FF), 0.6)


def levels(stream_key, shape, cuts, least, largest):
    loudness = 1.0
    for axis_at, shards_of in cuts:
        steps = jax.random.uniform(jax.random.fold_in(jax.random.fold_in(stream_key, 6), axis_at), (shards_of,), jnp.float32, least / len(cuts), largest / len(cuts))
        loudness = loudness * jnp.repeat(jnp.exp(steps), shape[axis_at] // shards_of).reshape((-1,) + (1,) * (len(shape) - 1 - axis_at))
    return loudness


def split_up(count, total, bound, lean):
    portions = [(1 << 20) // math.isqrt(grade ** lean) + 1 for grade in range(2, count + 1)]
    rest, counts = total - bound - (count - 1), [1] * (count - 1)
    while rest > 0:
        movable = [i for i in range(count - 1) if counts[i] < bound]
        mass, left = sum([portions[i] for i in movable]), rest
        for i in movable:
            extra = min(bound - counts[i], max(1, left * portions[i] // mass), rest)
            counts[i] = counts[i] + extra
            rest = rest - extra
    return np.array([bound] + counts)


def uneven_parts(own_key, number_of, total, bound, slope):
    if number_of == 2:
        one = jax.random.randint(own_key, (), max(1, total - bound), min(bound, total - 1) + 1)
        return jnp.stack([one, total - one])
    sizes = jnp.asarray(split_up(number_of, total, bound, slope), jnp.int32)
    pairs = (number_of - 1) // 2
    donor, receiver = sizes[1:1 + 2 * pairs:2], sizes[2:2 + 2 * pairs:2]
    margin = jnp.minimum(donor - 1, bound - receiver)
    moved = jax.random.randint(jax.random.fold_in(own_key, 1), (pairs,), 0, 1 << 20) % (margin + 1)
    sizes = sizes.at[1:1 + 2 * pairs:2].set(donor - moved).at[2:2 + 2 * pairs:2].set(receiver + moved)
    return sizes[jax.random.permutation(jax.random.fold_in(own_key, 2), number_of)]


def noise(rng, extent, scale, limit, cuts=(), held_as=jnp.bfloat16):
    factor_of = levels(rng, extent, cuts, -0.22, 0.18) if cuts else 1.0
    values = jax.random.normal(rng, extent, jnp.float32) * scale * factor_of
    return jnp.minimum(jnp.maximum(values, -limit), limit).astype(held_as)


def setup_inputs(seed: int = 0) -> dict:
    key_list = jax.random.split(jax.random.key(seed), 17)
    return {
        "tokens": draw_tokens(jax.random.fold_in(key_list[16], 71), 0),
        "cotangent": draw_cotangent(jax.random.fold_in(key_list[16], 71), 0),
        "lengths": jax.vmap(lambda own: uneven_parts(own, SEQS, PACK_LEN, LONGEST, 1))(jax.random.split(key_list[2], PACKS)).reshape((PACKS, SEQS)).astype(jnp.int32),
        "deal": jax.vmap(lambda own: jax.random.permutation(own, PACK_LEN))(jax.random.split(key_list[3], PACKS)).reshape((PACKS, PACK_LEN)).astype(jnp.int32),
        "att_proj": noise(key_list[4], (3, D, D), D ** -0.5, 0.125, ((1, 8), (2, 4)), jnp.float32),
        "attn_out": noise(key_list[5], (D, D), (D // 32) ** -0.5, 0.75, ((0, 8), (1, 4)), jnp.float32),
        "ff_proj": noise(key_list[6], (2, D, FF), D ** -0.5, 0.125, ((1, 8), (2, 4)), jnp.float32),
        "ff_out": noise(key_list[7], (D, FF), FF ** -0.5, 0.0625, ((0, 8), (1, 4)), jnp.float32),
        "att_proj_first": draw_att_proj_first(jax.random.fold_in(key_list[16], 71), 0),
        "attn_out_first": draw_attn_out_first(jax.random.fold_in(key_list[16], 71), 0),
        "ff_proj_first": draw_ff_proj_first(jax.random.fold_in(key_list[16], 71), 0),
        "ff_out_first": draw_ff_out_first(jax.random.fold_in(key_list[16], 71), 0),
        "att_proj_second": draw_att_proj_second(jax.random.fold_in(key_list[16], 71), 0),
        "attn_out_second": draw_attn_out_second(jax.random.fold_in(key_list[16], 71), 0),
        "ff_proj_second": draw_ff_proj_second(jax.random.fold_in(key_list[16], 71), 0),
        "ff_out_second": draw_ff_out_second(jax.random.fold_in(key_list[16], 71), 0),
    }


@jax.custom_vjp
def low(v):
    return lax.optimization_barrier(v.astype(jnp.bfloat16)).astype(jnp.float32)

@jax.custom_vjp
def low_back(v):
    return v

def low_keep(v):
    return (low(v), None)

def low_pass(kept, grad):
    return (grad,)

def back_keep(v):
    return (v, None)

def back_low(kept, grad):
    return (low(grad),)
low.defvjp(low_keep, low_pass)
low_back.defvjp(back_keep, back_low)
EPS_NORM = 1e-05
BETA_ONE = 0.9
BETA_TWO = 0.95
EPS_ADAM = 1e-08
DECAY = 0.1
MAX_NORM = 1.0
NEG_FILL = -1e+30
HIGHEST = lax.Precision.HIGHEST

def layer_norm(values):
    centre = values - lax.optimization_barrier(jnp.mean(values, axis=-1, keepdims=True))
    spread = lax.optimization_barrier(jnp.mean(centre * centre, axis=-1, keepdims=True))
    return centre * lax.rsqrt(spread + EPS_NORM)

def rotary(values, cos_table, sine_table):
    half_dim = values.shape[-1] // 2
    turned = jnp.concatenate([-values[..., half_dim:], values[..., :half_dim]], axis=-1)
    return values * cos_table + turned * sine_table

def rope_tables(places):
    freq_steps = jnp.arange(HEAD_DIM // 2, dtype=jnp.float32)
    inverse = jnp.power(10000.0, -2.0 * freq_steps / HEAD_DIM)
    angles = places.astype(jnp.float32)[:, None] * inverse[None, :]
    doubled = jnp.concatenate([angles, angles], axis=1)
    return (jnp.cos(doubled)[:, None, :], jnp.sin(doubled)[:, None, :])

def first_positions(deal_row, length_row):
    seq_ends = jnp.cumsum(length_row).astype(jnp.int32)
    starts = (seq_ends - length_row).astype(jnp.int32)
    inside = (deal_row[:, None] >= starts[None, :]) & (deal_row[:, None] < seq_ends[None, :])
    return lax.optimization_barrier(jnp.sum(jnp.where(inside, starts[None, :], 0), axis=1)).astype(jnp.int32)

def swiglu(gate_up):
    return gate_up[1] * jax.nn.sigmoid(gate_up[1]) * gate_up[0]

def adam_step(weight, grad_sum, first, second, clip_factor, learn_rate):
    clipped = grad_sum * clip_factor
    first_new = BETA_ONE * first + (1.0 - BETA_ONE) * clipped
    second_new = BETA_TWO * second + (1.0 - BETA_TWO) * clipped * clipped
    first_hat = first_new / (1.0 - BETA_ONE ** STEP)
    second_hat = second_new / (1.0 - BETA_TWO ** STEP)
    weight_new = weight - learn_rate * (first_hat / (jnp.sqrt(second_hat) + EPS_ADAM) + DECAY * weight)
    return (first_new, second_new, weight_new)

def block_forward(resid_in, att_w, out_w, proj_w, down_w, deal_row, length_row):
    pack_len = resid_in.shape[0]
    score_scale = HEAD_DIM ** (-0.5)
    att_w = low(att_w)
    out_w = low(out_w)
    proj_w = low(proj_w)
    down_w = low(down_w)
    key_first = first_positions(deal_row, length_row)
    cos_table, sine_table = rope_tables(deal_row - key_first)
    act_one = low(layer_norm(resid_in))
    joint_qkv = low_back(jnp.einsum('td,cdf->ctf', act_one, att_w, precision=HIGHEST))
    query_low = low(rotary(joint_qkv[0].reshape(pack_len, HEADS, HEAD_DIM), cos_table, sine_table))
    key_low = low(rotary(joint_qkv[1].reshape(pack_len, HEADS, HEAD_DIM), cos_table, sine_table))
    value_low = low(joint_qkv[2].reshape(pack_len, HEADS, HEAD_DIM))
    block_rows = min(512, pack_len)
    block_count = pack_len // block_rows

    def attend(block_args):
        query_part, place_part, first_part = block_args
        raw_scores = jnp.einsum('thd,khd->htk', query_part, key_low, precision=HIGHEST) * score_scale
        allowed = (deal_row[None, :] <= place_part[:, None]) & (deal_row[None, :] >= first_part[:, None])
        scores = low_back(jnp.where(allowed[None], raw_scores, NEG_FILL))
        row_peak = lax.optimization_barrier(jnp.max(scores, axis=2, keepdims=True))
        exp_scores = jnp.exp(scores - row_peak)
        probs = low(exp_scores / lax.optimization_barrier(jnp.sum(exp_scores, axis=2, keepdims=True)))
        return jnp.einsum('htk,khd->thd', probs, value_low, precision=HIGHEST)
    attended = lax.map(jax.checkpoint(attend), (query_low.reshape(block_count, block_rows, HEADS, HEAD_DIM), deal_row.reshape(block_count, block_rows), key_first.reshape(block_count, block_rows)))
    attended_low = low_back(low(attended.reshape(pack_len, HEADS * HEAD_DIM)))
    attn_branch = low_back(jnp.einsum('tf,df->td', attended_low, out_w, precision=HIGHEST))
    resid_mid = resid_in + attn_branch
    act_two = low(layer_norm(resid_mid))
    gate_up = low_back(jnp.einsum('td,cdf->ctf', act_two, proj_w, precision=HIGHEST))
    hidden_low = low(swiglu(gate_up))
    return resid_mid + jnp.einsum('tf,df->td', hidden_low, down_w, precision=HIGHEST)

def reference(tokens, cotangent, lengths, deal, att_proj, attn_out, ff_proj, ff_out, att_proj_first, attn_out_first, ff_proj_first, ff_out_first, att_proj_second, attn_out_second, ff_proj_second, ff_out_second):
    masters = (att_proj, attn_out, ff_proj, ff_out)

    def one_pack(totals, packed):
        token_rows, cot_rows, length_row, deal_row = packed

        def forward(resid_in, att_w, out_w, proj_w, down_w):
            return block_forward(resid_in, att_w, out_w, proj_w, down_w, deal_row, length_row)
        block_value, pull_back = jax.vjp(forward, token_rows.astype(jnp.float32), att_proj, attn_out, ff_proj, ff_out)
        grads_all = pull_back(cot_rows.astype(jnp.float32))
        totals = tuple((total + new_grad for total, new_grad in zip(totals, grads_all[1:])))
        return (totals, (block_value.astype(jnp.bfloat16), grads_all[0]))
    start_sums = tuple((jnp.zeros_like(master) for master in masters))
    totals, (block_out, input_grad) = lax.scan(one_pack, start_sums, (tokens, cotangent, lengths, deal))
    squares = jnp.sum(totals[0] * totals[0]) + jnp.sum(totals[1] * totals[1]) + jnp.sum(totals[2] * totals[2]) + jnp.sum(totals[3] * totals[3])
    norm_value = jnp.sqrt(squares)
    clip_factor = jnp.minimum(1.0, MAX_NORM / (norm_value + 1e-06))
    base_rate = D ** (-0.5)
    out_rate = (D // 32) ** (-0.5)
    rates = (base_rate, out_rate, base_rate, base_rate)
    firsts = (att_proj_first, attn_out_first, ff_proj_first, ff_out_first)
    seconds = (att_proj_second, attn_out_second, ff_proj_second, ff_out_second)
    updated = [adam_step(masters[slot], totals[slot], firsts[slot], seconds[slot], clip_factor, rates[slot]) for slot in range(4)]
    return (block_out, input_grad, norm_value.reshape(1), totals[0], totals[1], totals[2], totals[3], updated[0][0], updated[1][0], updated[2][0], updated[3][0], updated[0][1], updated[1][1], updated[2][1], updated[3][1], updated[0][2], updated[1][2], updated[2][2], updated[3][2], updated[0][2].astype(jnp.bfloat16), updated[1][2].astype(jnp.bfloat16), updated[2][2].astype(jnp.bfloat16), updated[3][2].astype(jnp.bfloat16))
```

```python
import jax
import jax.numpy as jnp
from jax import lax
from jax.sharding import PartitionSpec as P

HEAD_DIM = 128
STEP = 10
EPS_NORM = 1e-05
BETA_ONE = 0.9
BETA_TWO = 0.95
EPS_ADAM = 1e-08
DECAY = 0.1
MAX_NORM = 1.0
NEG_FILL = -1e30
BF = jnp.bfloat16
F32 = jnp.float32


def mean_spread(values):
    centre = values - jnp.mean(values, axis=-1, keepdims=True)
    spread = jnp.mean(centre * centre, axis=-1, keepdims=True)
    scale = lax.rsqrt(spread + EPS_NORM)
    return centre * scale, scale


def norm_back(grad, normed, scale):
    return scale * (
        grad
        - jnp.mean(grad, axis=-1, keepdims=True)
        - normed * jnp.mean(grad * normed, axis=-1, keepdims=True)
    )


def dot(left, right, dims):
    return lax.dot_general(left, right, (dims, ((), ())), preferred_element_type=F32)


def adam_step(weight, grad_sum, first, second, clip_factor, learn_rate):
    clipped = grad_sum * clip_factor
    first_new = BETA_ONE * first + (1.0 - BETA_ONE) * clipped
    second_new = BETA_TWO * second + (1.0 - BETA_TWO) * clipped * clipped
    first_hat = first_new / (1.0 - BETA_ONE**STEP)
    second_hat = second_new / (1.0 - BETA_TWO**STEP)
    weight_new = weight - learn_rate * (
        first_hat / (jnp.sqrt(second_hat) + EPS_ADAM) + DECAY * weight
    )
    return (first_new, second_new, weight_new)


def make_shards(mesh):
    n_f, n_c, n_t = (mesh.shape[a] for a in ("fsdp", "ctx", "tp"))

    def by_ctx(block, shift):
        return lax.ppermute(block, "ctx", [(i, (i + shift) % n_c) for i in range(n_c)])

    def by_core(block):
        return lax.ppermute(block, "tp", [(i, i ^ 1) for i in range(n_t)])

    def by_pack(block, shift, other):
        pairs = [
            (f * n_t + t, ((f + shift) % n_f) * n_t + (t ^ (2 * other)))
            for f in range(n_f)
            for t in range(n_t)
        ]
        return lax.ppermute(block, ("fsdp", "tp"), pairs)

    def gather_rows(half):
        mine = jnp.stack([half] + [by_ctx(half, s) for s in range(1, n_c)])
        both = jnp.stack([mine, by_core(mine)], axis=1)
        return both.reshape(-1, half.shape[1])

    def scatter_rows(partial):
        width = partial.shape[1]
        split = partial.astype(BF).reshape(n_c, 2, -1, width)
        summed = split[:, 0].astype(F32) + by_core(split[:, 1]).astype(F32)
        sent = summed.astype(BF)
        total = summed[0]
        for j in range(1, n_c):
            total = total + by_ctx(sent[j], -j).astype(F32)
        return total

    def gather_weight(shard):
        swapped = lax.all_to_all(shard.astype(BF), "ctx", 2, 1, tiled=True)
        columns = []
        for other in range(2):
            parts = [
                swapped if (s == 0 and other == 0) else by_pack(swapped, s, other)
                for s in range(n_f)
            ]
            columns.append(jnp.concatenate(parts, axis=1))
        return jnp.concatenate(columns, axis=2)

    def scatter_grad(grad):
        count, height, width = grad.shape
        low = grad.astype(BF).reshape(count, n_f, height // n_f, 2, width // 2)
        total = grad.reshape(low.shape)[:, 0, :, 0]
        for other in range(2):
            for i in range(n_f):
                if i or other:
                    total = total + by_pack(low[:, i, :, other], -i, other).astype(F32)
        return lax.all_to_all(total.astype(BF), "ctx", 1, 2, tiled=True).astype(F32)

    def shards(
        tokens,
        cotangent,
        lengths,
        deal,
        att_proj,
        attn_out,
        ff_proj,
        ff_out,
        att_proj_first,
        attn_out_first,
        ff_proj_first,
        ff_out_first,
        att_proj_second,
        attn_out_second,
        ff_proj_second,
        ff_out_second,
    ):
        f_at, c_at, t_at = (lax.axis_index(a) for a in ("fsdp", "ctx", "tp"))
        pack_at, core_at = t_at // 2, t_at % 2
        packs, row_count, width = tokens.shape
        half = row_count // 2
        pack_len = deal.shape[1]
        score_scale = HEAD_DIM ** (-0.5)
        f_width = width // n_f

        def turned(rows):
            return jnp.concatenate(
                [
                    lax.dynamic_slice_in_dim(rows, ((f_at - i) % n_f) * f_width, f_width, 1)
                    for i in range(n_f)
                ],
                axis=1,
            )

        def own_rows(array):
            rows = array.reshape(packs * 2, half, width)
            return turned(lax.dynamic_index_in_dim(rows, t_at, 0, keepdims=False))

        own_tokens = own_rows(tokens)
        own_cot = own_rows(cotangent)
        att_w = gather_weight(jnp.concatenate([att_proj, attn_out[None]]))
        own_input = own_tokens.astype(F32)
        normed_one, scale_one = mean_spread(own_input)
        act_one = gather_rows(normed_one.astype(BF))

        deal_pack = lax.dynamic_index_in_dim(deal, pack_at, 0, keepdims=False)
        length_row = lax.dynamic_index_in_dim(lengths, pack_at, 0, keepdims=False)
        places = jnp.concatenate(
            [
                lax.dynamic_slice_in_dim(
                    deal_pack, ((c_at - j) % n_c) * row_count + ((core_at + h) % 2) * half, half
                )
                for j in range(n_c)
                for h in range(2)
            ]
        )
        seqs = lengths.shape[1]
        before = jnp.arange(seqs)[:, None] > jnp.arange(seqs)[None, :]
        starts = jnp.sum(jnp.where(before, length_row[None, :], 0), axis=1)
        inside = (places[:, None] >= starts[None, :]) & (
            places[:, None] < (starts + length_row)[None, :]
        )
        firsts = jnp.sum(jnp.where(inside, starts[None, :], 0), axis=1)
        allowed = (places[None, :] <= places[:, None]) & (places[None, :] >= firsts[:, None])
        freq_steps = jnp.arange(HEAD_DIM // 2, dtype=F32)
        inverse = jnp.power(10000.0, -2.0 * freq_steps / HEAD_DIM)
        angles = (places - firsts).astype(F32)[:, None] * inverse[None, :]
        cos_table, sine_table = jnp.cos(angles), jnp.sin(angles)

        def turn(values, sign):
            low, high = values[..., : HEAD_DIM // 2], values[..., HEAD_DIM // 2 :]
            sine = sign * sine_table[:, None, :]
            cos = cos_table[:, None, :]
            return jnp.concatenate([low * cos - high * sine, high * cos + low * sine], axis=-1)

        rank_width = att_w.shape[2]
        heads = rank_width // HEAD_DIM
        raw = [
            dot(act_one, att_w[i], ((1,), (0,))).reshape(pack_len, heads, HEAD_DIM)
            for i in range(3)
        ]
        query = turn(raw[0], 1.0).astype(BF)
        key = turn(raw[1], 1.0).astype(BF)
        value = raw[2].astype(BF)
        scores = (
            jnp.einsum("thd,khd->htk", query, key, preferred_element_type=F32) * score_scale
        )
        scores = jnp.where(allowed[None], scores, NEG_FILL)
        exp_scores = jnp.exp(scores - jnp.max(scores, axis=2, keepdims=True))
        probs = exp_scores / jnp.sum(exp_scores, axis=2, keepdims=True)
        probs_low = probs.astype(BF)
        attended = jnp.einsum("htk,khd->thd", probs_low, value, preferred_element_type=F32)
        attended_low = attended.reshape(pack_len, rank_width).astype(BF)
        out_part = dot(attended_low, att_w[3], ((1,), (1,)))
        resid_mid = own_input + scatter_rows(out_part)
        normed_two, scale_two = mean_spread(resid_mid)
        act_two = gather_rows(normed_two.astype(BF))

        ff_w = gather_weight(jnp.concatenate([ff_proj, ff_out[None]]))
        cot_rows = gather_rows(own_cot)
        up = dot(act_two, ff_w[0], ((1,), (0,)))
        gate = dot(act_two, ff_w[1], ((1,), (0,)))
        sigma = jax.nn.sigmoid(gate)
        hidden_low = (gate * sigma * up).astype(BF)
        hidden_grad = dot(cot_rows, ff_w[2], ((1,), (0,)))
        up_grad = (hidden_grad * gate * sigma).astype(BF)
        gate_grad = (hidden_grad * up * sigma * (1.0 + gate * (1.0 - sigma))).astype(BF)
        act_two_part = dot(up_grad, ff_w[0], ((1,), (1,))) + dot(gate_grad, ff_w[1], ((1,), (1,)))
        act_two_grad = scatter_rows(act_two_part)
        mid_grad = own_cot.astype(F32) + norm_back(act_two_grad, normed_two, scale_two)
        mid_rows = gather_rows(mid_grad.astype(BF))

        ff_branch = scatter_rows(dot(hidden_low, ff_w[2], ((1,), (1,))))
        block_rows = turned((resid_mid + ff_branch).astype(BF))
        block_out = lax.all_gather(block_rows, "tp", axis=0, tiled=True)
        ff_grad = jnp.stack(
            [
                dot(act_two, up_grad, ((0,), (0,))),
                dot(act_two, gate_grad, ((0,), (0,))),
                dot(cot_rows, hidden_low, ((0,), (0,))),
            ]
        )
        ff_total = scatter_grad(ff_grad)

        attended_grad = dot(mid_rows, att_w[3], ((1,), (0,))).astype(BF)
        attended_grad = attended_grad.reshape(pack_len, heads, HEAD_DIM)
        value_grad = jnp.einsum(
            "htk,thd->khd", probs_low, attended_grad, preferred_element_type=F32
        )
        prob_grad = jnp.einsum("thd,khd->htk", attended_grad, value, preferred_element_type=F32)
        delta_rows = jnp.sum(probs * prob_grad, axis=2, keepdims=True)
        score_grad = (probs * (prob_grad - delta_rows)).astype(BF)
        query_grad = (
            jnp.einsum("htk,khd->thd", score_grad, key, preferred_element_type=F32) * score_scale
        )
        key_grad = (
            jnp.einsum("htk,thd->khd", score_grad, query, preferred_element_type=F32)
            * score_scale
        )
        joint_grad = [
            part.reshape(pack_len, rank_width).astype(BF)
            for part in (turn(query_grad, -1.0), turn(key_grad, -1.0), value_grad)
        ]
        act_one_part = sum(dot(joint_grad[i], att_w[i], ((1,), (1,))) for i in range(3))
        act_one_grad = scatter_rows(act_one_part)
        input_rows = turned(norm_back(act_one_grad, normed_one, scale_one) + mid_grad)
        input_grad = lax.all_gather(input_rows, "tp", axis=0, tiled=True)
        att_grad = jnp.stack(
            [dot(act_one, part, ((0,), (0,))) for part in joint_grad]
            + [dot(mid_rows, attended_low, ((0,), (0,)))]
        )
        att_total = scatter_grad(att_grad)

        square_sum = lax.psum(
            jnp.sum(att_total * att_total) + jnp.sum(ff_total * ff_total), ("fsdp", "ctx", "tp")
        )
        norm_value = jnp.sqrt(square_sum)
        clip_factor = jnp.minimum(1.0, MAX_NORM / (norm_value + 1e-06))
        base_rate = width ** (-0.5)
        out_rate = (width // 32) ** (-0.5)
        grads = (att_total[:3], att_total[3], ff_total[:2], ff_total[2])
        weights = (att_proj, attn_out, ff_proj, ff_out)
        firsts_old = (att_proj_first, attn_out_first, ff_proj_first, ff_out_first)
        seconds_old = (att_proj_second, attn_out_second, ff_proj_second, ff_out_second)
        rates = (base_rate, out_rate, base_rate, base_rate)
        news = [
            adam_step(w, g, m, v, clip_factor, r)
            for w, g, m, v, r in zip(weights, grads, firsts_old, seconds_old, rates)
        ]
        return (
            block_out.reshape(tokens.shape),
            input_grad.reshape(tokens.shape),
            norm_value.reshape(1),
            *grads,
            *(n[0] for n in news),
            *(n[1] for n in news),
            *(n[2] for n in news),
            *(n[2].astype(BF) for n in news),
        )

    return shards


def solution(mesh):
    act = P("fsdp", "ctx", None)
    table = P("fsdp", None)
    cube = P(None, ("fsdp", "ctx"), "tp")
    flat = P(("fsdp", "ctx"), "tp")
    group = (cube, flat, cube, flat)
    in_specs = (act, act, table, table) + group * 3
    out_specs = (act, act, P()) + group * 5
    return jax.shard_map(
        make_shards(mesh), mesh=mesh, in_specs=in_specs, out_specs=out_specs, check_vma=False
    )
```

```python
import functools

import jax
import jax.numpy as jnp
from jax import lax
from jax.experimental import pallas as pl
from jax.experimental.pallas import tpu as pltpu
from jax.sharding import PartitionSpec as P

HEAD_DIM = 128
STEP = 10
EPS_NORM = 1e-05
BETA_ONE = 0.9
BETA_TWO = 0.95
EPS_ADAM = 1e-08
DECAY = 0.1
MAX_NORM = 1.0
NEG_FILL = -1e30
BF = jnp.bfloat16
F32 = jnp.float32
MESH = pl.DeviceIdType.MESH
ANY = pl.BlockSpec(memory_space=pl.ANY)
VMEM = pl.BlockSpec(memory_space=pltpu.VMEM)
ROWS = 16


def mean_spread(values):
    centre = values - jnp.mean(values, axis=-1, keepdims=True)
    spread = jnp.mean(centre * centre, axis=-1, keepdims=True)
    scale = lax.rsqrt(spread + EPS_NORM)
    return centre * scale, scale


def norm_back(grad, normed, scale):
    return scale * (
        grad
        - jnp.mean(grad, axis=-1, keepdims=True)
        - normed * jnp.mean(grad * normed, axis=-1, keepdims=True)
    )


def dot(left, right, dims):
    return lax.dot_general(left, right, (dims, ((), ())), preferred_element_type=F32)


def adam_step(weight, grad_sum, first, second, clip_factor, learn_rate):
    clipped = grad_sum * clip_factor
    first_new = BETA_ONE * first + (1.0 - BETA_ONE) * clipped
    second_new = BETA_TWO * second + (1.0 - BETA_TWO) * clipped * clipped
    first_hat = first_new / (1.0 - BETA_ONE**STEP)
    second_hat = second_new / (1.0 - BETA_TWO**STEP)
    weight_new = weight - learn_rate * (
        first_hat / (jnp.sqrt(second_hat) + EPS_ADAM) + DECAY * weight
    )
    return (first_new, second_new, weight_new)


class Place:
    def __init__(self, sizes):
        self.n_f, self.n_c, self.n_t = sizes
        self.f, self.c, self.t = (lax.axis_index(a) for a in ("fsdp", "ctx", "tp"))
        self.hi, self.lo = self.t // 2, lax.rem(self.t, 2)
        self.core = (self.f, self.c, self.t + 1 - 2 * self.lo)
        self.block = self.c * 2 + self.lo
        self.pairs = [(s, o) for o in range(2) for s in range(self.n_f) if s or o]

    def ctx(self, shift):
        return lax.rem(self.c + shift + self.n_c, self.n_c)

    def fsdp(self, shift):
        return lax.rem(self.f + shift + self.n_f, self.n_f)

    def other(self, o):
        return self.hi + o * (1 - 2 * self.hi)

    def z(self, shift):
        return (self.f, self.ctx(shift), self.t)

    def xy(self, shift, o):
        return (self.fsdp(shift), self.c, self.t + o * (2 - 4 * self.hi))

    def greet(self, peers):
        barrier = pltpu.get_barrier_semaphore()
        for peer in peers:
            pl.semaphore_signal(barrier, inc=1, device_id=peer, device_id_type=MESH)
        pl.semaphore_wait(barrier, len(peers))

    def all_z(self):
        return [self.z(s) for s in range(1, self.n_c)]

    def all_xy(self):
        return [self.xy(s, o) for s, o in self.pairs]


def remote(src, dst, send, recv, peer):
    return pltpu.make_async_remote_copy(
        src_ref=src, dst_ref=dst, send_sem=send, recv_sem=recv, device_id=peer, device_id_type=MESH
    )


def by_rows(count, step):
    @pl.loop(0, count // ROWS)
    def _(i):
        step(pl.ds(pl.multiple_of(i * ROWS, ROWS), ROWS))


class Gather:
    def __init__(self, at, src, out, send, recv, local):
        self.at, self.src, self.out, self.send, self.recv = at, src, out, send, recv
        self.local = pltpu.make_async_copy(src, out.at[at.block], local)
        self.far, self.near = [], []

    def start(self):
        at = self.at
        for s in range(1, at.n_c):
            copy = remote(
                self.src, self.out.at[at.block], self.send.at[s], self.recv.at[s], at.z(s)
            )
            copy.start()
            self.far.append(copy)
        copy = remote(
            self.src, self.out.at[at.block], self.send.at[0], self.recv.at[0], at.core
        )
        copy.start()
        self.near.append(copy)
        self.local.start()

    def forward(self):
        at = self.at
        for s in range(1, at.n_c):
            self.far[s - 1].wait_recv()
            block = self.out.at[at.ctx(-s) * 2 + at.lo]
            copy = remote(
                block, block, self.send.at[at.n_c + s], self.recv.at[at.n_c + s], at.core
            )
            copy.start()
            self.near.append(copy)

    def finish(self):
        for copy in self.far:
            copy.wait_send()
        for copy in self.near:
            copy.wait()
        self.local.wait()


def gather_sems(n_c):
    return [
        pltpu.SemaphoreType.DMA((2 * n_c,)),
        pltpu.SemaphoreType.DMA((2 * n_c,)),
        pltpu.SemaphoreType.DMA,
    ]


class Scatter:
    def __init__(self, at, partial, own, near, sent, got, send, recv, local):
        self.at, self.own, self.near, self.sent, self.got = at, own, near, sent, got
        self.send, self.recv = send, recv
        self.locals, self.cores, self.far = [], [], []
        for s in range(at.n_c):
            c = at.ctx(s)
            self.locals.append(
                pltpu.make_async_copy(partial.at[c * 2 + at.lo], own.at[s], local.at[s])
            )
            self.cores.append(
                remote(
                    partial.at[c * 2 + 1 - at.lo], near.at[s], send.at[s], recv.at[s], at.core
                )
            )

    def start(self):
        order = [*range(1, self.at.n_c), 0]
        for s in order:
            self.cores[s].start()
            self.locals[s].start()

    def pass_on(self):
        at = self.at
        for s in range(1, at.n_c):
            self.cores[s].wait_recv()
            self.locals[s].wait()

            def add(rows, s=s):
                self.sent[s - 1, rows] = (
                    self.own[s, rows].astype(F32) + self.near[s, rows].astype(F32)
                ).astype(BF)

            by_rows(self.own.shape[1], add)
            copy = remote(
                self.sent.at[s - 1],
                self.got.at[s - 1],
                self.send.at[at.n_c + s],
                self.recv.at[at.n_c + s],
                at.z(s),
            )
            copy.start()
            self.far.append(copy)
        self.cores[0].wait_recv()
        self.locals[0].wait()

    def arrive(self):
        for copy in self.far:
            copy.wait_recv()

    def total(self, rows):
        value = self.own[0, rows].astype(F32) + self.near[0, rows].astype(F32)
        for s in range(1, self.at.n_c):
            value = value + self.got[s - 1, rows].astype(F32)
        return value

    def finish(self):
        for copy in (*self.cores, *self.far):
            copy.wait_send()


def scatter_scratch(n_c, half, width):
    return [
        pltpu.VMEM((n_c, half, width), BF),
        pltpu.VMEM((n_c, half, width), BF),
        pltpu.VMEM((n_c - 1, half, width), BF),
        pltpu.VMEM((n_c - 1, half, width), BF),
        pltpu.SemaphoreType.DMA((2 * n_c,)),
        pltpu.SemaphoreType.DMA((2 * n_c,)),
        pltpu.SemaphoreType.DMA((n_c,)),
    ]


class Swap:
    def __init__(self, at, shard, full, send, recv, local):
        self.at = at
        rows, width = shard.shape[1], full.shape[3]
        here = pl.ds((at.f * at.n_c + at.c) * rows, rows)
        target = full.at[at.hi, :, here, :]

        def columns(c):
            return shard.at[:, :, pl.ds(pl.multiple_of(c * width, 128), width)]

        self.local = pltpu.make_async_copy(columns(at.c), target, local)
        self.far = [
            remote(columns(at.ctx(s)), target, send.at[s], recv.at[s], at.z(s))
            for s in range(1, at.n_c)
        ]

    def start(self):
        self.local.start()
        for copy in self.far:
            copy.start()

    def wait(self):
        self.local.wait()
        for copy in self.far:
            copy.wait()


class Spread:
    def __init__(self, at, full, send, recv):
        height = full.shape[2] // at.n_f
        part = full.at[at.hi, :, pl.ds(at.f * height, height), :]
        self.copies = [
            remote(part, part, send.at[i], recv.at[i], at.xy(s, o))
            for i, (s, o) in enumerate(at.pairs)
        ]

    def start(self):
        for copy in self.copies:
            copy.start()

    def wait(self):
        for copy in self.copies:
            copy.wait()


class Collect:
    def __init__(self, at, partial, got, send, recv):
        height = partial.shape[2] // at.n_f
        self.copies = []
        for i, (s, o) in enumerate(at.pairs):
            part = partial.at[at.other(o), :, pl.ds(at.fsdp(s) * height, height), :]
            self.copies.append(remote(part, got.at[i], send.at[i], recv.at[i], at.xy(s, o)))

    def start(self):
        for copy in self.copies:
            copy.start()

    def wait(self):
        for copy in self.copies:
            copy.wait()


class Return:
    def __init__(self, at, summed, shard, send, recv, local):
        rows, width = shard.shape[1], summed.shape[2]
        target = shard.at[:, :, pl.ds(pl.multiple_of(at.c * width, 128), width)]

        def part(c):
            return summed.at[:, pl.ds(pl.multiple_of(c * rows, rows), rows), :]

        self.local = pltpu.make_async_copy(part(at.c), target, local)
        self.far = [
            remote(part(at.ctx(s)), target, send.at[s], recv.at[s], at.z(s))
            for s in range(1, at.n_c)
        ]

    start = Swap.start
    wait = Swap.wait


def dma(count):
    return pltpu.SemaphoreType.DMA((count,))


def make_shards(mesh):
    sizes = tuple(mesh.shape[a] for a in ("fsdp", "ctx", "tp"))
    n_f, n_c, n_t = sizes
    pairs = 2 * n_f - 1

    def call(kernel, name, collective, outs, ins, out_specs, scratch, aliases=None, vmem=40):
        return pl.pallas_call(
            kernel,
            out_shape=outs,
            in_specs=ins,
            out_specs=out_specs,
            scratch_shapes=scratch,
            input_output_aliases=aliases or {},
            compiler_params=pltpu.CompilerParams(
                collective_id=collective, has_side_effects=True, vmem_limit_bytes=vmem << 20
            ),
            name=name,
        )

    def first_kernel(
        a1_ref, att_ref, ff_ref, rows_ref, attw_ref, ffw_ref, gs, gr, gl, s1, r1, l1, s2, r2, l2, s3, r3
    ):
        at = Place(sizes)
        at.greet([at.core, *at.all_z(), *at.all_xy()])
        gather = Gather(at, a1_ref, rows_ref, gs, gr, gl)
        swap_att = Swap(at, att_ref, attw_ref, s1, r1, l1)
        swap_ff = Swap(at, ff_ref, ffw_ref, s2, r2, l2)
        swap_att.start()
        gather.start()
        swap_ff.start()
        swap_att.wait()
        spread = Spread(at, attw_ref, s3, r3)
        spread.start()
        gather.forward()
        gather.finish()
        spread.wait()
        swap_ff.wait()

    def second_kernel(
        part_ref, x_ref, cot_ref, ffw_in, a2_ref, cots_ref, mid_ref, ffw_ref,
        own, near, sent, got, ss, sr, sl, low, s1, r1, l1, s2, r2, l2, s3, r3,
    ):
        at = Place(sizes)
        at.greet([at.core, *at.all_z(), *at.all_xy()])
        scatter = Scatter(at, part_ref, own, near, sent, got, ss, sr, sl)
        spread = Spread(at, ffw_ref, s3, r3)
        cots = Gather(at, cot_ref, cots_ref, s1, r1, l1)
        scatter.start()
        spread.start()
        scatter.pass_on()
        cots.start()
        scatter.arrive()

        def norm(rows):
            mid = x_ref[rows].astype(F32) + scatter.total(rows)
            mid_ref[rows] = mid
            low[rows] = mean_spread(mid)[0].astype(BF)

        by_rows(x_ref.shape[0], norm)
        a2 = Gather(at, low, a2_ref, s2, r2, l2)
        a2.start()
        cots.forward()
        a2.forward()
        cots.finish()
        a2.finish()
        scatter.finish()
        spread.wait()

    def third_kernel(
        part_ref, branch_ref, mid_ref, cot_ref, grad_ref, rows_ref, block_ref, own_ref, got_ref,
        own, near, sent, got, ss, sr, sl, own2, near2, sent2, got2, ss2, sr2, sl2, low, s1, r1, l1, s3, r3,
    ):
        at = Place(sizes)
        at.greet([at.core, *at.all_z(), *at.all_xy()])
        scatter = Scatter(at, part_ref, own, near, sent, got, ss, sr, sl)
        branch = Scatter(at, branch_ref, own2, near2, sent2, got2, ss2, sr2, sl2)
        collect = Collect(at, grad_ref, got_ref, s3, r3)
        scatter.start()
        collect.start()
        scatter.pass_on()
        branch.start()
        branch.pass_on()
        scatter.arrive()

        def norm(rows):
            normed, scale = mean_spread(mid_ref[rows])
            grad = cot_ref[rows].astype(F32) + norm_back(scatter.total(rows), normed, scale)
            own_ref[rows] = grad
            low[rows] = grad.astype(BF)

        by_rows(mid_ref.shape[0], norm)
        gather = Gather(at, low, rows_ref, s1, r1, l1)
        gather.start()
        branch.arrive()

        def add(rows):
            block_ref[rows] = (mid_ref[rows] + branch.total(rows)).astype(BF)

        by_rows(mid_ref.shape[0], add)
        gather.forward()
        gather.finish()
        scatter.finish()
        branch.finish()
        collect.wait()

    def fourth_kernel(
        part_ref, x_ref, mid_ref, block_ref, att_ref, ff_ref, input_ref, out_ref, attg_ref, ffg_ref,
        own, near, sent, got, ss, sr, sl, mine, theirs, total, low, s1, r1, l1, s2, r2, l2, s3, r3, s4, r4, l4,
    ):
        at = Place(sizes)
        tps = [(at.f, at.c, lax.rem(at.t + s, n_t)) for s in range(1, n_t)]
        at.greet([*tps, *at.all_z(), *[at.xy(s, o) for s, o in at.pairs if s]])
        scatter = Scatter(at, part_ref, own, near, sent, got, ss, sr, sl)
        collect = Collect(at, att_ref, theirs, s3, r3)
        height = att_ref.shape[2] // n_f
        kept = pltpu.make_async_copy(
            att_ref.at[at.hi, :, pl.ds(at.f * height, height), :], mine, l4.at[0]
        )
        give_ff = Return(at, ff_ref, ffg_ref, s2, r2, l2)
        scatter.start()
        collect.start()
        kept.start()

        def tp_gather(src, dst, k):
            copies = [
                remote(src, dst.at[at.t], s4.at[k, i], r4.at[k, i], peer) for i, peer in enumerate(tps)
            ]
            keep = pltpu.make_async_copy(src, dst.at[at.t], l4.at[1 + k])
            for copy in (*copies, keep):
                copy.start()
            return [*copies, keep]

        waits = tp_gather(block_ref, out_ref, 0)
        scatter.pass_on()
        kept.wait()
        collect.wait()
        for m in range(mine.shape[0]):

            def add(rows, m=m):
                value = mine[m, rows].astype(F32)
                for i in range(pairs):
                    value = value + theirs[i, m, rows].astype(F32)
                total[m, rows] = value.astype(BF)

            by_rows(height, add)
        give_att = Return(at, total, attg_ref, s1, r1, l1)
        give_att.start()
        give_ff.start()
        scatter.arrive()

        def norm(rows):
            normed, scale = mean_spread(x_ref[rows].astype(F32))
            low[rows] = mid_ref[rows] + norm_back(scatter.total(rows), normed, scale)

        by_rows(mid_ref.shape[0], norm)
        waits += tp_gather(low, input_ref, 1)
        for copy in waits:
            copy.wait()
        scatter.finish()
        give_att.wait()
        give_ff.wait()

    def norm_kernel(value_ref, out_ref, everyone, send, recv):
        f, c, t = (lax.axis_index(a) for a in ("fsdp", "ctx", "tp"))
        me = (f * n_c + c) * n_t + t
        count = n_f * n_c * n_t

        def device(i):
            i = lax.rem(me + i, count)
            return (i // (n_c * n_t), lax.rem(i // n_t, n_c), lax.rem(i, n_t))

        barrier = pltpu.get_barrier_semaphore()
        for i in range(1, count):
            pl.semaphore_signal(barrier, inc=1, device_id=device(i), device_id_type=MESH)
        pl.semaphore_wait(barrier, count - 1)
        copies = [
            remote(value_ref, everyone.at[i], send.at[i], recv.at[i], device(i))
            for i in range(1, count)
        ]
        for copy in copies:
            copy.start()
        everyone[0] = value_ref[...]
        for copy in copies:
            copy.wait()
        out_ref[...] = jnp.sum(everyone[...], axis=0)

    def shards(
        tokens,
        cotangent,
        lengths,
        deal,
        att_proj,
        attn_out,
        ff_proj,
        ff_out,
        att_proj_first,
        attn_out_first,
        ff_proj_first,
        ff_out_first,
        att_proj_second,
        attn_out_second,
        ff_proj_second,
        ff_out_second,
    ):
        t_at = lax.axis_index("tp")
        f_at = lax.axis_index("fsdp")
        pack_at = t_at // 2
        packs, row_count, width = tokens.shape
        half = row_count // 2
        pack_len = deal.shape[1]
        blocks = n_c * 2
        score_scale = HEAD_DIM ** (-0.5)
        rows_bf = jax.ShapeDtypeStruct((blocks, half, width), BF)
        own_f32 = jax.ShapeDtypeStruct((half, width), F32)
        own_bf = jax.ShapeDtypeStruct((half, width), BF)

        def own_rows(array):
            rows = array.reshape(packs * 2, half, width)
            return lax.dynamic_index_in_dim(rows, t_at, 0, keepdims=False)

        own_tokens = own_rows(tokens)
        own_cot = own_rows(cotangent)
        att_low = jnp.concatenate([att_proj, attn_out[None]]).astype(BF)
        ff_low = jnp.concatenate([ff_proj, ff_out[None]]).astype(BF)
        normed_one, _ = mean_spread(own_tokens.astype(F32))
        att_cols, ff_cols = att_low.shape[2] // n_c, ff_low.shape[2] // n_c
        act_one, att_w, ff_w = call(
            first_kernel,
            "first",
            0,
            (
                rows_bf,
                jax.ShapeDtypeStruct((2, 4, width, att_cols), BF),
                jax.ShapeDtypeStruct((2, 3, width, ff_cols), BF),
            ),
            [ANY] * 3,
            (ANY,) * 3,
            gather_sems(n_c)
            + [dma(n_c), dma(n_c), pltpu.SemaphoreType.DMA] * 2
            + [dma(pairs), dma(pairs)],
        )(normed_one.astype(BF), att_low, ff_low)
        act_one = act_one.reshape(pack_len, width)

        places = lax.dynamic_index_in_dim(deal, pack_at, 0, keepdims=False)
        length_row = lax.dynamic_index_in_dim(lengths, pack_at, 0, keepdims=False)
        seqs = lengths.shape[1]
        before = jnp.arange(seqs)[:, None] > jnp.arange(seqs)[None, :]
        starts = jnp.sum(jnp.where(before, length_row[None, :], 0), axis=1)
        inside = (places[:, None] >= starts[None, :]) & (
            places[:, None] < (starts + length_row)[None, :]
        )
        firsts = jnp.sum(jnp.where(inside, starts[None, :], 0), axis=1)
        allowed = (places[None, :] <= places[:, None]) & (places[None, :] >= firsts[:, None])
        freq_steps = jnp.arange(HEAD_DIM // 2, dtype=F32)
        inverse = jnp.power(10000.0, -2.0 * freq_steps / HEAD_DIM)
        angles = (places - firsts).astype(F32)[:, None] * inverse[None, :]
        cos_table, sine_table = jnp.cos(angles), jnp.sin(angles)

        def turn(values, sign):
            low, high = values[..., : HEAD_DIM // 2], values[..., HEAD_DIM // 2 :]
            sine = sign * sine_table
            return jnp.concatenate(
                [low * cos_table - high * sine, high * cos_table + low * sine], axis=-1
            )

        def heads_of(rows, matrix):
            return jnp.stack([dot(rows, att_w[y, matrix], ((1,), (0,))) for y in range(2)])

        query = turn(heads_of(act_one, 0), 1.0).astype(BF)
        key = turn(heads_of(act_one, 1), 1.0).astype(BF)
        value = heads_of(act_one, 2).astype(BF)
        scores = (
            jnp.einsum("htd,hkd->htk", query, key, preferred_element_type=F32) * score_scale
        )
        scores = jnp.where(allowed[None], scores, NEG_FILL)
        exp_scores = jnp.exp(scores - jnp.max(scores, axis=2, keepdims=True))
        probs = exp_scores / jnp.sum(exp_scores, axis=2, keepdims=True)
        probs_low = probs.astype(BF)
        attended = jnp.einsum(
            "htk,hkd->htd", probs_low, value, preferred_element_type=F32
        ).astype(BF)
        out_part = sum(dot(attended[y], att_w[y, 3], ((1,), (1,))) for y in range(2))
        act_two, cot_rows, resid_mid, ff_w = call(
            second_kernel,
            "second",
            1,
            (rows_bf, rows_bf, own_f32, jax.ShapeDtypeStruct(ff_w.shape, BF)),
            [ANY, VMEM, VMEM, ANY],
            (ANY, ANY, VMEM, ANY),
            scatter_scratch(n_c, half, width)
            + [pltpu.VMEM((half, width), BF)]
            + gather_sems(n_c) * 2
            + [dma(pairs), dma(pairs)],
            {3: 3},
        )(out_part.astype(BF).reshape(rows_bf.shape), own_tokens, own_cot, ff_w)
        act_two = act_two.reshape(pack_len, width)
        cot_rows = cot_rows.reshape(pack_len, width)

        act_two_part, branch_part, ff_grads = 0.0, 0.0, []
        for y in range(2):
            up = dot(act_two, ff_w[y, 0], ((1,), (0,)))
            gate = dot(act_two, ff_w[y, 1], ((1,), (0,)))
            sigma = jax.nn.sigmoid(gate)
            hidden_low = (gate * sigma * up).astype(BF)
            hidden_grad = dot(cot_rows, ff_w[y, 2], ((1,), (0,)))
            up_grad = (hidden_grad * gate * sigma).astype(BF)
            gate_grad = (hidden_grad * up * sigma * (1.0 + gate * (1.0 - sigma))).astype(BF)
            act_two_part += dot(up_grad, ff_w[y, 0], ((1,), (1,)))
            act_two_part += dot(gate_grad, ff_w[y, 1], ((1,), (1,)))
            branch_part += dot(hidden_low, ff_w[y, 2], ((1,), (1,)))
            ff_grads.append(
                jnp.stack(
                    [
                        dot(act_two, up_grad, ((0,), (0,))).astype(BF),
                        dot(act_two, gate_grad, ((0,), (0,))).astype(BF),
                        dot(cot_rows, hidden_low, ((0,), (0,))).astype(BF),
                    ]
                )
            )
        ff_grad = jnp.stack(ff_grads)
        height = width // n_f
        mid_rows, block_own, mid_grad, ff_got = call(
            third_kernel,
            "third",
            2,
            (rows_bf, own_bf, own_f32, jax.ShapeDtypeStruct((pairs, 3, height, ff_cols), BF)),
            [ANY, ANY, VMEM, VMEM, ANY],
            (ANY, VMEM, VMEM, ANY),
            scatter_scratch(n_c, half, width) * 2
            + [pltpu.VMEM((half, width), BF)]
            + gather_sems(n_c)
            + [dma(pairs), dma(pairs)],
        )(
            act_two_part.astype(BF).reshape(rows_bf.shape),
            branch_part.astype(BF).reshape(rows_bf.shape),
            resid_mid,
            own_cot,
            ff_grad,
        )
        mid_rows = mid_rows.reshape(pack_len, width)
        ff_mine = lax.dynamic_slice(
            ff_grad, (pack_at, 0, f_at * height, 0), (1, 3, height, ff_cols)
        )[0]
        ff_sum = ff_mine.astype(F32) + sum(ff_got[i].astype(F32) for i in range(pairs))

        attended_grad = heads_of(mid_rows, 3).astype(BF)
        value_grad = jnp.einsum(
            "htk,htd->hkd", probs_low, attended_grad, preferred_element_type=F32
        )
        prob_grad = jnp.einsum("htd,hkd->htk", attended_grad, value, preferred_element_type=F32)
        delta_rows = jnp.sum(probs * prob_grad, axis=2, keepdims=True)
        score_grad = (probs * (prob_grad - delta_rows)).astype(BF)
        query_grad = (
            jnp.einsum("htk,hkd->htd", score_grad, key, preferred_element_type=F32) * score_scale
        )
        key_grad = (
            jnp.einsum("htk,htd->hkd", score_grad, query, preferred_element_type=F32)
            * score_scale
        )
        joint_grad = [
            part.astype(BF) for part in (turn(query_grad, -1.0), turn(key_grad, -1.0), value_grad)
        ]
        act_one_part = sum(
            dot(joint_grad[i][y], att_w[y, i], ((1,), (1,))) for i in range(3) for y in range(2)
        )
        att_grad = jnp.stack(
            [
                jnp.stack(
                    [dot(act_one, part[y], ((0,), (0,))).astype(BF) for part in joint_grad]
                    + [dot(mid_rows, attended[y], ((0,), (0,))).astype(BF)]
                )
                for y in range(2)
            ]
        )
        input_grad, block_out, att_total, ff_total = call(
            fourth_kernel,
            "fourth",
            3,
            (
                jax.ShapeDtypeStruct((n_t, half, width), F32),
                jax.ShapeDtypeStruct((n_t, half, width), BF),
                jax.ShapeDtypeStruct(att_low.shape, BF),
                jax.ShapeDtypeStruct(ff_low.shape, BF),
            ),
            [ANY, VMEM, VMEM, ANY, ANY, ANY],
            (ANY,) * 4,
            scatter_scratch(n_c, half, width)
            + [
                pltpu.VMEM((4, height, att_cols), BF),
                pltpu.VMEM((pairs, 4, height, att_cols), BF),
                pltpu.VMEM((4, height, att_cols), BF),
                pltpu.VMEM((half, width), F32),
            ]
            + [dma(n_c), dma(n_c), pltpu.SemaphoreType.DMA] * 2
            + [dma(pairs), dma(pairs)]
            + [
                pltpu.SemaphoreType.DMA((2, n_t - 1)),
                pltpu.SemaphoreType.DMA((2, n_t - 1)),
                dma(3),
            ],
        )(
            act_one_part.astype(BF).reshape(rows_bf.shape),
            own_tokens,
            mid_grad,
            block_own,
            att_grad,
            ff_sum.astype(BF),
        )
        att_total, ff_total = att_total.astype(F32), ff_total.astype(F32)

        square = jnp.sum(att_total * att_total) + jnp.sum(ff_total * ff_total)
        count = n_f * n_c * n_t
        square_sum = call(
            norm_kernel,
            "norm",
            4,
            jax.ShapeDtypeStruct((8, 128), F32),
            [VMEM],
            VMEM,
            [pltpu.VMEM((count, 8, 128), F32), dma(count), dma(count)],
            vmem=8,
        )(jnp.broadcast_to(square, (8, 128)))[0, 0]
        norm_value = jnp.sqrt(square_sum)
        clip_factor = jnp.minimum(1.0, MAX_NORM / (norm_value + 1e-06))
        base_rate = width ** (-0.5)
        out_rate = (width // 32) ** (-0.5)
        grads = (att_total[:3], att_total[3], ff_total[:2], ff_total[2])
        weights = (att_proj, attn_out, ff_proj, ff_out)
        firsts_old = (att_proj_first, attn_out_first, ff_proj_first, ff_out_first)
        seconds_old = (att_proj_second, attn_out_second, ff_proj_second, ff_out_second)
        rates = (base_rate, out_rate, base_rate, base_rate)
        news = [
            adam_step(w, g, m, v, clip_factor, r)
            for w, g, m, v, r in zip(weights, grads, firsts_old, seconds_old, rates)
        ]
        return (
            block_out.reshape(tokens.shape),
            input_grad.reshape(tokens.shape),
            norm_value.reshape(1),
            *grads,
            *(n[0] for n in news),
            *(n[1] for n in news),
            *(n[2] for n in news),
            *(n[2].astype(BF) for n in news),
        )

    return shards


def solution(mesh):
    act = P("fsdp", "ctx", None)
    table = P("fsdp", None)
    cube = P(None, ("fsdp", "ctx"), "tp")
    flat = P(("fsdp", "ctx"), "tp")
    group = (cube, flat, cube, flat)
    in_specs = (act, act, table, table) + group * 3
    out_specs = (act, act, P()) + group * 5
    return jax.shard_map(
        make_shards(mesh), mesh=mesh, in_specs=in_specs, out_specs=out_specs, check_vma=False
    )
```

```python
import functools

import jax
import jax.numpy as jnp
from jax import lax
from jax.experimental import pallas as pl
from jax.experimental.pallas import tpu as pltpu
from jax.sharding import PartitionSpec as P

HEAD_DIM = 128
STEP = 10
EPS_NORM = 1e-05
BETA_ONE = 0.9
BETA_TWO = 0.95
EPS_ADAM = 1e-08
DECAY = 0.1
MAX_NORM = 1.0
NEG_FILL = -1e30
BF = jnp.bfloat16
F32 = jnp.float32
MESH = pl.DeviceIdType.MESH
ANY = pl.BlockSpec(memory_space=pl.ANY)
VMEM = pl.BlockSpec(memory_space=pltpu.VMEM)
ROWS = 16
QUERIES = 256
SCORE_SCALE = HEAD_DIM ** (-0.5)


def mean_spread(values):
    centre = values - jnp.mean(values, axis=-1, keepdims=True)
    spread = jnp.mean(centre * centre, axis=-1, keepdims=True)
    scale = lax.rsqrt(spread + EPS_NORM)
    return centre * scale, scale


def norm_back(grad, normed, scale):
    return scale * (
        grad
        - jnp.mean(grad, axis=-1, keepdims=True)
        - normed * jnp.mean(grad * normed, axis=-1, keepdims=True)
    )


def dot(left, right, dims):
    return lax.dot_general(left, right, (dims, ((), ())), preferred_element_type=F32)


def adam_step(weight, grad_sum, first, second, clip_factor, learn_rate):
    clipped = grad_sum * clip_factor
    first_new = BETA_ONE * first + (1.0 - BETA_ONE) * clipped
    second_new = BETA_TWO * second + (1.0 - BETA_TWO) * clipped * clipped
    first_hat = first_new / (1.0 - BETA_ONE**STEP)
    second_hat = second_new / (1.0 - BETA_TWO**STEP)
    weight_new = weight - learn_rate * (
        first_hat / (jnp.sqrt(second_hat) + EPS_ADAM) + DECAY * weight
    )
    return (first_new, second_new, weight_new)


class Place:
    def __init__(self, sizes):
        self.n_f, self.n_c, self.n_t = sizes
        self.f, self.c, self.t = (lax.axis_index(a) for a in ("fsdp", "ctx", "tp"))
        self.hi, self.lo = self.t // 2, lax.rem(self.t, 2)
        self.core = (self.f, self.c, self.t + 1 - 2 * self.lo)
        self.block = self.c * 2 + self.lo
        self.pairs = [(s, o) for o in range(2) for s in range(self.n_f) if s or o]

    def ctx(self, shift):
        return lax.rem(self.c + shift + self.n_c, self.n_c)

    def fsdp(self, shift):
        return lax.rem(self.f + shift + self.n_f, self.n_f)

    def other(self, o):
        return self.hi + o * (1 - 2 * self.hi)

    def z(self, shift):
        return (self.f, self.ctx(shift), self.t)

    def xy(self, shift, o):
        return (self.fsdp(shift), self.c, self.t + o * (2 - 4 * self.hi))

    def greet(self, peers):
        barrier = pltpu.get_barrier_semaphore()
        for peer in peers:
            pl.semaphore_signal(barrier, inc=1, device_id=peer, device_id_type=MESH)
        pl.semaphore_wait(barrier, len(peers))

    def all_z(self):
        return [self.z(s) for s in range(1, self.n_c)]

    def all_xy(self):
        return [self.xy(s, o) for s, o in self.pairs]


def remote(src, dst, send, recv, peer):
    return pltpu.make_async_remote_copy(
        src_ref=src, dst_ref=dst, send_sem=send, recv_sem=recv, device_id=peer, device_id_type=MESH
    )


def by_rows(count, step):
    @pl.loop(0, count // ROWS)
    def _(i):
        step(pl.ds(pl.multiple_of(i * ROWS, ROWS), ROWS))


class Gather:
    def __init__(self, at, src, out, send, recv, local):
        self.at, self.src, self.out, self.send, self.recv = at, src, out, send, recv
        self.local = pltpu.make_async_copy(src, out.at[at.block], local)

    def far(self, way, hop, src=None):
        at = self.at
        block = self.out.at[jnp.clip(at.c - way * (hop - 1), 0, at.n_c - 1) * 2 + at.lo]
        k = hop + (0 if way > 0 else at.n_c)
        return remote(
            block if src is None else src, block, self.send.at[k], self.recv.at[k], at.z(way)
        )

    def near(self, distance, src=None):
        at = self.at
        block = self.out.at[jnp.clip(at.c - distance, 0, at.n_c - 1) * 2 + at.lo]
        k = 2 * at.n_c + distance + at.n_c
        return remote(
            block if src is None else src, block, self.send.at[k], self.recv.at[k], at.core
        )

    def there(self, way, hop):
        return self.at.c + hop < self.at.n_c if way > 0 else self.at.c >= hop

    def start(self):
        for way in (1, -1):

            @pl.when(self.there(way, 1))
            def _(way=way):
                self.far(way, 1, self.src).start()

        self.near(0, self.src).start()
        self.local.start()

    def forward(self, hops=None):
        at = self.at
        for hop in hops or range(1, at.n_c):
            for way in (1, -1):

                @pl.when(self.there(-way, hop))
                def _(way=way, hop=hop):
                    self.far(way, hop).wait_recv()
                    if hop < at.n_c - 1:

                        @pl.when(self.there(way, 1))
                        def _():
                            self.far(way, hop + 1).start()

                    self.near(way * hop).start()

    def finish(self):
        at = self.at
        for hop in range(1, at.n_c):
            for way in (1, -1):

                @pl.when(self.there(way, 1) & self.there(-way, hop - 1))
                def _(way=way, hop=hop):
                    self.far(way, hop).wait_send()

                @pl.when(self.there(-way, hop))
                def _(way=way, hop=hop):
                    self.near(way * hop).wait()

        self.near(0, self.src).wait()
        self.local.wait()


def gather_sems(n_c):
    return [
        pltpu.SemaphoreType.DMA((4 * n_c,)),
        pltpu.SemaphoreType.DMA((4 * n_c,)),
        pltpu.SemaphoreType.DMA,
    ]


class Scatter:
    def __init__(self, at, partial, own, near, sent, got, send, recv, local):
        self.at, self.partial, self.own, self.near = at, partial, own, near
        self.sent, self.got, self.send, self.recv, self.local = sent, got, send, recv, local

    def keep(self, c):
        return pltpu.make_async_copy(
            self.partial.at[c * 2 + self.at.lo], self.own.at[c], self.local.at[c]
        )

    def core(self, c):
        at = self.at
        return remote(
            self.partial.at[c * 2 + 1 - at.lo], self.near.at[c], self.send.at[c], self.recv.at[c], at.core
        )

    def far(self, way, hop):
        at = self.at
        c = jnp.clip(at.c + way * hop, 0, at.n_c - 1)
        slot = c if hop > 1 else c + (0 if way > 0 else at.n_c)
        k = at.n_c + hop + (0 if way > 0 else at.n_c)
        return remote(
            self.sent.at[c], self.got.at[slot], self.send.at[k], self.recv.at[k], at.z(way)
        )

    there = Gather.there

    def start(self):
        at = self.at
        for i in range(at.n_c):
            c = jnp.where(at.c * 2 < at.n_c, at.n_c - 1 - i, i)
            self.core(c).start()
            self.keep(c).start()

    def pass_on(self):
        at = self.at
        for hop in range(at.n_c - 1, 0, -1):
            for way in (1, -1):

                @pl.when(self.there(way, hop))
                def _(way=way, hop=hop):
                    c = at.c + way * hop
                    self.core(c).wait_recv()
                    self.keep(c).wait()
                    if hop < at.n_c - 1:
                        more = self.there(-way, 1)

                        @pl.when(more)
                        def _():
                            self.far(way, hop + 1).wait_recv()

                            def add(rows):
                                self.sent[c, rows] = (
                                    self.own[c, rows].astype(F32)
                                    + self.near[c, rows].astype(F32)
                                    + self.got[c, rows].astype(F32)
                                ).astype(BF)

                            by_rows(self.own.shape[1], add)

                        @pl.when(jnp.logical_not(more))
                        def _():
                            self.both(c)

                    else:
                        self.both(c)
                    self.far(way, hop).start()

        self.core(at.c).wait_recv()
        self.keep(at.c).wait()

    def both(self, c):
        def add(rows):
            self.sent[c, rows] = (
                self.own[c, rows].astype(F32) + self.near[c, rows].astype(F32)
            ).astype(BF)

        by_rows(self.own.shape[1], add)

    def arrive(self):
        at = self.at
        for way in (1, -1):

            @pl.when(self.there(-way, 1))
            def _(way=way):
                self.far(way, 1).wait_recv()

            @pl.when(jnp.logical_not(self.there(-way, 1)))
            def _(way=way):
                slot = at.c + (0 if way > 0 else at.n_c)
                self.got[slot] = jnp.zeros(self.got.shape[1:], BF)

    def total(self, rows):
        c = self.at.c
        return (
            self.own[c, rows].astype(F32)
            + self.near[c, rows].astype(F32)
            + self.got[c, rows].astype(F32)
            + self.got[c + self.at.n_c, rows].astype(F32)
        )

    def finish(self):
        at = self.at
        for c in range(at.n_c):
            self.core(c).wait_send()
        for hop in range(1, at.n_c):
            for way in (1, -1):

                @pl.when(self.there(way, hop))
                def _(way=way, hop=hop):
                    self.far(way, hop).wait_send()


def scatter_scratch(n_c, half, width):
    return [
        pltpu.VMEM((n_c, half, width), BF),
        pltpu.VMEM((n_c, half, width), BF),
        pltpu.VMEM((n_c, half, width), BF),
        pltpu.VMEM((2 * n_c, half, width), BF),
        pltpu.SemaphoreType.DMA((3 * n_c,)),
        pltpu.SemaphoreType.DMA((3 * n_c,)),
        pltpu.SemaphoreType.DMA((n_c,)),
    ]


class Swap:
    def __init__(self, at, shard, full, send, recv, local):
        self.at = at
        rows, width = shard.shape[1], full.shape[3]
        here = pl.ds((at.f * at.n_c + at.c) * rows, rows)
        target = full.at[at.hi, :, here, :]

        def columns(c):
            return shard.at[:, :, pl.ds(pl.multiple_of(c * width, 128), width)]

        self.local = pltpu.make_async_copy(columns(at.c), target, local)
        self.far = [
            remote(columns(at.ctx(s)), target, send.at[s], recv.at[s], at.z(s))
            for s in range(1, at.n_c)
        ]

    def start(self):
        self.local.start()
        for copy in self.far:
            copy.start()

    def wait(self):
        self.local.wait()
        for copy in self.far:
            copy.wait()


class Spread:
    def __init__(self, at, full, send, recv):
        self.at, self.full, self.send, self.recv = at, full, send, recv
        self.height = full.shape[2] // at.n_f // 2

    def part(self, o, shift, half):
        at = self.at
        first = (at.fsdp(shift) * 2 + half) * self.height
        return self.full.at[at.other(o), :, pl.ds(first, self.height), :]

    def copy(self, part, k, peer):
        return remote(part, part, self.send.at[k], self.recv.at[k], peer)

    def copies(self):
        at = self.at
        n = at.n_f
        return [
            *(
                self.copy(self.part(0, 0, h), h * n + s, at.xy(s, 0))
                for h in range(2)
                for s in range(1, n)
            ),
            *(self.copy(self.part(0, 0, h), 2 * n + h, at.xy(0, 1)) for h in (1, 0)),
        ]

    def passes(self):
        at = self.at
        n = at.n_f
        return [
            *(self.copy(self.part(0, -s, 0), 3 * n + s, at.xy(0, 1)) for s in range(1, n)),
            *(self.copy(self.part(1, 0, 1), 4 * n + s, at.xy(s, 0)) for s in range(1, n)),
        ]

    def start(self):
        for copy in self.copies():
            copy.start()

    def forward(self):
        copies, n = self.copies(), self.at.n_f
        for copy in copies[: n - 1]:
            copy.wait_recv()
        copies[2 * n - 2].wait_recv()
        for copy in self.passes():
            copy.start()

    def wait(self):
        copies, n = self.copies(), self.at.n_f
        for copy in copies[n - 1 : 2 * n - 2]:
            copy.wait_recv()
        copies[2 * n - 1].wait_recv()
        for copy in copies:
            copy.wait_send()
        for copy in self.passes():
            copy.wait()


class Collect:
    def __init__(self, at, partial, mine, by_x, by_y, pass_x, pass_y, part_x, part_y, send, recv, local):
        self.at, self.partial, self.mine, self.by_x, self.by_y = at, partial, mine, by_x, by_y
        self.pass_x, self.pass_y, self.part_x, self.part_y = pass_x, pass_y, part_x, part_y
        self.send, self.recv, self.local = send, recv, local
        self.height = partial.shape[2] // at.n_f // 2

    def part(self, o, shift, half):
        at = self.at
        first = (at.fsdp(shift) * 2 + half) * self.height
        return self.partial.at[at.other(o), :, pl.ds(first, self.height), :]

    def half(self, ref, half):
        return ref.at[:, pl.ds(half * self.height, self.height), :]

    def copy(self, src, dst, k, peer):
        return remote(src, dst, self.send.at[k], self.recv.at[k], peer)

    def raw(self):
        at = self.at
        n, shifts = at.n_f, range(1, at.n_f)
        return [
            [self.copy(self.part(1, s, 0), self.pass_x.at[s - 1], s, at.xy(s, 0)) for s in shifts],
            [self.copy(self.part(1, s, 1), self.pass_y.at[s - 1], n + s, at.xy(0, 1)) for s in shifts],
            [
                *(
                    self.copy(self.part(0, s, 0), self.half(self.by_x.at[s - 1], 0), 2 * n + s, at.xy(s, 0))
                    for s in shifts
                ),
                self.copy(self.part(1, 0, 1), self.half(self.by_y, 1), 0, at.xy(0, 1)),
            ],
        ]

    def added(self):
        at = self.at
        n, shifts = at.n_f, range(1, at.n_f)
        return [
            self.copy(self.part_y, self.half(self.by_y, 0), n, at.xy(0, 1)),
            *(
                self.copy(self.part_x.at[s - 1], self.half(self.by_x.at[s - 1], 1), 3 * n + s, at.xy(s, 0))
                for s in shifts
            ),
        ]

    def keeps(self):
        first = self.at.f * 2 * self.height
        own = self.partial.at[self.at.hi, :, pl.ds(first, 2 * self.height), :]
        return [
            pltpu.make_async_copy(own, self.mine, self.local.at[0]),
            pltpu.make_async_copy(self.part(1, 0, 0), self.part_y, self.local.at[1]),
            *(
                pltpu.make_async_copy(self.part(0, s, 1), self.part_x.at[s - 1], self.local.at[1 + s])
                for s in range(1, self.at.n_f)
            ),
        ]

    def start(self):
        for copies in self.raw():
            for copy in copies:
                copy.start()
        for copy in self.keeps():
            copy.start()

    def forward(self):
        raw, added, keeps = self.raw(), self.added(), self.keeps()
        for copy in (*raw[0], keeps[1]):
            copy.wait() if copy is keeps[1] else copy.wait_recv()
        n = self.at.n_f
        for m in range(self.mine.shape[0]):

            def add_y(rows, m=m):
                value = self.part_y[m, rows].astype(F32)
                for s in range(n - 1):
                    value = value + self.pass_x[s, m, rows].astype(F32)
                self.part_y[m, rows] = value.astype(BF)

            by_rows(self.height, add_y)
        added[0].start()
        for s in range(1, n):
            raw[1][s - 1].wait_recv()
            keeps[1 + s].wait()
            for m in range(self.mine.shape[0]):

                def add_x(rows, m=m, s=s):
                    self.part_x[s - 1, m, rows] = (
                        self.part_x[s - 1, m, rows].astype(F32) + self.pass_y[s - 1, m, rows].astype(F32)
                    ).astype(BF)

                by_rows(self.height, add_x)
            added[s].start()

    def total(self, out):
        raw, added = self.raw(), self.added()
        for copy in (*raw[2], *added):
            copy.wait_recv()
        self.keeps()[0].wait()
        for m in range(self.mine.shape[0]):

            def add(rows, m=m):
                value = self.mine[m, rows].astype(F32) + self.by_y[m, rows].astype(F32)
                for s in range(self.at.n_f - 1):
                    value = value + self.by_x[s, m, rows].astype(F32)
                out[m, rows] = value.astype(BF)

            by_rows(2 * self.height, add)

    def finish(self):
        for copies in (*self.raw(), self.added()):
            for copy in copies:
                copy.wait_send()


def collect_scratch(n_f, matrices, height, columns):
    half = (matrices, height // 2, columns)
    return [
        pltpu.VMEM((matrices, height, columns), BF),
        pltpu.VMEM((n_f - 1, matrices, height, columns), BF),
        pltpu.VMEM((matrices, height, columns), BF),
        pltpu.VMEM((n_f - 1, *half), BF),
        pltpu.VMEM((n_f - 1, *half), BF),
        pltpu.VMEM((n_f - 1, *half), BF),
        pltpu.VMEM(half, BF),
        dma(4 * n_f),
        dma(4 * n_f),
        dma(n_f + 1),
    ]


class Return:
    def __init__(self, at, summed, shard, send, recv, local):
        rows, width = shard.shape[1], summed.shape[2]
        target = shard.at[:, :, pl.ds(pl.multiple_of(at.c * width, 128), width)]

        def part(c):
            return summed.at[:, pl.ds(pl.multiple_of(c * rows, rows), rows), :]

        self.local = pltpu.make_async_copy(part(at.c), target, local)
        self.far = [
            remote(part(at.ctx(s)), target, send.at[s], recv.at[s], at.z(s))
            for s in range(1, at.n_c)
        ]

    start = Swap.start
    wait = Swap.wait


def pack_weights(w, packed):
    heads = w.shape[0]
    for i in range(4):
        for y in range(heads):
            k = (i * heads + y) * HEAD_DIM
            packed[:, k : k + HEAD_DIM] = w[y, i]


def turn(values, cos, sine):
    return values * cos + pltpu.roll(values, HEAD_DIM // 2, 1) * sine


def dma(count):
    return pltpu.SemaphoreType.DMA((count,))


def make_shards(mesh):
    sizes = tuple(mesh.shape[a] for a in ("fsdp", "ctx", "tp"))
    n_f, n_c, n_t = sizes

    def call(kernel, name, collective, outs, ins, out_specs, scratch, aliases=None, vmem=40):
        return pl.pallas_call(
            kernel,
            out_shape=outs,
            in_specs=ins,
            out_specs=out_specs,
            scratch_shapes=scratch,
            input_output_aliases=aliases or {},
            compiler_params=pltpu.CompilerParams(
                collective_id=collective, has_side_effects=True, vmem_limit_bytes=vmem << 20
            ),
            name=name,
        )

    def local(kernel, name, outs, scratch):
        return pl.pallas_call(
            kernel,
            out_shape=outs,
            scratch_shapes=scratch,
            compiler_params=pltpu.CompilerParams(vmem_limit_bytes=60 << 20),
            name=name,
        )

    def first_kernel(
        a1_ref, att_ref, ff_ref, rows_ref, attw_ref, ffw_ref, gs, gr, gl, s1, r1, l1, s2, r2, l2, s3, r3
    ):
        at = Place(sizes)
        at.greet([at.core, *at.all_z(), *at.all_xy()])
        gather = Gather(at, a1_ref, rows_ref, gs, gr, gl)
        swap_att = Swap(at, att_ref, attw_ref, s1, r1, l1)
        swap_ff = Swap(at, ff_ref, ffw_ref, s2, r2, l2)
        spread = Spread(at, attw_ref, s3, r3)
        swap_att.start()
        gather.start()
        swap_ff.start()
        swap_att.wait()
        spread.start()
        gather.forward()
        spread.forward()
        gather.finish()
        spread.wait()
        swap_ff.wait()

    def second_kernel(
        part_ref, x_ref, cot_ref, ffw_in, a2_ref, cots_ref, mid_ref, ffw_ref,
        own, near, sent, got, ss, sr, sl, low, s1, r1, l1, s2, r2, l2, s3, r3,
    ):
        at = Place(sizes)
        at.greet([at.core, *at.all_z(), *at.all_xy()])
        scatter = Scatter(at, part_ref, own, near, sent, got, ss, sr, sl)
        spread = Spread(at, ffw_ref, s3, r3)
        cots = Gather(at, cot_ref, cots_ref, s1, r1, l1)
        scatter.start()
        spread.start()
        scatter.pass_on()
        cots.start()
        scatter.arrive()

        def norm(rows):
            mid = x_ref[rows].astype(F32) + scatter.total(rows)
            mid_ref[rows] = mid
            low[rows] = mean_spread(mid)[0].astype(BF)

        by_rows(x_ref.shape[0], norm)
        a2 = Gather(at, low, a2_ref, s2, r2, l2)
        a2.start()
        spread.forward()
        for hop in range(1, n_c):
            cots.forward(range(hop, hop + 1))
            a2.forward(range(hop, hop + 1))
        cots.finish()
        a2.finish()
        scatter.finish()
        spread.wait()

    def third_kernel(
        part_ref, branch_ref, mid_ref, cot_ref, grad_ref, rows_ref, block_ref, own_ref, sum_ref,
        own, near, sent, got, ss, sr, sl, own2, near2, sent2, got2, ss2, sr2, sl2, low, s1, r1, l1, *collected,
    ):
        at = Place(sizes)
        at.greet([at.core, *at.all_z(), *at.all_xy()])
        scatter = Scatter(at, part_ref, own, near, sent, got, ss, sr, sl)
        branch = Scatter(at, branch_ref, own2, near2, sent2, got2, ss2, sr2, sl2)
        collect = Collect(at, grad_ref, *collected)
        scatter.start()
        collect.start()
        scatter.pass_on()
        branch.start()
        scatter.arrive()

        def norm(rows):
            normed, scale = mean_spread(mid_ref[rows])
            grad = cot_ref[rows].astype(F32) + norm_back(scatter.total(rows), normed, scale)
            own_ref[rows] = grad
            low[rows] = grad.astype(BF)

        by_rows(mid_ref.shape[0], norm)
        gather = Gather(at, low, rows_ref, s1, r1, l1)
        gather.start()
        branch.pass_on()
        gather.forward(range(1, 2))
        collect.forward()
        gather.forward(range(2, n_c))
        branch.arrive()

        def add(rows):
            block_ref[rows] = (mid_ref[rows] + branch.total(rows)).astype(BF)

        by_rows(mid_ref.shape[0], add)
        gather.finish()
        scatter.finish()
        branch.finish()
        collect.total(sum_ref)
        collect.finish()

    def fourth_kernel(
        part_ref, x_ref, mid_ref, block_ref, att_ref, ff_ref, input_ref, out_ref, attg_ref, ffg_ref,
        own, near, sent, got, ss, sr, sl, total, low, s1, r1, l1, s2, r2, l2, s4, r4, l4, *collected,
    ):
        at = Place(sizes)
        tps = [(at.f, at.c, lax.rem(at.t + s, n_t)) for s in range(1, n_t)]
        at.greet([*tps, *at.all_z(), *[at.xy(s, o) for s, o in at.pairs if s]])
        scatter = Scatter(at, part_ref, own, near, sent, got, ss, sr, sl)
        collect = Collect(at, att_ref, *collected)
        give_ff = Return(at, ff_ref, ffg_ref, s2, r2, l2)
        scatter.start()
        collect.start()

        def tp_gather(src, dst, k):
            copies = [
                remote(src, dst.at[at.t], s4.at[k, i], r4.at[k, i], peer) for i, peer in enumerate(tps)
            ]
            keep = pltpu.make_async_copy(src, dst.at[at.t], l4.at[k])
            for copy in (*copies, keep):
                copy.start()
            return [*copies, keep]

        scatter.pass_on()
        give_ff.start()
        collect.forward()
        waits = tp_gather(block_ref, out_ref, 0)
        collect.total(total)
        give_att = Return(at, total, attg_ref, s1, r1, l1)
        give_att.start()
        scatter.arrive()

        def norm(rows):
            normed, scale = mean_spread(x_ref[rows].astype(F32))
            low[rows] = mid_ref[rows] + norm_back(scatter.total(rows), normed, scale)

        by_rows(mid_ref.shape[0], norm)
        waits += tp_gather(low, input_ref, 1)
        for copy in waits:
            copy.wait()
        scatter.finish()
        collect.finish()
        give_att.wait()
        give_ff.wait()

    def norm_kernel(value_ref, out_ref, total, got_t, got_c, got_f, send, recv):
        at = Place(sizes)
        tps = [(at.f, at.c, lax.rem(at.t + s, n_t)) for s in range(1, n_t)]
        fs = [at.xy(s, 0) for s in range(1, n_f)]
        at.greet([*tps, *at.all_z(), *fs])
        total[0] = value_ref[...]
        base = 0
        for stage, (peers, got) in enumerate(((tps, got_t), (at.all_z(), got_c), (fs, got_f))):
            copies = [
                remote(total.at[stage], got.at[i], send.at[base + i], recv.at[base + i], peer)
                for i, peer in enumerate(peers)
            ]
            base += len(peers)
            for copy in copies:
                copy.start()
            for copy in copies:
                copy.wait()
            value = total[stage]
            for i in range(len(peers)):
                value = value + got[i]
            total[stage + 1] = value
        out_ref[...] = total[3]

    def forward_kernel(
        a1, w, place, key_place, first, cos, sine, qkv, attended, mass, part, packed
    ):
        heads = w.shape[0]
        wide = heads * HEAD_DIM
        pack_weights(w, packed)
        for i in range(3):
            joint = dot(a1[...], packed[:, i * wide : (i + 1) * wide], ((1,), (0,)))
            for y in range(heads):
                cols = slice(y * HEAD_DIM, (y + 1) * HEAD_DIM)
                head = joint[:, cols]
                if i < 2:
                    head = turn(head, cos[...], sine[...])
                qkv[i, :, cols] = head.astype(BF)
        for y in range(heads):
            cols = slice(y * HEAD_DIM, (y + 1) * HEAD_DIM)

            @pl.loop(0, a1.shape[0] // QUERIES)
            def _(c, y=y, cols=cols):
                rows = pl.ds(pl.multiple_of(c * QUERIES, QUERIES), QUERIES)
                scores = dot(qkv[0, rows, cols], qkv[1, :, cols], ((1,), (1,))) * SCORE_SCALE
                allowed = (key_place[...] <= place[rows]) & (key_place[...] >= first[rows])
                scores = jnp.where(allowed, scores, NEG_FILL)
                peak = jnp.max(scores, axis=1, keepdims=True)
                exp_scores = jnp.exp(scores - peak)
                total = jnp.sum(exp_scores, axis=1, keepdims=True)
                probs = (exp_scores * (1.0 / total)).astype(BF)
                attended[rows, cols] = dot(probs, qkv[2, :, cols], ((1,), (0,))).astype(BF)
                mass[rows, y : y + 1] = peak + jnp.log(total)

        width = part.shape[1] // 4

        @pl.loop(0, 4)
        def _(c):
            cols = pl.ds(pl.multiple_of(c * width, width), width)
            part[:, cols] = dot(attended[...], packed[cols, 3 * wide :], ((1,), (1,))).astype(BF)

    def backward_kernel(
        mid, a1, w, place, key_place, first, cos, sine, qkv, attended, mass, part, grad, packed, joint, d_v, d_k
    ):
        heads = w.shape[0]
        wide = heads * HEAD_DIM
        pack_weights(w, packed)
        joint[:, :wide] = dot(mid[...], packed[:, 3 * wide :], ((1,), (0,))).astype(BF)
        for y in range(heads):
            cols = slice(y * HEAD_DIM, (y + 1) * HEAD_DIM)

            @pl.loop(0, a1.shape[0] // QUERIES)
            def _(c, y=y, cols=cols):
                rows = pl.ds(pl.multiple_of(c * QUERIES, QUERIES), QUERIES)
                query, key, value = qkv[0, rows, cols], qkv[1, :, cols], qkv[2, :, cols]
                d_att = joint[rows, cols]
                scores = dot(query, key, ((1,), (1,))) * SCORE_SCALE
                allowed = (key_place[...] <= place[rows]) & (key_place[...] >= first[rows])
                probs = jnp.exp(jnp.where(allowed, scores, NEG_FILL) - mass[rows, y : y + 1])
                d_prob = dot(d_att, value, ((1,), (1,)))
                delta = jnp.sum(probs * d_prob, axis=1, keepdims=True)
                d_score = (probs * (d_prob - delta)).astype(BF)
                v_part = dot(probs.astype(BF), d_att, ((0,), (0,)))
                k_part = dot(d_score, query, ((0,), (0,)))

                @pl.when(c == 0)
                def _():
                    d_v[...] = v_part
                    d_k[...] = k_part

                @pl.when(c > 0)
                def _():
                    d_v[...] += v_part
                    d_k[...] += k_part

                d_query = dot(d_score, key, ((1,), (0,))) * SCORE_SCALE
                joint[rows, cols] = turn(d_query, cos[rows], -sine[rows]).astype(BF)

            joint[:, wide + y * HEAD_DIM : wide + (y + 1) * HEAD_DIM] = turn(
                d_k[...] * SCORE_SCALE, cos[...], -sine[...]
            ).astype(BF)
            joint[:, 2 * wide + y * HEAD_DIM : 2 * wide + (y + 1) * HEAD_DIM] = d_v[...].astype(BF)
        width = part.shape[1] // 4

        @pl.loop(0, 4)
        def _(c):
            cols = pl.ds(pl.multiple_of(c * width, width), width)
            part[:, cols] = dot(joint[...], packed[cols, : 3 * wide], ((1,), (1,))).astype(BF)

        @pl.loop(0, 2)
        def _(c):
            cols = pl.ds(pl.multiple_of(c * 2 * width, width), 2 * width)
            for i in range(4):
                if i < 3:
                    value = dot(a1[:, cols], joint[:, i * wide : (i + 1) * wide], ((0,), (0,)))
                else:
                    value = dot(mid[:, cols], attended[...], ((0,), (0,)))
                for y in range(heads):
                    grad[y, i, cols] = value[:, y * HEAD_DIM : (y + 1) * HEAD_DIM].astype(BF)

    def hidden_kernel(a2, cot, w, d_a2, branch, grad, hidden, d_up, d_gate, kept):
        step, steps = pl.program_id(0), pl.num_programs(0)
        tile = w.shape[3]
        here = pl.ds(pl.multiple_of(step * tile, tile), tile)
        length, width = a2.shape
        chunk = length // 2

        @pl.loop(0, 2)
        def _(i):
            rows = pl.ds(pl.multiple_of(i * chunk, chunk), chunk)
            up = dot(a2[rows], w[0, 0], ((1,), (0,)))
            gate = dot(a2[rows], w[0, 1], ((1,), (0,)))
            d_hid = dot(cot[rows], w[0, 2], ((1,), (0,)))
            sigma = jax.nn.sigmoid(gate)
            act = gate * sigma
            hidden[rows, here] = (act * up).astype(BF)
            d_up[rows, here] = (d_hid * act).astype(BF)
            d_gate[rows, here] = (d_hid * up * sigma * (1.0 + gate * (1.0 - sigma))).astype(BF)

        for m in range(3):
            kept[m, :, here] = w[0, m]
        grad[0, 0] = dot(a2[...], d_up[:, here], ((0,), (0,))).astype(BF)
        grad[0, 1] = dot(a2[...], d_gate[:, here], ((0,), (0,))).astype(BF)
        grad[0, 2] = dot(cot[...], hidden[:, here], ((0,), (0,))).astype(BF)

        @pl.when(step == steps - 1)
        def _():
            @pl.loop(0, 8)
            def _(i):
                cols = pl.ds(pl.multiple_of(i * (width // 8), width // 8), width // 8)
                d_a2[:, cols] = (
                    dot(d_up[...], kept[0, cols], ((1,), (1,)))
                    + dot(d_gate[...], kept[1, cols], ((1,), (1,)))
                ).astype(BF)
                branch[:, cols] = dot(hidden[...], kept[2, cols], ((1,), (1,))).astype(BF)

    def shards(
        tokens,
        cotangent,
        lengths,
        deal,
        att_proj,
        attn_out,
        ff_proj,
        ff_out,
        att_proj_first,
        attn_out_first,
        ff_proj_first,
        ff_out_first,
        att_proj_second,
        attn_out_second,
        ff_proj_second,
        ff_out_second,
    ):
        t_at = lax.axis_index("tp")
        pack_at = t_at // 2
        packs, row_count, width = tokens.shape
        half = row_count // 2
        pack_len = deal.shape[1]
        blocks = n_c * 2
        rows_bf = jax.ShapeDtypeStruct((blocks, half, width), BF)
        own_f32 = jax.ShapeDtypeStruct((half, width), F32)
        own_bf = jax.ShapeDtypeStruct((half, width), BF)

        def own_rows(array):
            rows = array.reshape(packs * 2, half, width)
            return lax.dynamic_index_in_dim(rows, t_at, 0, keepdims=False)

        own_tokens = own_rows(tokens)
        own_cot = own_rows(cotangent)
        att_low = jnp.concatenate([att_proj, attn_out[None]]).astype(BF)
        ff_low = jnp.concatenate([ff_proj, ff_out[None]]).astype(BF)
        normed_one, _ = mean_spread(own_tokens.astype(F32))
        att_cols, ff_cols = att_low.shape[2] // n_c, ff_low.shape[2] // n_c
        act_one, att_w, ff_w = call(
            first_kernel,
            "first",
            0,
            (
                rows_bf,
                jax.ShapeDtypeStruct((2, 4, width, att_cols), BF),
                jax.ShapeDtypeStruct((2, 3, width, ff_cols), BF),
            ),
            [ANY] * 3,
            (ANY,) * 3,
            gather_sems(n_c)
            + [dma(n_c), dma(n_c), pltpu.SemaphoreType.DMA] * 2
            + [dma(5 * n_f), dma(5 * n_f)],
        )(normed_one.astype(BF), att_low, ff_low)
        act_one = act_one.reshape(pack_len, width)

        places = lax.dynamic_index_in_dim(deal, pack_at, 0, keepdims=False)
        length_row = lax.dynamic_index_in_dim(lengths, pack_at, 0, keepdims=False)
        seqs = lengths.shape[1]
        before = jnp.arange(seqs)[:, None] > jnp.arange(seqs)[None, :]
        starts = jnp.sum(jnp.where(before, length_row[None, :], 0), axis=1)
        inside = (places[:, None] >= starts[None, :]) & (
            places[:, None] < (starts + length_row)[None, :]
        )
        firsts = jnp.sum(jnp.where(inside, starts[None, :], 0), axis=1)
        freq_steps = jnp.arange(HEAD_DIM // 2, dtype=F32)
        inverse = jnp.power(10000.0, -2.0 * freq_steps / HEAD_DIM)
        angles = (places - firsts).astype(F32)[:, None] * inverse[None, :]
        cos_table, sine_table = jnp.cos(angles), jnp.sin(angles)
        tables = (
            places[:, None],
            places[None, :],
            firsts[:, None],
            jnp.concatenate([cos_table, cos_table], axis=1),
            jnp.concatenate([-sine_table, sine_table], axis=1),
        )
        rank_width = 2 * att_cols
        qkv, attended, mass, out_part = local(
            forward_kernel,
            "forward",
            (
                jax.ShapeDtypeStruct((3, pack_len, rank_width), BF),
                jax.ShapeDtypeStruct((pack_len, rank_width), BF),
                jax.ShapeDtypeStruct((pack_len, 2), F32),
                jax.ShapeDtypeStruct((pack_len, width), BF),
            ),
            [pltpu.VMEM((width, 4 * rank_width), BF)],
        )(act_one, att_w, *tables)
        act_two, cot_rows, resid_mid, ff_w = call(
            second_kernel,
            "second",
            1,
            (rows_bf, rows_bf, own_f32, jax.ShapeDtypeStruct(ff_w.shape, BF)),
            [ANY, VMEM, VMEM, ANY],
            (ANY, ANY, VMEM, ANY),
            scatter_scratch(n_c, half, width)
            + [pltpu.VMEM((half, width), BF)]
            + gather_sems(n_c) * 2
            + [dma(5 * n_f), dma(5 * n_f)],
            {3: 3},
        )(out_part.reshape(rows_bf.shape), own_tokens, own_cot, ff_w)
        act_two = act_two.reshape(pack_len, width)
        cot_rows = cot_rows.reshape(pack_len, width)

        tile = 256
        tiles = ff_cols // tile
        kept = pl.BlockSpec((pack_len, width), lambda i: (0, 0), pipeline_mode=pl.Buffered(1))
        moved = pl.BlockSpec((1, 3, width, tile), lambda i: (i // tiles, 0, 0, i % tiles))
        rows_flat = jax.ShapeDtypeStruct((pack_len, width), BF)
        act_two_part, branch_part, ff_grad = pl.pallas_call(
            hidden_kernel,
            grid=(2 * tiles,),
            out_shape=(rows_flat, rows_flat, jax.ShapeDtypeStruct(ff_w.shape, BF)),
            in_specs=[kept, kept, moved],
            out_specs=(kept, kept, moved),
            scratch_shapes=[pltpu.VMEM((pack_len, 2 * ff_cols), BF)] * 3
            + [pltpu.VMEM((3, width, 2 * ff_cols), BF)],
            compiler_params=pltpu.CompilerParams(vmem_limit_bytes=60 << 20),
            name="hidden",
        )(act_two, cot_rows, ff_w)
        height = width // n_f
        mid_rows, block_own, mid_grad, ff_sum = call(
            third_kernel,
            "third",
            2,
            (rows_bf, own_bf, own_f32, jax.ShapeDtypeStruct((3, height, ff_cols), BF)),
            [ANY, ANY, VMEM, VMEM, ANY],
            (ANY, VMEM, VMEM, VMEM),
            scatter_scratch(n_c, half, width) * 2
            + [pltpu.VMEM((half, width), BF)]
            + gather_sems(n_c)
            + collect_scratch(n_f, 3, height, ff_cols),
            vmem=56,
        )(
            act_two_part.reshape(rows_bf.shape),
            branch_part.reshape(rows_bf.shape),
            resid_mid,
            own_cot,
            ff_grad,
        )
        mid_rows = mid_rows.reshape(pack_len, width)

        act_one_part, att_grad = local(
            backward_kernel,
            "backward",
            (rows_flat, jax.ShapeDtypeStruct(att_w.shape, BF)),
            [
                pltpu.VMEM((width, 4 * rank_width), BF),
                pltpu.VMEM((pack_len, 3 * rank_width), BF),
                pltpu.VMEM((pack_len, HEAD_DIM), F32),
                pltpu.VMEM((pack_len, HEAD_DIM), F32),
            ],
        )(mid_rows, act_one, att_w, *tables, qkv, attended, mass)
        input_grad, block_out, att_total, ff_total = call(
            fourth_kernel,
            "fourth",
            3,
            (
                jax.ShapeDtypeStruct((n_t, half, width), F32),
                jax.ShapeDtypeStruct((n_t, half, width), BF),
                jax.ShapeDtypeStruct(att_low.shape, BF),
                jax.ShapeDtypeStruct(ff_low.shape, BF),
            ),
            [ANY, VMEM, VMEM, ANY, ANY, ANY],
            (ANY,) * 4,
            scatter_scratch(n_c, half, width)
            + [pltpu.VMEM((4, height, att_cols), BF), pltpu.VMEM((half, width), F32)]
            + [dma(n_c), dma(n_c), pltpu.SemaphoreType.DMA] * 2
            + [
                pltpu.SemaphoreType.DMA((2, n_t - 1)),
                pltpu.SemaphoreType.DMA((2, n_t - 1)),
                dma(2),
            ]
            + collect_scratch(n_f, 4, height, att_cols),
        )(
            act_one_part.reshape(rows_bf.shape),
            own_tokens,
            mid_grad,
            block_own,
            att_grad,
            ff_sum,
        )
        att_total, ff_total = att_total.astype(F32), ff_total.astype(F32)

        square = jnp.sum(att_total * att_total) + jnp.sum(ff_total * ff_total)
        count = n_f + n_c + n_t
        square_sum = call(
            norm_kernel,
            "norm",
            4,
            jax.ShapeDtypeStruct((8, 128), F32),
            [VMEM],
            VMEM,
            [pltpu.VMEM((k, 8, 128), F32) for k in (4, n_t - 1, n_c - 1, n_f - 1)]
            + [dma(count), dma(count)],
            vmem=8,
        )(jnp.broadcast_to(square, (8, 128)))[0, 0]
        norm_value = jnp.sqrt(square_sum)
        clip_factor = jnp.minimum(1.0, MAX_NORM / (norm_value + 1e-06))
        base_rate = width ** (-0.5)
        out_rate = (width // 32) ** (-0.5)
        grads = (att_total[:3], att_total[3], ff_total[:2], ff_total[2])
        weights = (att_proj, attn_out, ff_proj, ff_out)
        firsts_old = (att_proj_first, attn_out_first, ff_proj_first, ff_out_first)
        seconds_old = (att_proj_second, attn_out_second, ff_proj_second, ff_out_second)
        rates = (base_rate, out_rate, base_rate, base_rate)
        news = [
            adam_step(w, g, m, v, clip_factor, r)
            for w, g, m, v, r in zip(weights, grads, firsts_old, seconds_old, rates)
        ]
        return (
            block_out.reshape(tokens.shape),
            input_grad.reshape(tokens.shape),
            norm_value.reshape(1),
            *grads,
            *(n[0] for n in news),
            *(n[1] for n in news),
            *(n[2] for n in news),
            *(n[2].astype(BF) for n in news),
        )

    return shards


def solution(mesh):
    act = P("fsdp", "ctx", None)
    table = P("fsdp", None)
    cube = P(None, ("fsdp", "ctx"), "tp")
    flat = P(("fsdp", "ctx"), "tp")
    group = (cube, flat, cube, flat)
    in_specs = (act, act, table, table) + group * 3
    out_specs = (act, act, P()) + group * 5
    return jax.shard_map(
        make_shards(mesh), mesh=mesh, in_specs=in_specs, out_specs=out_specs, check_vma=False
    )
```

```python
import functools

import jax
import jax.numpy as jnp
from jax import lax
from jax.experimental import pallas as pl
from jax.experimental.pallas import tpu as pltpu
from jax.sharding import PartitionSpec as P

HEAD_DIM = 128
STEP = 10
EPS_NORM = 1e-05
BETA_ONE = 0.9
BETA_TWO = 0.95
EPS_ADAM = 1e-08
DECAY = 0.1
MAX_NORM = 1.0
NEG_FILL = -1e30
BF = jnp.bfloat16
F32 = jnp.float32
MESH = pl.DeviceIdType.MESH
ANY = pl.BlockSpec(memory_space=pl.ANY)
VMEM = pl.BlockSpec(memory_space=pltpu.VMEM)
ROWS = 16
QUERIES = 256
SCORE_SCALE = HEAD_DIM ** (-0.5)


def mean_spread(values):
    centre = values - jnp.mean(values, axis=-1, keepdims=True)
    spread = jnp.mean(centre * centre, axis=-1, keepdims=True)
    scale = lax.rsqrt(spread + EPS_NORM)
    return centre * scale, scale


def norm_back(grad, normed, scale):
    return scale * (
        grad
        - jnp.mean(grad, axis=-1, keepdims=True)
        - normed * jnp.mean(grad * normed, axis=-1, keepdims=True)
    )


def dot(left, right, dims):
    return lax.dot_general(left, right, (dims, ((), ())), preferred_element_type=F32)


def adam_step(weight, grad_sum, first, second, clip_factor, learn_rate):
    clipped = grad_sum * clip_factor
    first_new = BETA_ONE * first + (1.0 - BETA_ONE) * clipped
    second_new = BETA_TWO * second + (1.0 - BETA_TWO) * clipped * clipped
    first_hat = first_new / (1.0 - BETA_ONE**STEP)
    second_hat = second_new / (1.0 - BETA_TWO**STEP)
    weight_new = weight - learn_rate * (
        first_hat / (jnp.sqrt(second_hat) + EPS_ADAM) + DECAY * weight
    )
    return (first_new, second_new, weight_new)


class Place:
    def __init__(self, sizes):
        self.n_f, self.n_c, self.n_t = sizes
        self.f, self.c, self.t = (lax.axis_index(a) for a in ("fsdp", "ctx", "tp"))
        self.hi, self.lo = self.t // 2, lax.rem(self.t, 2)
        self.core = (self.f, self.c, self.t + 1 - 2 * self.lo)
        self.block = self.c * 2 + self.lo
        self.pairs = [(s, o) for o in range(2) for s in range(self.n_f) if s or o]

    def ctx(self, shift):
        return lax.rem(self.c + shift + self.n_c, self.n_c)

    def fsdp(self, shift):
        return lax.rem(self.f + shift + self.n_f, self.n_f)

    def other(self, o):
        return self.hi + o * (1 - 2 * self.hi)

    def z(self, shift):
        return (self.f, self.ctx(shift), self.t)

    def xy(self, shift, o):
        return (self.fsdp(shift), self.c, self.t + o * (2 - 4 * self.hi))

    def greet(self, peers):
        barrier = pltpu.get_barrier_semaphore()
        for peer in peers:
            pl.semaphore_signal(barrier, inc=1, device_id=peer, device_id_type=MESH)
        pl.semaphore_wait(barrier, len(peers))

    def all_z(self):
        return [self.z(s) for s in range(1, self.n_c)]

    def all_xy(self):
        return [self.xy(s, o) for s, o in self.pairs]


def remote(src, dst, send, recv, peer):
    return pltpu.make_async_remote_copy(
        src_ref=src, dst_ref=dst, send_sem=send, recv_sem=recv, device_id=peer, device_id_type=MESH
    )


def by_rows(count, step):
    @pl.loop(0, count // ROWS)
    def _(i):
        step(pl.ds(pl.multiple_of(i * ROWS, ROWS), ROWS))


class Gather:
    def __init__(self, at, src, out, send, recv, local):
        self.at, self.src, self.out, self.send, self.recv = at, src, out, send, recv
        self.local = pltpu.make_async_copy(src, out.at[at.block], local)

    def far(self, way, hop, src=None):
        at = self.at
        block = self.out.at[jnp.clip(at.c - way * (hop - 1), 0, at.n_c - 1) * 2 + at.lo]
        k = hop + (0 if way > 0 else at.n_c)
        return remote(
            block if src is None else src, block, self.send.at[k], self.recv.at[k], at.z(way)
        )

    def near(self, distance, src=None):
        at = self.at
        block = self.out.at[jnp.clip(at.c - distance, 0, at.n_c - 1) * 2 + at.lo]
        k = 2 * at.n_c + distance + at.n_c
        return remote(
            block if src is None else src, block, self.send.at[k], self.recv.at[k], at.core
        )

    def there(self, way, hop):
        return self.at.c + hop < self.at.n_c if way > 0 else self.at.c >= hop

    def start(self):
        for way in (1, -1):

            @pl.when(self.there(way, 1))
            def _(way=way):
                self.far(way, 1, self.src).start()

        self.near(0, self.src).start()
        self.local.start()

    def forward(self, hops=None):
        at = self.at
        for hop in hops or range(1, at.n_c):
            for way in (1, -1):

                @pl.when(self.there(-way, hop))
                def _(way=way, hop=hop):
                    self.far(way, hop).wait_recv()
                    if hop < at.n_c - 1:

                        @pl.when(self.there(way, 1))
                        def _():
                            self.far(way, hop + 1).start()

                    self.near(way * hop).start()

    def finish(self):
        at = self.at
        for hop in range(1, at.n_c):
            for way in (1, -1):

                @pl.when(self.there(way, 1) & self.there(-way, hop - 1))
                def _(way=way, hop=hop):
                    self.far(way, hop).wait_send()

                @pl.when(self.there(-way, hop))
                def _(way=way, hop=hop):
                    self.near(way * hop).wait()

        self.near(0, self.src).wait()
        self.local.wait()


def gather_sems(n_c):
    return [
        pltpu.SemaphoreType.DMA((4 * n_c,)),
        pltpu.SemaphoreType.DMA((4 * n_c,)),
        pltpu.SemaphoreType.DMA,
    ]


class Scatter:
    def __init__(self, at, part, near, sent, got, send, recv):
        self.at, self.part, self.near = at, part, near
        self.sent, self.got, self.send, self.recv = sent, got, send, recv

    def core(self, c):
        at = self.at
        return remote(
            self.part.at[c * 2 + 1 - at.lo], self.near.at[c], self.send.at[c], self.recv.at[c], at.core
        )

    def far(self, way, hop, slot):
        at = self.at
        k = at.n_c + hop + (0 if way > 0 else at.n_c)
        sent = self.sent.at[jnp.clip(at.c + way * hop, 0, at.n_c - 1)]
        return remote(sent, self.got.at[slot], self.send.at[k], self.recv.at[k], at.z(way))

    def end(self, way):
        return self.at.n_c + (0 if way > 0 else 1)

    there = Gather.there

    def start(self):
        at = self.at
        for i in range(at.n_c):
            self.core(jnp.where(at.c * 2 < at.n_c, at.n_c - 1 - i, i)).start()

    def pass_on(self, hops=None):
        at = self.at
        for hop in hops or range(at.n_c - 1, 0, -1):
            for way in (1, -1):

                @pl.when(self.there(way, hop))
                def _(way=way, hop=hop):
                    c = at.c + way * hop
                    self.core(c).wait_recv()
                    if hop < at.n_c - 1:
                        more = self.there(-way, 1)

                        @pl.when(more)
                        def _():
                            self.far(way, hop + 1, c).wait_recv()
                            self.add(c, True)

                        @pl.when(jnp.logical_not(more))
                        def _():
                            self.add(c, False)

                    else:
                        self.add(c, False)
                    self.far(way, hop, self.end(way) if hop == 1 else c).start()

    def add(self, c, more):
        at = self.at

        def rows_of(rows):
            value = self.part[c * 2 + at.lo, rows].astype(F32) + self.near[c, rows].astype(F32)
            if more:
                value = value + self.got[c, rows].astype(F32)
            self.sent[c, rows] = value.astype(BF)

        by_rows(self.near.shape[1], rows_of)

    def arrive(self):
        self.core(self.at.c).wait_recv()
        for way in (1, -1):

            @pl.when(self.there(-way, 1))
            def _(way=way):
                self.far(way, 1, self.end(way)).wait_recv()

            @pl.when(jnp.logical_not(self.there(-way, 1)))
            def _(way=way):
                self.got[self.end(way)] = jnp.zeros(self.got.shape[1:], BF)

    def total(self, rows):
        c, at = self.at.c, self.at
        return (
            self.part[c * 2 + at.lo, rows].astype(F32)
            + self.near[c, rows].astype(F32)
            + self.got[self.end(1), rows].astype(F32)
            + self.got[self.end(-1), rows].astype(F32)
        )

    def finish(self):
        at = self.at
        for c in range(at.n_c):
            self.core(c).wait_send()
        for hop in range(1, at.n_c):
            for way in (1, -1):

                @pl.when(self.there(way, hop))
                def _(way=way, hop=hop):
                    self.far(way, hop, 0).wait_send()


def scatter_scratch(n_c, half, width):
    return [
        pltpu.VMEM((2 * n_c, half, width), BF),
        pltpu.VMEM((n_c, half, width), BF),
        pltpu.VMEM((n_c, half, width), BF),
        pltpu.VMEM((n_c + 2, half, width), BF),
        pltpu.SemaphoreType.DMA((3 * n_c,)),
        pltpu.SemaphoreType.DMA((3 * n_c,)),
    ]


class Swap:
    def __init__(self, at, shard, full, send, recv, local):
        self.at = at
        rows, width = shard.shape[1], full.shape[3]
        here = pl.ds((at.f * at.n_c + at.c) * rows, rows)
        target = full.at[at.hi, :, here, :]

        def columns(c):
            return shard.at[:, :, pl.ds(pl.multiple_of(c * width, 128), width)]

        self.local = pltpu.make_async_copy(columns(at.c), target, local)
        self.far = [
            remote(columns(at.ctx(s)), target, send.at[s], recv.at[s], at.z(s))
            for s in range(1, at.n_c)
        ]

    def start(self):
        self.local.start()
        for copy in self.far:
            copy.start()

    def wait(self):
        self.local.wait()
        for copy in self.far:
            copy.wait()


class Spread:
    def __init__(self, at, full, send, recv):
        self.at, self.full, self.send, self.recv = at, full, send, recv
        self.height = full.shape[2] // at.n_f // 2

    def part(self, o, shift, half):
        at = self.at
        first = (at.fsdp(shift) * 2 + half) * self.height
        return self.full.at[at.other(o), :, pl.ds(first, self.height), :]

    def copy(self, part, k, peer):
        return remote(part, part, self.send.at[k], self.recv.at[k], peer)

    def copies(self):
        at = self.at
        n = at.n_f
        return [
            *(
                self.copy(self.part(0, 0, h), h * n + s, at.xy(s, 0))
                for h in range(2)
                for s in range(1, n)
            ),
            *(self.copy(self.part(0, 0, h), 2 * n + h, at.xy(0, 1)) for h in (1, 0)),
        ]

    def passes(self):
        at = self.at
        n = at.n_f
        return [
            *(self.copy(self.part(0, -s, 0), 3 * n + s, at.xy(0, 1)) for s in range(1, n)),
            *(self.copy(self.part(1, 0, 1), 4 * n + s, at.xy(s, 0)) for s in range(1, n)),
        ]

    def start(self):
        for copy in self.copies():
            copy.start()

    def forward(self):
        copies, n = self.copies(), self.at.n_f
        for copy in copies[: n - 1]:
            copy.wait_recv()
        copies[2 * n - 2].wait_recv()
        for copy in self.passes():
            copy.start()

    def wait(self):
        copies, n = self.copies(), self.at.n_f
        for copy in copies[n - 1 : 2 * n - 2]:
            copy.wait_recv()
        copies[2 * n - 1].wait_recv()
        for copy in copies:
            copy.wait_send()
        for copy in self.passes():
            copy.wait()


class Collect:
    def __init__(self, at, partial, mine, by_x, by_y, pass_x, pass_y, part_x, part_y, send, recv, local):
        self.at, self.partial, self.mine, self.by_x, self.by_y = at, partial, mine, by_x, by_y
        self.pass_x, self.pass_y, self.part_x, self.part_y = pass_x, pass_y, part_x, part_y
        self.send, self.recv, self.local = send, recv, local
        self.height = partial.shape[2] // at.n_f // 2

    def part(self, o, shift, half):
        at = self.at
        first = (at.fsdp(shift) * 2 + half) * self.height
        return self.partial.at[at.other(o), :, pl.ds(first, self.height), :]

    def half(self, ref, half):
        return ref.at[:, pl.ds(half * self.height, self.height), :]

    def copy(self, src, dst, k, peer):
        return remote(src, dst, self.send.at[k], self.recv.at[k], peer)

    def raw(self):
        at = self.at
        n, shifts = at.n_f, range(1, at.n_f)
        return [
            [self.copy(self.part(1, s, 0), self.pass_x.at[s - 1], s, at.xy(s, 0)) for s in shifts],
            [self.copy(self.part(1, s, 1), self.pass_y.at[s - 1], n + s, at.xy(0, 1)) for s in shifts],
            [
                *(
                    self.copy(self.part(0, s, 0), self.half(self.by_x.at[s - 1], 0), 2 * n + s, at.xy(s, 0))
                    for s in shifts
                ),
                self.copy(self.part(1, 0, 1), self.half(self.by_y, 1), 0, at.xy(0, 1)),
            ],
        ]

    def added(self):
        at = self.at
        n, shifts = at.n_f, range(1, at.n_f)
        return [
            self.copy(self.part_y, self.half(self.by_y, 0), n, at.xy(0, 1)),
            *(
                self.copy(self.part_x.at[s - 1], self.half(self.by_x.at[s - 1], 1), 3 * n + s, at.xy(s, 0))
                for s in shifts
            ),
        ]

    def keeps(self):
        first = self.at.f * 2 * self.height
        own = self.partial.at[self.at.hi, :, pl.ds(first, 2 * self.height), :]
        return [
            pltpu.make_async_copy(own, self.mine, self.local.at[0]),
            pltpu.make_async_copy(self.part(1, 0, 0), self.part_y, self.local.at[1]),
            *(
                pltpu.make_async_copy(self.part(0, s, 1), self.part_x.at[s - 1], self.local.at[1 + s])
                for s in range(1, self.at.n_f)
            ),
        ]

    def start(self):
        for copies in self.raw():
            for copy in copies:
                copy.start()
        for copy in self.keeps():
            copy.start()

    def forward(self):
        raw, added, keeps = self.raw(), self.added(), self.keeps()
        for copy in (*raw[0], keeps[1]):
            copy.wait() if copy is keeps[1] else copy.wait_recv()
        n = self.at.n_f
        for m in range(self.mine.shape[0]):

            def add_y(rows, m=m):
                value = self.part_y[m, rows].astype(F32)
                for s in range(n - 1):
                    value = value + self.pass_x[s, m, rows].astype(F32)
                self.part_y[m, rows] = value.astype(BF)

            by_rows(self.height, add_y)
        added[0].start()
        for s in range(1, n):
            raw[1][s - 1].wait_recv()
            keeps[1 + s].wait()
            for m in range(self.mine.shape[0]):

                def add_x(rows, m=m, s=s):
                    self.part_x[s - 1, m, rows] = (
                        self.part_x[s - 1, m, rows].astype(F32) + self.pass_y[s - 1, m, rows].astype(F32)
                    ).astype(BF)

                by_rows(self.height, add_x)
            added[s].start()

    def total(self, out):
        raw, added = self.raw(), self.added()
        for copy in (*raw[2], *added):
            copy.wait_recv()
        self.keeps()[0].wait()
        for m in range(self.mine.shape[0]):

            def add(rows, m=m):
                value = self.mine[m, rows].astype(F32) + self.by_y[m, rows].astype(F32)
                for s in range(self.at.n_f - 1):
                    value = value + self.by_x[s, m, rows].astype(F32)
                out[m, rows] = value.astype(BF)

            by_rows(2 * self.height, add)

    def finish(self):
        for copies in (*self.raw(), self.added()):
            for copy in copies:
                copy.wait_send()


def collect_scratch(n_f, matrices, height, columns):
    half = (matrices, height // 2, columns)
    return [
        pltpu.VMEM((matrices, height, columns), BF),
        pltpu.VMEM((n_f - 1, matrices, height, columns), BF),
        pltpu.VMEM((matrices, height, columns), BF),
        pltpu.VMEM((n_f - 1, *half), BF),
        pltpu.VMEM((n_f - 1, *half), BF),
        pltpu.VMEM((n_f - 1, *half), BF),
        pltpu.VMEM(half, BF),
        dma(4 * n_f),
        dma(4 * n_f),
        dma(n_f + 1),
    ]


class Return:
    def __init__(self, at, summed, shard, send, recv, local):
        rows, width = shard.shape[1], summed.shape[2]
        target = shard.at[:, :, pl.ds(pl.multiple_of(at.c * width, 128), width)]

        def part(c):
            return summed.at[:, pl.ds(pl.multiple_of(c * rows, rows), rows), :]

        self.local = pltpu.make_async_copy(part(at.c), target, local)
        self.far = [
            remote(part(at.ctx(s)), target, send.at[s], recv.at[s], at.z(s))
            for s in range(1, at.n_c)
        ]

    start = Swap.start
    wait = Swap.wait


def pack_weights(w, packed):
    heads = w.shape[0]
    for i in range(4):
        for y in range(heads):
            k = (i * heads + y) * HEAD_DIM
            packed[:, k : k + HEAD_DIM] = w[y, i]


def turn(values, cos, sine):
    return values * cos + pltpu.roll(values, HEAD_DIM // 2, 1) * sine


def round_all(wide, low):
    for m in range(wide.shape[0]):

        def step(rows, m=m):
            low[m, rows] = wide[m, rows].astype(BF)

        by_rows(wide.shape[1], step)


def dma(count):
    return pltpu.SemaphoreType.DMA((count,))


def make_shards(mesh):
    sizes = tuple(mesh.shape[a] for a in ("fsdp", "ctx", "tp"))
    n_f, n_c, n_t = sizes

    def call(kernel, name, collective, outs, ins, out_specs, scratch, aliases=None, vmem=40):
        return pl.pallas_call(
            kernel,
            out_shape=outs,
            in_specs=ins,
            out_specs=out_specs,
            scratch_shapes=scratch,
            input_output_aliases=aliases or {},
            compiler_params=pltpu.CompilerParams(
                collective_id=collective, has_side_effects=True, vmem_limit_bytes=vmem << 20
            ),
            name=name,
        )

    def local(kernel, name, outs, scratch):
        return pl.pallas_call(
            kernel,
            out_shape=outs,
            scratch_shapes=scratch,
            compiler_params=pltpu.CompilerParams(vmem_limit_bytes=60 << 20),
            name=name,
        )

    def front_kernel(
        tok_ref, cot_ref, place, key_place, first, cos, sine, att_ref, out_ref, ffp_ref, ffo_ref,
        rows_ref, attw_ref, ffw_ref, a2_ref, cots_ref, qkv, attended, mass, mid_ref,
        x_ref, own_cot, att_wide, ff_wide, att_low, ff_low, low, a1, packed, lk, lp,
        part, near, sent, got, ss, sr, g1, h1, l1, g2, h2, l2, g3, h3, l3, s4, r4, l4, s5, r5, l5, s6, r6, s7, r7,
    ):
        at = Place(sizes)
        half = x_ref.shape[0]
        mine = pl.ds(pl.multiple_of(at.lo * half, half), half)
        loads = [
            pltpu.make_async_copy(tok_ref.at[at.hi, mine], x_ref, lk.at[0]),
            pltpu.make_async_copy(att_ref, att_wide.at[pl.ds(0, 3)], lk.at[1]),
            pltpu.make_async_copy(out_ref, att_wide.at[3], lk.at[2]),
            pltpu.make_async_copy(ffp_ref, ff_wide.at[pl.ds(0, 2)], lk.at[3]),
            pltpu.make_async_copy(ffo_ref, ff_wide.at[2], lk.at[4]),
            pltpu.make_async_copy(cot_ref.at[at.hi, mine], own_cot, lk.at[5]),
        ]
        for copy in loads:
            copy.start()
        scatter = Scatter(at, part, near, sent, got, ss, sr)
        gather = Gather(at, low, rows_ref, g1, h1, l1)
        cots = Gather(at, own_cot, cots_ref, g2, h2, l2)
        a2 = Gather(at, low, a2_ref, g3, h3, l3)
        swap_att = Swap(at, att_low, attw_ref, s4, r4, l4)
        swap_ff = Swap(at, ff_low, ffw_ref, s5, r5, l5)
        spread_att = Spread(at, attw_ref, s6, r6)
        spread_ff = Spread(at, ffw_ref, s7, r7)
        loads[0].wait()

        def norm_one(rows):
            low[rows] = mean_spread(x_ref[rows].astype(F32))[0].astype(BF)

        by_rows(half, norm_one)
        loads[1].wait()
        loads[2].wait()
        round_all(att_wide, att_low)
        at.greet([at.core, *at.all_z(), *at.all_xy()])
        gather.start()
        swap_att.start()
        for copy in loads[3:]:
            copy.wait()
        round_all(ff_wide, ff_low)
        gather.forward(range(1, 2))
        swap_att.wait()
        spread_att.start()
        gather.forward(range(2, n_c - 1))
        swap_ff.start()
        gather.forward(range(n_c - 1, n_c))
        spread_att.forward()
        gather.finish()
        take = [pltpu.make_async_copy(rows_ref.at[b], a1.at[pl.ds(b * half, half)], lp.at[b]) for b in range(2 * n_c)]
        for copy in take:
            copy.start()
        spread_att.wait()
        heads = attw_ref.shape[0]
        packs = [
            pltpu.make_async_copy(
                attw_ref.at[y, i],
                packed.at[:, pl.ds((i * heads + y) * HEAD_DIM, HEAD_DIM)],
                lp.at[2 * n_c + i * heads + y],
            )
            for i in range(4)
            for y in range(heads)
        ]
        for copy in packs:
            copy.start()
        for copy in (*take, *packs):
            copy.wait()
        attend(a1, packed, place, key_place, first, cos, sine, qkv, attended, mass, part)
        scatter.start()
        scatter.pass_on(range(n_c - 1, 1, -1))
        swap_ff.wait()
        spread_ff.start()
        scatter.pass_on(range(1, 2))
        cots.start()
        scatter.arrive()

        def norm_two(rows):
            mid = x_ref[rows].astype(F32) + scatter.total(rows)
            mid_ref[rows] = mid
            low[rows] = mean_spread(mid)[0].astype(BF)

        by_rows(half, norm_two)
        a2.start()
        cots.forward(range(1, 2))
        a2.forward(range(1, 2))
        spread_ff.forward()
        for hop in range(2, n_c):
            a2.forward(range(hop, hop + 1))
            cots.forward(range(hop, hop + 1))
        cots.finish()
        a2.finish()
        scatter.finish()
        spread_ff.wait()

    def third_kernel(
        part_ref, branch_ref, mid_ref, cot_ref, grad_ref, rows_ref, block_ref, own_ref, sum_ref,
        part, near, sent, got, ss, sr, part2, near2, sent2, got2, ss2, sr2, ls, low, s1, r1, l1, *collected,
    ):
        at = Place(sizes)
        loads = [
            pltpu.make_async_copy(part_ref, part, ls.at[0]),
            pltpu.make_async_copy(branch_ref, part2, ls.at[1]),
        ]
        for copy in loads:
            copy.start()
        at.greet([at.core, *at.all_z(), *at.all_xy()])
        scatter = Scatter(at, part, near, sent, got, ss, sr)
        branch = Scatter(at, part2, near2, sent2, got2, ss2, sr2)
        for copy in loads:
            copy.wait()
        collect = Collect(at, grad_ref, *collected)
        scatter.start()
        collect.start()
        scatter.pass_on()
        branch.start()
        scatter.arrive()

        def norm(rows):
            normed, scale = mean_spread(mid_ref[rows])
            grad = cot_ref[rows].astype(F32) + norm_back(scatter.total(rows), normed, scale)
            own_ref[rows] = grad
            low[rows] = grad.astype(BF)

        by_rows(mid_ref.shape[0], norm)
        gather = Gather(at, low, rows_ref, s1, r1, l1)
        gather.start()
        branch.pass_on()
        gather.forward(range(1, 2))
        collect.forward()
        gather.forward(range(2, n_c))
        branch.arrive()

        def add(rows):
            block_ref[rows] = (mid_ref[rows] + branch.total(rows)).astype(BF)

        by_rows(mid_ref.shape[0], add)
        gather.finish()
        scatter.finish()
        branch.finish()
        collect.total(sum_ref)
        collect.finish()

    def fourth_kernel(
        part_ref, x_ref, mid_ref, block_ref, att_ref, ff_ref, input_ref, out_ref, attg_ref, ffg_ref,
        part, near, sent, got, ss, sr, total, low, s1, r1, l1, s2, r2, l2, s4, r4, l4, *collected,
    ):
        at = Place(sizes)
        load = pltpu.make_async_copy(part_ref, part, l4.at[2])
        load.start()
        tps = [(at.f, at.c, lax.rem(at.t + s, n_t)) for s in range(1, n_t)]
        at.greet([*tps, *at.all_z(), *[at.xy(s, o) for s, o in at.pairs if s]])
        load.wait()
        scatter = Scatter(at, part, near, sent, got, ss, sr)
        collect = Collect(at, att_ref, *collected)
        give_ff = Return(at, ff_ref, ffg_ref, s2, r2, l2)
        scatter.start()
        collect.start()

        def tp_gather(src, dst, k):
            copies = [
                remote(src, dst.at[at.t], s4.at[k, i], r4.at[k, i], peer) for i, peer in enumerate(tps)
            ]
            keep = pltpu.make_async_copy(src, dst.at[at.t], l4.at[k])
            for copy in (*copies, keep):
                copy.start()
            return [*copies, keep]

        scatter.pass_on()
        give_ff.start()
        collect.forward()
        waits = tp_gather(block_ref, out_ref, 0)
        collect.total(total)
        give_att = Return(at, total, attg_ref, s1, r1, l1)
        give_att.start()
        scatter.arrive()

        def norm(rows):
            normed, scale = mean_spread(x_ref[rows].astype(F32))
            low[rows] = mid_ref[rows] + norm_back(scatter.total(rows), normed, scale)

        by_rows(mid_ref.shape[0], norm)
        waits += tp_gather(low, input_ref, 1)
        for copy in waits:
            copy.wait()
        scatter.finish()
        collect.finish()
        give_att.wait()
        give_ff.wait()

    def norm_kernel(attg_ref, ffg_ref, norm_ref, low_att, low_ff, total, got_t, got_c, got_f, send, recv, ls):
        at = Place(sizes)
        loads = [
            pltpu.make_async_copy(attg_ref, low_att, ls.at[0]),
            pltpu.make_async_copy(ffg_ref, low_ff, ls.at[1]),
        ]
        for copy in loads:
            copy.start()
        tps = [(at.f, at.c, lax.rem(at.t + s, n_t)) for s in range(1, n_t)]
        fs = [at.xy(s, 0) for s in range(1, n_f)]
        at.greet([*tps, *at.all_z(), *fs])
        for copy in loads:
            copy.wait()
        sum_norm(at, (low_att, low_ff), norm_ref, total, got_t, got_c, got_f, send, recv)

    def sum_norm(at, grads, norm_ref, total, got_t, got_c, got_f, send, recv):
        tps = [(at.f, at.c, lax.rem(at.t + s, n_t)) for s in range(1, n_t)]
        fs = [at.xy(s, 0) for s in range(1, n_f)]
        total[0] = jnp.zeros(total.shape[1:], F32)
        for low in grads:
            for m in range(low.shape[0]):

                def square(rows, low=low, m=m):
                    value = low[m, rows].astype(F32)
                    value = value * value
                    value = value[: ROWS // 2] + value[ROWS // 2 :]
                    lanes = value[:, :128]
                    for c in range(1, value.shape[1] // 128):
                        lanes = lanes + value[:, c * 128 : (c + 1) * 128]
                    total[0] += lanes

                by_rows(low.shape[1], square)
        base = 0
        stages = ((tps, got_t, at.t), (at.all_z(), got_c, at.c), (fs, got_f, at.f))
        for stage, (peers, got, place) in enumerate(stages):
            copies = [
                remote(total.at[stage], got.at[place], send.at[base + i], recv.at[base + i], peer)
                for i, peer in enumerate(peers)
            ]
            base += len(peers)
            for copy in copies:
                copy.start()
            got[place] = total[stage]
            for copy in copies:
                copy.wait()
            value = got[0]
            for i in range(1, got.shape[0]):
                value = value + got[i]
            total[stage + 1] = value
        norm = jnp.sqrt(jnp.sum(total[3], axis=(0, 1), keepdims=True))
        norm_ref[...] = jnp.broadcast_to(norm, norm_ref.shape)

    def finish_kernel(norm_ref, block_in, input_in, attg_ref, ffg_ref, *refs):
        olds, outs, scratch = refs[:12], refs[12:34], refs[34:]
        low_att, low_ff, wide_att, wide_ff, old_att, old_ff, block_keep, input_keep, ls = scratch
        groups = (
            (attg_ref, low_att, wide_att, old_att, 0, attg_ref.shape[1]),
            (ffg_ref, low_ff, wide_ff, old_ff, 2, attg_ref.shape[1] // 4),
        )
        chunks = [
            (group, m, r)
            for group in groups
            for m in range(group[0].shape[0])
            for r in range(group[0].shape[1] // group[5])
        ]

        def sheet(array, first, m, group):
            last = group[0].shape[0] - 1
            return array[first + 1] if m == last else array[first].at[m]

        loads, stores = [], []
        for i, (group, m, r) in enumerate(chunks):
            here = pl.ds(r * group[5], group[5])
            one = [pltpu.make_async_copy(group[0].at[m, here], group[1].at[m, here], ls.at[i, 0, 3])]
            one += [
                pltpu.make_async_copy(
                    sheet(olds, 4 * j + group[4], m, group).at[here], group[3].at[j, m, here], ls.at[i, 0, j]
                )
                for j in range(3)
            ]
            for copy in one:
                copy.start()
            loads.append(one)
        kept = ((block_in, block_keep, outs[20]), (input_in, input_keep, outs[21]))
        through = []
        for i, (src, keep, out) in enumerate(kept):
            copy = pltpu.make_async_copy(src, keep, ls.at[len(chunks), 0, i])
            copy.start()
            through.append((copy, pltpu.make_async_copy(keep, out, ls.at[len(chunks), 1, i])))
        norm = norm_ref[0:1, 0:1]
        clip = jnp.minimum(1.0, MAX_NORM / (norm + 1e-06))
        width = ffg_ref.shape[1] * n_f * n_c
        for i, (group, m, r) in enumerate(chunks):
            for copy in loads[i]:
                copy.wait()
            low, wide, old = group[1:4]
            rate = (width // 32) ** (-0.5) if group[4] == 0 and m == 3 else width ** (-0.5)

            @pl.loop(0, group[5] // ROWS)
            def _(k, low=low, wide=wide, old=old, m=m, r=r, step=group[5], rate=rate):
                rows = pl.ds(pl.multiple_of(r * step + k * ROWS, ROWS), ROWS)
                grad = low[m, rows].astype(F32)
                wide[m, rows] = grad
                first_new, second_new, weight_new = adam_step(
                    old[0, m, rows], grad, old[1, m, rows], old[2, m, rows], clip, rate
                )
                old[0, m, rows] = weight_new
                old[1, m, rows] = first_new
                old[2, m, rows] = second_new
                low[m, rows] = weight_new.astype(BF)

            here = pl.ds(r * group[5], group[5])
            for k, (src, out) in enumerate(
                ((wide, 0), (old.at[1], 4), (old.at[2], 8), (old.at[0], 12), (low, 16))
            ):
                store = pltpu.make_async_copy(
                    src.at[m, here], sheet(outs, out + group[4], m, group).at[here], ls.at[i, 1, k]
                )
                store.start()
                stores.append(store)
        for load, store in through:
            load.wait()
            store.start()
            stores.append(store)
        for store in stores:
            store.wait()

    def attend(a1, packed, place, key_place, first, cos, sine, qkv, attended, mass, part):
        wide = attended.shape[1]
        heads = wide // HEAD_DIM
        for i in range(3):
            joint = dot(a1[...], packed[:, i * wide : (i + 1) * wide], ((1,), (0,)))
            for y in range(heads):
                cols = slice(y * HEAD_DIM, (y + 1) * HEAD_DIM)
                head = joint[:, cols]
                if i < 2:
                    head = turn(head, cos[...], sine[...])
                qkv[i, :, cols] = head.astype(BF)
        for y in range(heads):
            cols = slice(y * HEAD_DIM, (y + 1) * HEAD_DIM)

            @pl.loop(0, a1.shape[0] // QUERIES)
            def _(c, y=y, cols=cols):
                rows = pl.ds(pl.multiple_of(c * QUERIES, QUERIES), QUERIES)
                scores = dot(qkv[0, rows, cols], qkv[1, :, cols], ((1,), (1,))) * SCORE_SCALE
                allowed = (key_place[...] <= place[rows]) & (key_place[...] >= first[rows])
                scores = jnp.where(allowed, scores, NEG_FILL)
                peak = jnp.max(scores, axis=1, keepdims=True)
                exp_scores = jnp.exp(scores - peak)
                total = jnp.sum(exp_scores, axis=1, keepdims=True)
                probs = (exp_scores * (1.0 / total)).astype(BF)
                attended[rows, cols] = dot(probs, qkv[2, :, cols], ((1,), (0,))).astype(BF)
                mass[rows, y : y + 1] = peak + jnp.log(total)

        width = part.shape[2] // 4

        @pl.loop(0, 4)
        def _(c):
            cols = pl.ds(pl.multiple_of(c * width, width), width)
            value = dot(attended[...], packed[cols, 3 * wide :], ((1,), (1,))).astype(BF)
            part[:, :, cols] = value.reshape(part.shape[0], part.shape[1], width)

    def backward_kernel(
        mid, a1, w, place, key_place, first, cos, sine, qkv, attended, mass, part, grad, packed, joint, d_v, d_k
    ):
        heads = w.shape[0]
        wide = heads * HEAD_DIM
        pack_weights(w, packed)
        joint[:, :wide] = dot(mid[...], packed[:, 3 * wide :], ((1,), (0,))).astype(BF)
        for y in range(heads):
            cols = slice(y * HEAD_DIM, (y + 1) * HEAD_DIM)

            @pl.loop(0, a1.shape[0] // QUERIES)
            def _(c, y=y, cols=cols):
                rows = pl.ds(pl.multiple_of(c * QUERIES, QUERIES), QUERIES)
                query, key, value = qkv[0, rows, cols], qkv[1, :, cols], qkv[2, :, cols]
                d_att = joint[rows, cols]
                scores = dot(query, key, ((1,), (1,))) * SCORE_SCALE
                allowed = (key_place[...] <= place[rows]) & (key_place[...] >= first[rows])
                probs = jnp.exp(jnp.where(allowed, scores, NEG_FILL) - mass[rows, y : y + 1])
                d_prob = dot(d_att, value, ((1,), (1,)))
                delta = jnp.sum(probs * d_prob, axis=1, keepdims=True)
                d_score = (probs * (d_prob - delta)).astype(BF)
                v_part = dot(probs.astype(BF), d_att, ((0,), (0,)))
                k_part = dot(d_score, query, ((0,), (0,)))

                @pl.when(c == 0)
                def _():
                    d_v[...] = v_part
                    d_k[...] = k_part

                @pl.when(c > 0)
                def _():
                    d_v[...] += v_part
                    d_k[...] += k_part

                d_query = dot(d_score, key, ((1,), (0,))) * SCORE_SCALE
                joint[rows, cols] = turn(d_query, cos[rows], -sine[rows]).astype(BF)

            joint[:, wide + y * HEAD_DIM : wide + (y + 1) * HEAD_DIM] = turn(
                d_k[...] * SCORE_SCALE, cos[...], -sine[...]
            ).astype(BF)
            joint[:, 2 * wide + y * HEAD_DIM : 2 * wide + (y + 1) * HEAD_DIM] = d_v[...].astype(BF)
        width = part.shape[1] // 4

        @pl.loop(0, 4)
        def _(c):
            cols = pl.ds(pl.multiple_of(c * width, width), width)
            part[:, cols] = dot(joint[...], packed[cols, : 3 * wide], ((1,), (1,))).astype(BF)

        @pl.loop(0, 2)
        def _(c):
            cols = pl.ds(pl.multiple_of(c * 2 * width, width), 2 * width)
            for i in range(4):
                if i < 3:
                    value = dot(a1[:, cols], joint[:, i * wide : (i + 1) * wide], ((0,), (0,)))
                else:
                    value = dot(mid[:, cols], attended[...], ((0,), (0,)))
                for y in range(heads):
                    grad[y, i, cols] = value[:, y * HEAD_DIM : (y + 1) * HEAD_DIM].astype(BF)

    def hidden_kernel(a2, cot, w, d_a2, branch, grad, hidden, d_up, d_gate, kept):
        step, steps = pl.program_id(0), pl.num_programs(0)
        tile = w.shape[3]
        here = pl.ds(pl.multiple_of(step * tile, tile), tile)
        length, width = a2.shape
        chunk = length // 2

        @pl.loop(0, 2)
        def _(i):
            rows = pl.ds(pl.multiple_of(i * chunk, chunk), chunk)
            up = dot(a2[rows], w[0, 0], ((1,), (0,)))
            gate = dot(a2[rows], w[0, 1], ((1,), (0,)))
            d_hid = dot(cot[rows], w[0, 2], ((1,), (0,)))
            sigma = jax.nn.sigmoid(gate)
            act = gate * sigma
            hidden[rows, here] = (act * up).astype(BF)
            d_up[rows, here] = (d_hid * act).astype(BF)
            d_gate[rows, here] = (d_hid * up * sigma * (1.0 + gate * (1.0 - sigma))).astype(BF)

        for m in range(3):
            kept[m, :, here] = w[0, m]
        grad[0, 0] = dot(a2[...], d_up[:, here], ((0,), (0,))).astype(BF)
        grad[0, 1] = dot(a2[...], d_gate[:, here], ((0,), (0,))).astype(BF)
        grad[0, 2] = dot(cot[...], hidden[:, here], ((0,), (0,))).astype(BF)

        @pl.when(step == steps - 1)
        def _():
            @pl.loop(0, 8)
            def _(i):
                cols = pl.ds(pl.multiple_of(i * (width // 8), width // 8), width // 8)
                d_a2[:, cols] = (
                    dot(d_up[...], kept[0, cols], ((1,), (1,)))
                    + dot(d_gate[...], kept[1, cols], ((1,), (1,)))
                ).astype(BF)
                branch[:, cols] = dot(hidden[...], kept[2, cols], ((1,), (1,))).astype(BF)

    def shards(
        tokens,
        cotangent,
        lengths,
        deal,
        att_proj,
        attn_out,
        ff_proj,
        ff_out,
        att_proj_first,
        attn_out_first,
        ff_proj_first,
        ff_out_first,
        att_proj_second,
        attn_out_second,
        ff_proj_second,
        ff_out_second,
    ):
        t_at = lax.axis_index("tp")
        pack_at = t_at // 2
        packs, row_count, width = tokens.shape
        half = row_count // 2
        pack_len = deal.shape[1]
        blocks = n_c * 2
        rows_bf = jax.ShapeDtypeStruct((blocks, half, width), BF)
        own_f32 = jax.ShapeDtypeStruct((half, width), F32)
        own_bf = jax.ShapeDtypeStruct((half, width), BF)

        def own_rows(array):
            rows = array.reshape(packs * 2, half, width)
            return lax.dynamic_index_in_dim(rows, t_at, 0, keepdims=False)

        own_tokens = own_rows(tokens)
        own_cot = own_rows(cotangent)
        att_cols, ff_cols = att_proj.shape[2] // n_c, ff_proj.shape[2] // n_c
        att_shape, ff_shape = (4, *att_proj.shape[1:]), (3, *ff_proj.shape[1:])
        att_full = jax.ShapeDtypeStruct((2, 4, width, att_cols), BF)
        ff_full = jax.ShapeDtypeStruct((2, 3, width, ff_cols), BF)
        places = lax.dynamic_index_in_dim(deal, pack_at, 0, keepdims=False)
        length_row = lax.dynamic_index_in_dim(lengths, pack_at, 0, keepdims=False)
        seqs = lengths.shape[1]
        before = jnp.arange(seqs)[:, None] > jnp.arange(seqs)[None, :]
        starts = jnp.sum(jnp.where(before, length_row[None, :], 0), axis=1)
        inside = (places[:, None] >= starts[None, :]) & (
            places[:, None] < (starts + length_row)[None, :]
        )
        firsts = jnp.sum(jnp.where(inside, starts[None, :], 0), axis=1)
        freq_steps = jnp.arange(HEAD_DIM // 2, dtype=F32)
        inverse = jnp.power(10000.0, -2.0 * freq_steps / HEAD_DIM)
        angles = (places - firsts).astype(F32)[:, None] * inverse[None, :]
        cos_table, sine_table = jnp.cos(angles), jnp.sin(angles)
        tables = (
            places[:, None],
            places[None, :],
            firsts[:, None],
            jnp.concatenate([cos_table, cos_table], axis=1),
            jnp.concatenate([-sine_table, sine_table], axis=1),
        )
        rank_width = 2 * att_cols
        act_one, att_w, ff_w, act_two, cot_rows, qkv, attended, mass, resid_mid = call(
            front_kernel,
            "front",
            0,
            (
                rows_bf,
                att_full,
                ff_full,
                rows_bf,
                rows_bf,
                jax.ShapeDtypeStruct((3, pack_len, rank_width), BF),
                jax.ShapeDtypeStruct((pack_len, rank_width), BF),
                jax.ShapeDtypeStruct((pack_len, 2), F32),
                own_f32,
            ),
            [ANY, ANY] + [VMEM] * 5 + [ANY] * 4,
            (ANY,) * 5 + (VMEM,) * 4,
            [
                pltpu.VMEM((half, width), BF),
                pltpu.VMEM((half, width), BF),
                pltpu.VMEM(att_shape, F32),
                pltpu.VMEM(ff_shape, F32),
                pltpu.VMEM(att_shape, BF),
                pltpu.VMEM(ff_shape, BF),
                pltpu.VMEM((half, width), BF),
                pltpu.VMEM((pack_len, width), BF),
                pltpu.VMEM((width, 4 * rank_width), BF),
                dma(6),
                dma(2 * n_c + 8),
            ]
            + scatter_scratch(n_c, half, width)
            + gather_sems(n_c) * 3
            + [dma(n_c), dma(n_c), pltpu.SemaphoreType.DMA] * 2
            + [dma(5 * n_f)] * 4,
            vmem=56,
        )(tokens, cotangent, *tables, att_proj, attn_out, ff_proj, ff_out)
        act_one = act_one.reshape(pack_len, width)
        act_two = act_two.reshape(pack_len, width)
        cot_rows = cot_rows.reshape(pack_len, width)

        tile = 256
        tiles = ff_cols // tile
        kept = pl.BlockSpec((pack_len, width), lambda i: (0, 0), pipeline_mode=pl.Buffered(1))
        moved = pl.BlockSpec((1, 3, width, tile), lambda i: (i // tiles, 0, 0, i % tiles))
        rows_flat = jax.ShapeDtypeStruct((pack_len, width), BF)
        act_two_part, branch_part, ff_grad = pl.pallas_call(
            hidden_kernel,
            grid=(2 * tiles,),
            out_shape=(rows_flat, rows_flat, jax.ShapeDtypeStruct(ff_w.shape, BF)),
            in_specs=[kept, kept, moved],
            out_specs=(kept, kept, moved),
            scratch_shapes=[pltpu.VMEM((pack_len, 2 * ff_cols), BF)] * 3
            + [pltpu.VMEM((3, width, 2 * ff_cols), BF)],
            compiler_params=pltpu.CompilerParams(vmem_limit_bytes=60 << 20),
            name="hidden",
        )(act_two, cot_rows, ff_w)
        height = width // n_f
        mid_rows, block_own, mid_grad, ff_sum = call(
            third_kernel,
            "third",
            2,
            (rows_bf, own_bf, own_f32, jax.ShapeDtypeStruct((3, height, ff_cols), BF)),
            [ANY, ANY, VMEM, VMEM, ANY],
            (ANY, VMEM, VMEM, VMEM),
            scatter_scratch(n_c, half, width) * 2
            + [dma(2), pltpu.VMEM((half, width), BF)]
            + gather_sems(n_c)
            + collect_scratch(n_f, 3, height, ff_cols),
            vmem=56,
        )(
            act_two_part.reshape(rows_bf.shape),
            branch_part.reshape(rows_bf.shape),
            resid_mid,
            own_cot,
            ff_grad,
        )
        mid_rows = mid_rows.reshape(pack_len, width)

        act_one_part, att_grad = local(
            backward_kernel,
            "backward",
            (rows_flat, jax.ShapeDtypeStruct(att_w.shape, BF)),
            [
                pltpu.VMEM((width, 4 * rank_width), BF),
                pltpu.VMEM((pack_len, 3 * rank_width), BF),
                pltpu.VMEM((pack_len, HEAD_DIM), F32),
                pltpu.VMEM((pack_len, HEAD_DIM), F32),
            ],
        )(mid_rows, act_one, att_w, *tables, qkv, attended, mass)
        input_grad, block_out, att_total, ff_total = call(
            fourth_kernel,
            "fourth",
            3,
            (
                jax.ShapeDtypeStruct((n_t, half, width), F32),
                jax.ShapeDtypeStruct((n_t, half, width), BF),
                jax.ShapeDtypeStruct(att_shape, BF),
                jax.ShapeDtypeStruct(ff_shape, BF),
            ),
            [ANY, VMEM, VMEM, ANY, ANY, ANY],
            (ANY,) * 4,
            scatter_scratch(n_c, half, width)
            + [pltpu.VMEM((4, height, att_cols), BF), pltpu.VMEM((half, width), F32)]
            + [dma(n_c), dma(n_c), pltpu.SemaphoreType.DMA] * 2
            + [
                pltpu.SemaphoreType.DMA((2, n_t - 1)),
                pltpu.SemaphoreType.DMA((2, n_t - 1)),
                dma(3),
            ]
            + collect_scratch(n_f, 4, height, att_cols),
        )(
            act_one_part.reshape(rows_bf.shape),
            own_tokens,
            mid_grad,
            block_own,
            att_grad,
            ff_sum,
        )
        weights = (att_proj, attn_out, ff_proj, ff_out)
        firsts_old = (att_proj_first, attn_out_first, ff_proj_first, ff_out_first)
        seconds_old = (att_proj_second, attn_out_second, ff_proj_second, ff_out_second)
        count = n_f + n_c + n_t
        norm_value = call(
            norm_kernel,
            "norm",
            4,
            jax.ShapeDtypeStruct((8, 128), F32),
            [ANY] * 2,
            VMEM,
            [pltpu.VMEM(att_shape, BF), pltpu.VMEM(ff_shape, BF)]
            + [pltpu.VMEM((k, 8, 128), F32) for k in (4, n_t, n_c, n_f)]
            + [dma(count), dma(count), dma(2)],
            vmem=16,
        )(att_total, ff_total)
        results = pl.pallas_call(
            finish_kernel,
            out_shape=(
                *(jax.ShapeDtypeStruct(w.shape, F32) for w in weights * 4),
                *(jax.ShapeDtypeStruct(w.shape, BF) for w in weights),
                jax.ShapeDtypeStruct(block_out.shape, BF),
                jax.ShapeDtypeStruct(input_grad.shape, F32),
            ),
            in_specs=[VMEM] + [ANY] * 16,
            out_specs=(ANY,) * 22,
            scratch_shapes=[
                pltpu.VMEM(att_shape, BF),
                pltpu.VMEM(ff_shape, BF),
                pltpu.VMEM(att_shape, F32),
                pltpu.VMEM(ff_shape, F32),
                pltpu.VMEM((3, *att_shape), F32),
                pltpu.VMEM((3, *ff_shape), F32),
                pltpu.VMEM(block_out.shape, BF),
                pltpu.VMEM(input_grad.shape, F32),
                pltpu.SemaphoreType.DMA((17, 2, 5)),
            ],
            compiler_params=pltpu.CompilerParams(vmem_limit_bytes=56 << 20),
            name="finish",
        )(norm_value, block_out, input_grad, att_total, ff_total, *weights, *firsts_old, *seconds_old)
        return (
            results[20].reshape(tokens.shape),
            results[21].reshape(tokens.shape),
            norm_value[0, :1],
            *results[:20],
        )

    return shards


def solution(mesh):
    act = P("fsdp", "ctx", None)
    table = P("fsdp", None)
    cube = P(None, ("fsdp", "ctx"), "tp")
    flat = P(("fsdp", "ctx"), "tp")
    group = (cube, flat, cube, flat)
    in_specs = (act, act, table, table) + group * 3
    out_specs = (act, act, P()) + group * 5
    return jax.shard_map(
        make_shards(mesh), mesh=mesh, in_specs=in_specs, out_specs=out_specs, check_vma=False
    )
```

```python
import functools

import jax
import jax.numpy as jnp
from jax import lax
from jax.experimental import pallas as pl
from jax.experimental.pallas import tpu as pltpu
from jax.sharding import PartitionSpec as P

HEAD_DIM = 128
STEP = 10
EPS_NORM = 1e-05
BETA_ONE = 0.9
BETA_TWO = 0.95
EPS_ADAM = 1e-08
DECAY = 0.1
MAX_NORM = 1.0
NEG_FILL = -1e30
BF = jnp.bfloat16
F32 = jnp.float32
MESH = pl.DeviceIdType.MESH
ANY = pl.BlockSpec(memory_space=pl.ANY)
VMEM = pl.BlockSpec(memory_space=pltpu.VMEM)
ROWS = 16
QUERIES = 256
SCORE_SCALE = HEAD_DIM ** (-0.5)


def mean_spread(values):
    centre = values - jnp.mean(values, axis=-1, keepdims=True)
    spread = jnp.mean(centre * centre, axis=-1, keepdims=True)
    scale = lax.rsqrt(spread + EPS_NORM)
    return centre * scale, scale


def norm_back(grad, normed, scale):
    return scale * (
        grad
        - jnp.mean(grad, axis=-1, keepdims=True)
        - normed * jnp.mean(grad * normed, axis=-1, keepdims=True)
    )


def dot(left, right, dims):
    return lax.dot_general(left, right, (dims, ((), ())), preferred_element_type=F32)


def adam_step(weight, grad_sum, first, second, clip_factor, learn_rate):
    clipped = grad_sum * clip_factor
    first_new = BETA_ONE * first + (1.0 - BETA_ONE) * clipped
    second_new = BETA_TWO * second + (1.0 - BETA_TWO) * clipped * clipped
    first_hat = first_new / (1.0 - BETA_ONE**STEP)
    second_hat = second_new / (1.0 - BETA_TWO**STEP)
    weight_new = weight - learn_rate * (
        first_hat / (jnp.sqrt(second_hat) + EPS_ADAM) + DECAY * weight
    )
    return (first_new, second_new, weight_new)


class Place:
    def __init__(self, sizes):
        self.n_f, self.n_c, self.n_t = sizes
        self.f, self.c, self.t = (lax.axis_index(a) for a in ("fsdp", "ctx", "tp"))
        self.hi, self.lo = self.t // 2, lax.rem(self.t, 2)
        self.core = (self.f, self.c, self.t + 1 - 2 * self.lo)
        self.block = self.c * 2 + self.lo
        self.pairs = [(s, o) for o in range(2) for s in range(self.n_f) if s or o]

    def ctx(self, shift):
        return lax.rem(self.c + shift + self.n_c, self.n_c)

    def fsdp(self, shift):
        return lax.rem(self.f + shift + self.n_f, self.n_f)

    def other(self, o):
        return self.hi + o * (1 - 2 * self.hi)

    def z(self, shift):
        return (self.f, self.ctx(shift), self.t)

    def xy(self, shift, o):
        return (self.fsdp(shift), self.c, self.t + o * (2 - 4 * self.hi))

    def greet(self, peers):
        barrier = pltpu.get_barrier_semaphore()
        for peer in peers:
            pl.semaphore_signal(barrier, inc=1, device_id=peer, device_id_type=MESH)
        pl.semaphore_wait(barrier, len(peers))

    def all_z(self):
        return [self.z(s) for s in range(1, self.n_c)]

    def all_xy(self):
        return [self.xy(s, o) for s, o in self.pairs]


def remote(src, dst, send, recv, peer):
    return pltpu.make_async_remote_copy(
        src_ref=src, dst_ref=dst, send_sem=send, recv_sem=recv, device_id=peer, device_id_type=MESH
    )


def by_rows(count, step):
    @pl.loop(0, count // ROWS)
    def _(i):
        step(pl.ds(pl.multiple_of(i * ROWS, ROWS), ROWS))


class Gather:
    def __init__(self, at, src, out, send, recv, local):
        self.at, self.src, self.out, self.send, self.recv = at, src, out, send, recv
        self.local = pltpu.make_async_copy(src, out.at[at.block], local)

    def far(self, way, hop, src=None):
        at = self.at
        block = self.out.at[jnp.clip(at.c - way * (hop - 1), 0, at.n_c - 1) * 2 + at.lo]
        k = hop + (0 if way > 0 else at.n_c)
        return remote(
            block if src is None else src, block, self.send.at[k], self.recv.at[k], at.z(way)
        )

    def near(self, distance, src=None):
        at = self.at
        block = self.out.at[jnp.clip(at.c - distance, 0, at.n_c - 1) * 2 + at.lo]
        k = 2 * at.n_c + distance + at.n_c
        return remote(
            block if src is None else src, block, self.send.at[k], self.recv.at[k], at.core
        )

    def there(self, way, hop):
        return self.at.c + hop < self.at.n_c if way > 0 else self.at.c >= hop

    def start(self):
        for way in (1, -1):

            @pl.when(self.there(way, 1))
            def _(way=way):
                self.far(way, 1, self.src).start()

        self.near(0, self.src).start()
        self.local.start()

    def forward(self, hops=None):
        at = self.at
        for hop in hops or range(1, at.n_c):
            for way in (1, -1):

                @pl.when(self.there(-way, hop))
                def _(way=way, hop=hop):
                    self.far(way, hop).wait_recv()
                    if hop < at.n_c - 1:

                        @pl.when(self.there(way, 1))
                        def _():
                            self.far(way, hop + 1).start()

                    self.near(way * hop).start()

    def finish(self):
        at = self.at
        for hop in range(1, at.n_c):
            for way in (1, -1):

                @pl.when(self.there(way, 1) & self.there(-way, hop - 1))
                def _(way=way, hop=hop):
                    self.far(way, hop).wait_send()

                @pl.when(self.there(-way, hop))
                def _(way=way, hop=hop):
                    self.near(way * hop).wait()

        self.near(0, self.src).wait()
        self.local.wait()


def gather_sems(n_c):
    return [
        pltpu.SemaphoreType.DMA((4 * n_c,)),
        pltpu.SemaphoreType.DMA((4 * n_c,)),
        pltpu.SemaphoreType.DMA,
    ]


class Scatter:
    def __init__(self, at, part, near, sent, got, send, recv):
        self.at, self.part, self.near = at, part, near
        self.sent, self.got, self.send, self.recv = sent, got, send, recv

    def core(self, c):
        at = self.at
        return remote(
            self.part.at[c * 2 + 1 - at.lo], self.near.at[c], self.send.at[c], self.recv.at[c], at.core
        )

    def far(self, way, hop, slot):
        at = self.at
        k = at.n_c + hop + (0 if way > 0 else at.n_c)
        sent = self.sent.at[jnp.clip(at.c + way * hop, 0, at.n_c - 1)]
        return remote(sent, self.got.at[slot], self.send.at[k], self.recv.at[k], at.z(way))

    def end(self, way):
        return self.at.n_c + (0 if way > 0 else 1)

    there = Gather.there

    def start(self):
        at = self.at
        for i in range(at.n_c):
            self.core(jnp.where(at.c * 2 < at.n_c, at.n_c - 1 - i, i)).start()

    def pass_on(self, hops=None):
        at = self.at
        for hop in hops or range(at.n_c - 1, 0, -1):
            for way in (1, -1):

                @pl.when(self.there(way, hop))
                def _(way=way, hop=hop):
                    c = at.c + way * hop
                    self.core(c).wait_recv()
                    if hop < at.n_c - 1:
                        more = self.there(-way, 1)

                        @pl.when(more)
                        def _():
                            self.far(way, hop + 1, c).wait_recv()
                            self.add(c, True)

                        @pl.when(jnp.logical_not(more))
                        def _():
                            self.add(c, False)

                    else:
                        self.add(c, False)
                    self.far(way, hop, self.end(way) if hop == 1 else c).start()

    def add(self, c, more):
        at = self.at

        def rows_of(rows):
            value = self.part[c * 2 + at.lo, rows].astype(F32) + self.near[c, rows].astype(F32)
            if more:
                value = value + self.got[c, rows].astype(F32)
            self.sent[c, rows] = value.astype(BF)

        by_rows(self.near.shape[1], rows_of)

    def arrive(self):
        self.core(self.at.c).wait_recv()
        for way in (1, -1):

            @pl.when(self.there(-way, 1))
            def _(way=way):
                self.far(way, 1, self.end(way)).wait_recv()

            @pl.when(jnp.logical_not(self.there(-way, 1)))
            def _(way=way):
                self.got[self.end(way)] = jnp.zeros(self.got.shape[1:], BF)

    def total(self, rows):
        c, at = self.at.c, self.at
        return (
            self.part[c * 2 + at.lo, rows].astype(F32)
            + self.near[c, rows].astype(F32)
            + self.got[self.end(1), rows].astype(F32)
            + self.got[self.end(-1), rows].astype(F32)
        )

    def free(self, credit):
        at = self.at

        def tell(k, peer):
            pl.semaphore_signal(credit.at[k], inc=1, device_id=peer, device_id_type=MESH)

        tell(0, at.core)
        for k, way in ((1, 1), (2, -1)):

            @pl.when(self.there(way, 1))
            def _(k=k, way=way):
                tell(k, at.z(way))

        pl.semaphore_wait(credit.at[0], 1)
        for k, way in ((1, 1), (2, -1)):

            @pl.when(self.there(-way, 1))
            def _(k=k):
                pl.semaphore_wait(credit.at[k], 1)

    def finish(self):
        at = self.at
        for c in range(at.n_c):
            self.core(c).wait_send()
        for hop in range(1, at.n_c):
            for way in (1, -1):

                @pl.when(self.there(way, hop))
                def _(way=way, hop=hop):
                    self.far(way, hop, 0).wait_send()


def scatter_scratch(n_c, half, width):
    return [
        pltpu.VMEM((2 * n_c, half, width), BF),
        pltpu.VMEM((n_c, half, width), BF),
        pltpu.VMEM((n_c, half, width), BF),
        pltpu.VMEM((n_c + 2, half, width), BF),
        pltpu.SemaphoreType.DMA((3 * n_c,)),
        pltpu.SemaphoreType.DMA((3 * n_c,)),
    ]


class Swap:
    def __init__(self, at, shard, full, send, recv, local):
        self.at = at
        rows, width = shard.shape[1], full.shape[3]
        here = pl.ds((at.f * at.n_c + at.c) * rows, rows)
        target = full.at[at.hi, :, here, :]

        def columns(c):
            return shard.at[:, :, pl.ds(pl.multiple_of(c * width, 128), width)]

        self.local = pltpu.make_async_copy(columns(at.c), target, local)
        self.far = [
            remote(columns(at.ctx(s)), target, send.at[s], recv.at[s], at.z(s))
            for s in range(1, at.n_c)
        ]

    def start(self):
        self.local.start()
        for copy in self.far:
            copy.start()

    def wait(self):
        self.local.wait()
        for copy in self.far:
            copy.wait()


class Spread:
    def __init__(self, at, full, send, recv):
        self.at, self.full, self.send, self.recv = at, full, send, recv
        self.height = full.shape[2] // at.n_f // 2

    def part(self, o, shift, half):
        at = self.at
        first = (at.fsdp(shift) * 2 + half) * self.height
        return self.full.at[at.other(o), :, pl.ds(first, self.height), :]

    def copy(self, part, k, peer):
        return remote(part, part, self.send.at[k], self.recv.at[k], peer)

    def copies(self):
        at = self.at
        n = at.n_f
        return [
            *(
                self.copy(self.part(0, 0, h), h * n + s, at.xy(s, 0))
                for h in range(2)
                for s in range(1, n)
            ),
            *(self.copy(self.part(0, 0, h), 2 * n + h, at.xy(0, 1)) for h in (1, 0)),
        ]

    def passes(self):
        at = self.at
        n = at.n_f
        return [
            *(self.copy(self.part(0, -s, 0), 3 * n + s, at.xy(0, 1)) for s in range(1, n)),
            *(self.copy(self.part(1, 0, 1), 4 * n + s, at.xy(s, 0)) for s in range(1, n)),
        ]

    def start(self):
        for copy in self.copies():
            copy.start()

    def forward(self):
        copies, n = self.copies(), self.at.n_f
        for copy in copies[: n - 1]:
            copy.wait_recv()
        copies[2 * n - 2].wait_recv()
        for copy in self.passes():
            copy.start()

    def wait(self):
        copies, n = self.copies(), self.at.n_f
        for copy in copies[n - 1 : 2 * n - 2]:
            copy.wait_recv()
        copies[2 * n - 1].wait_recv()
        for copy in copies:
            copy.wait_send()
        for copy in self.passes():
            copy.wait()


class Collect:
    def __init__(self, at, partial, stage, local, by_x, by_y, pass_x, pass_y, send, recv):
        self.at, self.partial, self.stage, self.local = at, partial, stage, local
        self.by_x, self.by_y, self.pass_x, self.pass_y = by_x, by_y, pass_x, pass_y
        self.send, self.recv = send, recv
        self.matrices = by_y.shape[0]
        self.height = partial.shape[2] // at.n_f // 2

    def first(self, shift, half):
        return (self.at.fsdp(shift) * 2 + half) * self.height

    def part(self, o, shift, half, m):
        rows = pl.ds(self.first(shift, half), self.height)
        return self.partial.at[self.at.other(o), m, rows, :]

    def half(self, ref, half, m):
        return ref.at[m, pl.ds(half * self.height, self.height), :]

    def copy(self, src, dst, k, m, peer):
        k = k * self.matrices + m
        return remote(src, dst, self.send.at[k], self.recv.at[k], peer)

    def raw(self, group, m):
        at = self.at
        n, shifts = at.n_f, range(1, at.n_f)
        if group == 0:
            return [
                self.copy(self.part(1, s, 0, m), self.pass_x.at[s - 1, m], s, m, at.xy(s, 0)) for s in shifts
            ]
        if group == 1:
            return [
                self.copy(self.part(1, s, 1, m), self.pass_y.at[s - 1, m], n + s, m, at.xy(0, 1))
                for s in shifts
            ]
        return [
            *(
                self.copy(
                    self.part(0, s, 0, m), self.half(self.by_x.at[s - 1], 0, m), 2 * n + s, m, at.xy(s, 0)
                )
                for s in shifts
            ),
            self.copy(self.part(1, 0, 1, m), self.half(self.by_y, 1, m), 0, m, at.xy(0, 1)),
        ]

    def added(self, s, m):
        at = self.at
        if s == 0:
            return self.copy(self.pass_x.at[0, m], self.half(self.by_y, 0, m), at.n_f, m, at.xy(0, 1))
        target = self.half(self.by_x.at[s - 1], 1, m)
        return self.copy(self.pass_y.at[s - 1, m], target, 3 * at.n_f + s, m, at.xy(s, 0))

    def start(self, m):
        for group in range(3):
            for copy in self.raw(group, m):
                copy.start()

    def reader(self, o, shift, half):
        at = self.at
        if self.stage is None:
            first = self.first(shift, half)
            return lambda m, rows, start: self.partial[
                at.other(o), m, pl.ds(pl.multiple_of(first + start, ROWS), ROWS)
            ]
        loads = [
            pltpu.make_async_copy(
                self.part(o, shift, half, m), self.stage(m), self.local.at[m]
            )
            for m in range(self.matrices)
        ]
        for copy in loads:
            copy.start()
        for copy in loads:
            copy.wait()
        return lambda m, rows, start: self.stage(m)[rows]

    def sweep(self, step, m):
        @pl.loop(0, self.height // ROWS)
        def _(i):
            start = pl.multiple_of(i * ROWS, ROWS)
            step(m, pl.ds(start, ROWS), start)

    def forward(self):
        n = self.at.n_f
        own = self.reader(1, 0, 0)

        def add_y(m, rows, start):
            value = own(m, rows, start).astype(F32)
            for s in range(n - 1):
                value = value + self.pass_x[s, m, rows].astype(F32)
            self.pass_x[0, m, rows] = value.astype(BF)

        for m in range(self.matrices):
            for copy in self.raw(0, m):
                copy.wait_recv()
            self.sweep(add_y, m)
            self.added(0, m).start()
        for s in range(1, n):
            own_x = self.reader(0, s, 1)

            def add_x(m, rows, start, s=s, own_x=own_x):
                value = own_x(m, rows, start).astype(F32) + self.pass_y[s - 1, m, rows].astype(F32)
                self.pass_y[s - 1, m, rows] = value.astype(BF)

            for m in range(self.matrices):
                self.raw(1, m)[s - 1].wait_recv()
                self.sweep(add_x, m)
                self.added(s, m).start()

    def finish_sums(self, stage):
        self.stage = stage
        self.total()

    def total(self):
        n = self.at.n_f
        for half in range(2):
            own = self.reader(0, 0, half)

            def add(m, rows, start, half=half, own=own):
                here = pl.ds(pl.multiple_of(half * self.height + start, ROWS), ROWS)
                value = own(m, rows, start).astype(F32) + self.by_y[m, here].astype(F32)
                for s in range(n - 1):
                    value = value + self.by_x[s, m, here].astype(F32)
                self.by_y[m, here] = value.astype(BF)

            for m in range(self.matrices):
                if half == 0:
                    for copy in self.raw(2, m):
                        copy.wait_recv()
                    for s in range(n):
                        self.added(s, m).wait_recv()
                self.sweep(add, m)

    def finish(self):
        for m in range(self.matrices):
            for group in range(3):
                for copy in self.raw(group, m):
                    copy.wait_send()
            for s in range(self.at.n_f):
                self.added(s, m).wait_send()


class Share:
    def __init__(self, at, src, out, send, recv, local):
        self.at, self.local = at, pltpu.make_async_copy(src, out.at[at.t], local)
        across = at.t + 2 - 4 * at.hi
        self.first = [
            remote(src, out.at[at.t], send.at[0], recv.at[0], at.xy(0, 1)),
            remote(src, out.at[at.t], send.at[1], recv.at[1], at.core),
        ]
        self.second = remote(out.at[across], out.at[across], send.at[2], recv.at[2], at.core)

    def start(self):
        for copy in (*self.first, self.local):
            copy.start()

    def forward(self):
        self.first[0].wait_recv()
        self.second.start()

    def finish(self):
        self.first[0].wait_send()
        self.first[1].wait()
        self.second.wait()
        self.local.wait()


def collect_scratch(n_f, matrices, height, columns):
    half = (matrices, height // 2, columns)
    return [
        pltpu.VMEM((n_f - 1, matrices, height, columns), BF),
        pltpu.VMEM((matrices, height, columns), BF),
        pltpu.VMEM((n_f - 1, *half), BF),
        pltpu.VMEM((n_f - 1, *half), BF),
        dma(4 * n_f * matrices),
        dma(4 * n_f * matrices),
    ]


class Return:
    def __init__(self, at, summed, shard, send, recv, local):
        rows, sheets = shard.shape[1], summed.shape[0]
        beside = shard.shape[0] // sheets
        width = summed.shape[2] // beside
        self.local, self.far = [], []
        for m in range(shard.shape[0]):
            target = shard.at[m, :, pl.ds(pl.multiple_of(at.c * width, 128), width)]
            first = m % beside * width

            def part(c, m=m, first=first):
                here = pl.ds(pl.multiple_of(c * rows, rows), rows)
                return summed.at[m // beside, here, first : first + width]

            self.local.append(pltpu.make_async_copy(part(at.c), target, local.at[m]))
            for s in range(1, at.n_c):
                k = m * at.n_c + s
                self.far.append(remote(part(at.ctx(s)), target, send.at[k], recv.at[k], at.z(s)))

    def start(self):
        for copy in (*self.far, *self.local):
            copy.start()

    def wait(self):
        for copy in (*self.far, *self.local):
            copy.wait()


def pack_weights(w, packed):
    heads = w.shape[0]
    for i in range(4):
        for y in range(heads):
            k = (i * heads + y) * HEAD_DIM
            packed[:, k : k + HEAD_DIM] = w[y, i]


def turn(values, cos, sine):
    return values * cos + pltpu.roll(values, HEAD_DIM // 2, 1) * sine


def recast(wide, low):
    for m in range(wide.shape[0]):

        def step(rows, m=m):
            low[m, rows] = wide[m, rows].astype(low.dtype)

        by_rows(wide.shape[1], step)


def dma(count):
    return pltpu.SemaphoreType.DMA((count,))


def make_shards(mesh):
    sizes = tuple(mesh.shape[a] for a in ("fsdp", "ctx", "tp"))
    n_f, n_c, n_t = sizes

    def call(kernel, name, collective, outs, ins, out_specs, scratch, aliases=None, vmem=40):
        return pl.pallas_call(
            kernel,
            out_shape=outs,
            in_specs=ins,
            out_specs=out_specs,
            scratch_shapes=scratch,
            input_output_aliases=aliases or {},
            compiler_params=pltpu.CompilerParams(
                collective_id=collective, has_side_effects=True, vmem_limit_bytes=vmem << 20
            ),
            name=name,
        )

    def local(kernel, name, outs, scratch):
        return pl.pallas_call(
            kernel,
            out_shape=outs,
            scratch_shapes=scratch,
            compiler_params=pltpu.CompilerParams(vmem_limit_bytes=60 << 20),
            name=name,
        )

    def front_kernel(
        tok_ref, cot_ref, place, key_place, first, cos, sine, att_ref, out_ref, ffp_ref, ffo_ref,
        rows_ref, attw_ref, ffw_ref, a2_ref, cots_ref, qkv, attended, mass, mid_ref,
        x_ref, own_cot, att_wide, ff_wide, att_low, ff_low, low, a1, packed, lk, lp,
        part, near, sent, got, ss, sr, g1, h1, l1, g2, h2, l2, g3, h3, l3, s4, r4, l4, s5, r5, l5, s6, r6, s7, r7,
    ):
        at = Place(sizes)
        half = x_ref.shape[0]
        mine = pl.ds(pl.multiple_of(at.lo * half, half), half)
        loads = [
            pltpu.make_async_copy(tok_ref.at[at.hi, mine], x_ref, lk.at[0]),
            pltpu.make_async_copy(att_ref, att_wide.at[pl.ds(0, 3)], lk.at[1]),
            pltpu.make_async_copy(out_ref, att_wide.at[3], lk.at[2]),
            pltpu.make_async_copy(ffp_ref, ff_wide.at[pl.ds(0, 2)], lk.at[3]),
            pltpu.make_async_copy(ffo_ref, ff_wide.at[2], lk.at[4]),
            pltpu.make_async_copy(cot_ref.at[at.hi, mine], own_cot, lk.at[5]),
        ]
        for copy in loads:
            copy.start()
        scatter = Scatter(at, part, near, sent, got, ss, sr)
        gather = Gather(at, low, rows_ref, g1, h1, l1)
        cots = Gather(at, own_cot, cots_ref, g2, h2, l2)
        a2 = Gather(at, low, a2_ref, g3, h3, l3)
        swap_att = Swap(at, att_low, attw_ref, s4, r4, l4)
        swap_ff = Swap(at, ff_low, ffw_ref, s5, r5, l5)
        spread_att = Spread(at, attw_ref, s6, r6)
        spread_ff = Spread(at, ffw_ref, s7, r7)
        loads[0].wait()

        def norm_one(rows):
            low[rows] = mean_spread(x_ref[rows].astype(F32))[0].astype(BF)

        by_rows(half, norm_one)
        loads[1].wait()
        loads[2].wait()
        recast(att_wide, att_low)
        at.greet([at.core, *at.all_z(), *at.all_xy()])
        gather.start()
        swap_att.start()
        for copy in loads[3:]:
            copy.wait()
        recast(ff_wide, ff_low)
        gather.forward(range(1, 2))
        swap_att.wait()
        spread_att.start()
        gather.forward(range(2, n_c - 1))
        swap_ff.start()
        gather.forward(range(n_c - 1, n_c))
        spread_att.forward()
        gather.finish()
        take = [pltpu.make_async_copy(rows_ref.at[b], a1.at[pl.ds(b * half, half)], lp.at[b]) for b in range(2 * n_c)]
        for copy in take:
            copy.start()
        spread_att.wait()
        heads = attw_ref.shape[0]
        packs = [
            pltpu.make_async_copy(
                attw_ref.at[y, i],
                packed.at[:, pl.ds((i * heads + y) * HEAD_DIM, HEAD_DIM)],
                lp.at[2 * n_c + i * heads + y],
            )
            for i in range(4)
            for y in range(heads)
        ]
        for copy in packs:
            copy.start()
        for copy in (*take, *packs):
            copy.wait()
        attend(a1, packed, place, key_place, first, cos, sine, qkv, attended, mass, part)
        scatter.start()
        scatter.pass_on(range(n_c - 1, 1, -1))
        swap_ff.wait()
        spread_ff.start()
        scatter.pass_on(range(1, 2))
        cots.start()
        scatter.arrive()

        def norm_two(rows):
            mid = x_ref[rows].astype(F32) + scatter.total(rows)
            mid_ref[rows] = mid
            low[rows] = mean_spread(mid)[0].astype(BF)

        by_rows(half, norm_two)
        a2.start()
        cots.forward(range(1, 2))
        a2.forward(range(1, 2))
        spread_ff.forward()
        for hop in range(2, n_c):
            a2.forward(range(hop, hop + 1))
            cots.forward(range(hop, hop + 1))
        cots.finish()
        a2.finish()
        scatter.finish()
        spread_ff.wait()

    def back_kernel(
        a2_ref, cots_ref, joined_ref, d_a2_ref, branch_ref, mid_ref, tok_ref, cot_ref, a1_ref, attw_ref,
        place, key_place, first, cos, sine, qkv, attended, mass,
        input_ref, out_ref, attg_ref, ffg_ref, norm_ref, grad_ref, rows_ref,
        rows_one, rows_two, wide, sheets, d_v, d_k, own, block, low, x_ref, own_cot, lk, lg, credit,
        part, near, sent, got, ss, sr, g1, h1, l1, lf, s4, r4, l4, s5, r5, l5, s6, r6, l6,
        total, got_t, got_c, got_f, s7, r7, *collected,
    ):
        at = Place(sizes)
        half = own.shape[0]
        length, tall = rows_one.shape[0], wide.shape[1]
        mine = pl.ds(pl.multiple_of(at.lo * half, half), half)

        def load(*pairs):
            copies = [pltpu.make_async_copy(src, dst, lk.at[i]) for i, (src, dst) in enumerate(pairs)]
            for copy in copies:
                copy.start()
            for copy in copies:
                copy.wait()

        def in_blocks(src, dst):
            return [(src.at[b], dst.at[pl.ds(b * half, half)]) for b in range(2 * n_c)]

        scatter = Scatter(at, part, near, sent, got, ss, sr)
        gather = Gather(at, low, rows_ref, g1, h1, l1)
        columns = sheets.shape[3]
        high = tall // n_f // 2
        collect_ff = Collect(
            at, grad_ref, lambda m: sheets.at[0, 0, pl.ds(m * high, high)], lf, *collected[:6]
        )
        collect_att = Collect(at, sheets, None, None, *collected[6:])
        give_ff = Return(at, collected[1], ffg_ref, s5, r5, l5)
        give_att = Return(at, collected[7], attg_ref, s4, r4, l4)
        tps = [(at.f, at.c, lax.rem(at.t + s, n_t)) for s in range(1, n_t)]
        fs = [at.xy(s, 0) for s in range(1, n_f)]
        load((d_a2_ref, part))
        at.greet([*tps, *at.all_z(), *fs])
        scatter.start()
        load(
            (a2_ref, rows_one),
            (cots_ref, rows_two),
            (joined_ref.at[0], wide.at[0, pl.ds(0, length)]),
            (joined_ref.at[1], wide.at[0, pl.ds(length, length)]),
            (joined_ref.at[2], wide.at[1, pl.ds(0, length)]),
            (tok_ref.at[at.hi, mine], x_ref),
            (cot_ref.at[at.hi, mine], own_cot),
        )

        def keep(k):
            y, m = k % 2, k // 2
            return pltpu.make_async_copy(sheets.at[y, 0], grad_ref.at[y, m], lg.at[y])

        for k in range(6):
            y, m = k % 2, k // 2
            if k >= 2 and y == 0:
                keep(k - 2).wait()
                keep(k - 1).wait()
            rows = rows_two if m == 2 else rows_one
            slot, start = ((0, 0), (0, length), (1, 0))[m]

            @pl.loop(0, 2)
            def _(i, y=y, rows=rows, slot=slot, start=start):
                cols = pl.ds(pl.multiple_of(i * (tall // 2), tall // 2), tall // 2)
                side = wide[slot, start : start + length, y * columns : (y + 1) * columns]
                sheets[y, 0, cols] = dot(rows[:, cols], side, ((0,), (0,))).astype(BF)

            keep(k).start()
            if y == 0 and m > 0:
                collect_ff.start(m - 1)
            if k in (0, 3, 5):
                hop = {0: n_c - 1, 3: n_c - 2, 5: n_c - 3}[k]
                scatter.pass_on(range(hop, hop + 1))
        keep(4).wait()
        keep(5).wait()
        collect_ff.start(2)
        scatter.arrive()

        def norm_two(rows):
            normed, scale = mean_spread(mid_ref[rows])
            grad = own_cot[rows].astype(F32) + norm_back(scatter.total(rows), normed, scale)
            own[rows] = grad
            low[rows] = grad.astype(BF)

        by_rows(half, norm_two)
        gather.start()
        scatter.finish()
        scatter.free(credit.at[0])
        load((branch_ref, part))
        gather.forward(range(1, n_c - 1))
        scatter.start()
        collect_ff.forward()
        gather.forward(range(n_c - 1, n_c))
        heads = attw_ref.shape[0]
        load(
            *in_blocks(a1_ref, rows_two),
            *(
                (attw_ref.at[y, i], wide.at[0, :, pl.ds((i * heads + y) * HEAD_DIM, HEAD_DIM)])
                for i in range(4)
                for y in range(heads)
            ),
        )
        scatter.pass_on(range(n_c - 1, n_c - 2, -1))
        gather.finish()
        load(*in_blocks(rows_ref, rows_one))
        packed, joint = wide.at[0], wide.at[1, pl.ds(length, length)]
        wide_heads = heads * HEAD_DIM
        joint[:, :wide_heads] = dot(rows_one[...], packed[:, 3 * wide_heads :], ((1,), (0,))).astype(BF)
        for y in range(heads):
            attend_back(y, packed, joint, place, key_place, first, cos, sine, qkv, mass, d_v, d_k, heads)
            if y == 0:
                scatter.pass_on(range(n_c - 2, 1, -1))
        scatter.pass_on(range(1, 2))
        scatter.arrive()

        def add(rows):
            block[rows] = (mid_ref[rows] + scatter.total(rows)).astype(BF)

        by_rows(half, add)
        scatter.finish()
        scatter.free(credit.at[1])
        width = part.shape[2] // 4

        @pl.loop(0, 4)
        def _(c):
            cols = pl.ds(pl.multiple_of(c * width, width), width)
            value = dot(joint[:, : 3 * wide_heads], packed[cols, : 3 * wide_heads], ((1,), (1,))).astype(BF)
            part[:, :, cols] = value.reshape(part.shape[0], part.shape[1], width)

        scatter.start()

        @pl.loop(0, 2)
        def _(c):
            cols = pl.ds(pl.multiple_of(c * 2 * width, width), 2 * width)
            for i in range(4):
                if i < 3:
                    value = dot(
                        rows_two[:, cols], joint[:, i * wide_heads : (i + 1) * wide_heads], ((0,), (0,))
                    )
                else:
                    value = dot(rows_one[:, cols], attended[...], ((0,), (0,)))
                for y in range(heads):
                    sheets[y, 0, cols, i * HEAD_DIM : (i + 1) * HEAD_DIM] = value[
                        :, y * HEAD_DIM : (y + 1) * HEAD_DIM
                    ].astype(BF)

        collect_att.start(0)
        scatter.pass_on(range(n_c - 1, n_c - 2, -1))
        share_block = Share(at, block, out_ref, s6.at[0], r6.at[0], l6.at[0])
        share_input = Share(at, low, input_ref, s6.at[1], r6.at[1], l6.at[1])
        share_block.start()
        collect_ff.finish_sums(lambda m: rows_one.at[pl.ds(0, high), pl.ds(m * columns, columns)])
        give_ff.start()
        collect_att.forward()
        scatter.pass_on(range(n_c - 2, 0, -1))
        share_block.forward()
        collect_att.total()
        give_att.start()
        scatter.arrive()

        def norm_one(rows):
            normed, scale = mean_spread(x_ref[rows].astype(F32))
            low[rows] = (own[rows] + norm_back(scatter.total(rows), normed, scale)).astype(BF)

        by_rows(half, norm_one)
        share_input.start()
        scatter.finish()
        collect_ff.finish()
        collect_att.finish()
        share_input.forward()
        give_ff.wait()
        give_att.wait()
        own_rows, own_cols = ffg_ref.shape[1], attg_ref.shape[2]
        ff_low = [rows_one.at[pl.ds(m * own_rows, own_rows)] for m in range(3)]
        att_low = [
            rows_two.at[pl.ds(0, own_rows), pl.ds(m * own_cols, own_cols)] for m in range(4)
        ]
        load(
            *((ffg_ref.at[m], ff_low[m]) for m in range(3)),
            *((attg_ref.at[m], att_low[m]) for m in range(4)),
        )
        sum_norm(at, (*ff_low, *att_low), norm_ref, total, got_t, got_c, got_f, s7, r7)
        share_block.finish()
        share_input.finish()

    def sum_norm(at, grads, norm_ref, total, got_t, got_c, got_f, send, recv):
        tps = [(at.f, at.c, lax.rem(at.t + s, n_t)) for s in range(1, n_t)]
        fs = [at.xy(s, 0) for s in range(1, n_f)]
        total[0] = jnp.zeros(total.shape[1:], F32)
        for low in grads:

            def square(rows, low=low):
                value = low[rows].astype(F32)
                value = value * value
                value = value[: ROWS // 2] + value[ROWS // 2 :]
                lanes = value[:, :128]
                for c in range(1, value.shape[1] // 128):
                    lanes = lanes + value[:, c * 128 : (c + 1) * 128]
                total[0] += lanes

            by_rows(low.shape[0], square)
        base = 0
        stages = ((tps, got_t, at.t), (at.all_z(), got_c, at.c), (fs, got_f, at.f))
        for stage, (peers, got, place) in enumerate(stages):
            copies = [
                remote(total.at[stage], got.at[place], send.at[base + i], recv.at[base + i], peer)
                for i, peer in enumerate(peers)
            ]
            base += len(peers)
            for copy in copies:
                copy.start()
            got[place] = total[stage]
            for copy in copies:
                copy.wait()
            value = got[0]
            for i in range(1, got.shape[0]):
                value = value + got[i]
            total[stage + 1] = value
        norm = jnp.sqrt(jnp.sum(total[3], axis=(0, 1), keepdims=True))
        norm_ref[...] = jnp.broadcast_to(norm, norm_ref.shape)

    def finish_kernel(norm_ref, block_in, input_in, attg_ref, ffg_ref, *refs):
        olds, outs, scratch = refs[:12], refs[12:34], refs[34:]
        low_att, low_ff, wide_att, wide_ff, old_att, old_ff, block_keep, input_low, input_keep, ls = scratch
        groups = (
            (attg_ref, low_att, wide_att, old_att, 0, attg_ref.shape[1]),
            (ffg_ref, low_ff, wide_ff, old_ff, 2, attg_ref.shape[1] // 4),
        )
        chunks = [
            (group, m, r)
            for group in groups
            for m in range(group[0].shape[0])
            for r in range(group[0].shape[1] // group[5])
        ]

        def sheet(array, first, m, group):
            last = group[0].shape[0] - 1
            return array[first + 1] if m == last else array[first].at[m]

        loads, stores = [], []
        for i, (group, m, r) in enumerate(chunks):
            here = pl.ds(r * group[5], group[5])
            one = [pltpu.make_async_copy(group[0].at[m, here], group[1].at[m, here], ls.at[i, 0, 3])]
            one += [
                pltpu.make_async_copy(
                    sheet(olds, 4 * j + group[4], m, group).at[here], group[3].at[j, m, here], ls.at[i, 0, j]
                )
                for j in range(3)
            ]
            for copy in one:
                copy.start()
            loads.append(one)
        kept = ((block_in, block_keep, block_keep, outs[20]), (input_in, input_low, input_keep, outs[21]))
        through = []
        for i, (src, first, keep, out) in enumerate(kept):
            copy = pltpu.make_async_copy(src, first, ls.at[len(chunks), 0, i])
            copy.start()
            through.append((copy, pltpu.make_async_copy(keep, out, ls.at[len(chunks), 1, i])))
        norm = norm_ref[0:1, 0:1]
        clip = jnp.minimum(1.0, MAX_NORM / (norm + 1e-06))
        width = ffg_ref.shape[1] * n_f * n_c
        for i, (group, m, r) in enumerate(chunks):
            for copy in loads[i]:
                copy.wait()
            low, wide, old = group[1:4]
            rate = (width // 32) ** (-0.5) if group[4] == 0 and m == 3 else width ** (-0.5)

            @pl.loop(0, group[5] // ROWS)
            def _(k, low=low, wide=wide, old=old, m=m, r=r, step=group[5], rate=rate):
                rows = pl.ds(pl.multiple_of(r * step + k * ROWS, ROWS), ROWS)
                grad = low[m, rows].astype(F32)
                wide[m, rows] = grad
                first_new, second_new, weight_new = adam_step(
                    old[0, m, rows], grad, old[1, m, rows], old[2, m, rows], clip, rate
                )
                old[0, m, rows] = weight_new
                old[1, m, rows] = first_new
                old[2, m, rows] = second_new
                low[m, rows] = weight_new.astype(BF)

            here = pl.ds(r * group[5], group[5])
            for k, (src, out) in enumerate(
                ((wide, 0), (old.at[1], 4), (old.at[2], 8), (old.at[0], 12), (low, 16))
            ):
                store = pltpu.make_async_copy(
                    src.at[m, here], sheet(outs, out + group[4], m, group).at[here], ls.at[i, 1, k]
                )
                store.start()
                stores.append(store)
        for load, store in through:
            load.wait()
            if load is through[1][0]:
                recast(input_low, input_keep)
            store.start()
            stores.append(store)
        for store in stores:
            store.wait()

    def attend(a1, packed, place, key_place, first, cos, sine, qkv, attended, mass, part):
        wide = attended.shape[1]
        heads = wide // HEAD_DIM
        for i in range(3):
            joint = dot(a1[...], packed[:, i * wide : (i + 1) * wide], ((1,), (0,)))
            for y in range(heads):
                cols = slice(y * HEAD_DIM, (y + 1) * HEAD_DIM)
                head = joint[:, cols]
                if i < 2:
                    head = turn(head, cos[...], sine[...])
                qkv[i, :, cols] = head.astype(BF)
        for y in range(heads):
            cols = slice(y * HEAD_DIM, (y + 1) * HEAD_DIM)

            @pl.loop(0, a1.shape[0] // QUERIES)
            def _(c, y=y, cols=cols):
                rows = pl.ds(pl.multiple_of(c * QUERIES, QUERIES), QUERIES)
                scores = dot(qkv[0, rows, cols], qkv[1, :, cols], ((1,), (1,))) * SCORE_SCALE
                allowed = (key_place[...] <= place[rows]) & (key_place[...] >= first[rows])
                scores = jnp.where(allowed, scores, NEG_FILL)
                peak = jnp.max(scores, axis=1, keepdims=True)
                exp_scores = jnp.exp(scores - peak)
                total = jnp.sum(exp_scores, axis=1, keepdims=True)
                probs = (exp_scores * (1.0 / total)).astype(BF)
                attended[rows, cols] = dot(probs, qkv[2, :, cols], ((1,), (0,))).astype(BF)
                mass[rows, y : y + 1] = peak + jnp.log(total)

        width = part.shape[2] // 4

        @pl.loop(0, 4)
        def _(c):
            cols = pl.ds(pl.multiple_of(c * width, width), width)
            value = dot(attended[...], packed[cols, 3 * wide :], ((1,), (1,))).astype(BF)
            part[:, :, cols] = value.reshape(part.shape[0], part.shape[1], width)

    def attend_back(y, packed, joint, place, key_place, first, cos, sine, qkv, mass, d_v, d_k, heads):
        wide = heads * HEAD_DIM
        cols = slice(y * HEAD_DIM, (y + 1) * HEAD_DIM)

        @pl.loop(0, qkv.shape[1] // QUERIES)
        def _(c):
            rows = pl.ds(pl.multiple_of(c * QUERIES, QUERIES), QUERIES)
            query, key, value = qkv[0, rows, cols], qkv[1, :, cols], qkv[2, :, cols]
            d_att = joint[rows, cols]
            scores = dot(query, key, ((1,), (1,))) * SCORE_SCALE
            allowed = (key_place[...] <= place[rows]) & (key_place[...] >= first[rows])
            probs = jnp.exp(jnp.where(allowed, scores, NEG_FILL) - mass[rows, y : y + 1])
            d_prob = dot(d_att, value, ((1,), (1,)))
            delta = jnp.sum(probs * d_prob, axis=1, keepdims=True)
            d_score = (probs * (d_prob - delta)).astype(BF)
            v_part = dot(probs.astype(BF), d_att, ((0,), (0,)))
            k_part = dot(d_score, query, ((0,), (0,)))

            @pl.when(c == 0)
            def _():
                d_v[...] = v_part
                d_k[...] = k_part

            @pl.when(c > 0)
            def _():
                d_v[...] += v_part
                d_k[...] += k_part

            d_query = dot(d_score, key, ((1,), (0,))) * SCORE_SCALE
            joint[rows, cols] = turn(d_query, cos[rows], -sine[rows]).astype(BF)

        joint[:, wide + y * HEAD_DIM : wide + (y + 1) * HEAD_DIM] = turn(
            d_k[...] * SCORE_SCALE, cos[...], -sine[...]
        ).astype(BF)
        joint[:, 2 * wide + y * HEAD_DIM : 2 * wide + (y + 1) * HEAD_DIM] = d_v[...].astype(BF)

    def hidden_kernel(a2, cot, w, d_a2, branch, joined, kept):
        d_up, d_gate, hidden = joined.at[0], joined.at[1], joined.at[2]
        step, steps = pl.program_id(0), pl.num_programs(0)
        tile = w.shape[3]
        here = pl.ds(pl.multiple_of(step * tile, tile), tile)
        length, width = a2.shape
        chunk = length // 2

        @pl.loop(0, 2)
        def _(i):
            rows = pl.ds(pl.multiple_of(i * chunk, chunk), chunk)
            up = dot(a2[rows], w[0, 0], ((1,), (0,)))
            gate = dot(a2[rows], w[0, 1], ((1,), (0,)))
            d_hid = dot(cot[rows], w[0, 2], ((1,), (0,)))
            sigma = jax.nn.sigmoid(gate)
            act = gate * sigma
            hidden[rows, here] = (act * up).astype(BF)
            d_up[rows, here] = (d_hid * act).astype(BF)
            d_gate[rows, here] = (d_hid * up * sigma * (1.0 + gate * (1.0 - sigma))).astype(BF)

        for m in range(3):
            kept[m, :, here] = w[0, m]

        @pl.when(step == steps - 1)
        def _():
            @pl.loop(0, 8)
            def _(i):
                cols = pl.ds(pl.multiple_of(i * (width // 8), width // 8), width // 8)
                d_a2[:, cols] = (
                    dot(d_up[...], kept[0, cols], ((1,), (1,)))
                    + dot(d_gate[...], kept[1, cols], ((1,), (1,)))
                ).astype(BF)
                branch[:, cols] = dot(hidden[...], kept[2, cols], ((1,), (1,))).astype(BF)

    def shards(
        tokens,
        cotangent,
        lengths,
        deal,
        att_proj,
        attn_out,
        ff_proj,
        ff_out,
        att_proj_first,
        attn_out_first,
        ff_proj_first,
        ff_out_first,
        att_proj_second,
        attn_out_second,
        ff_proj_second,
        ff_out_second,
    ):
        t_at = lax.axis_index("tp")
        pack_at = t_at // 2
        packs, row_count, width = tokens.shape
        half = row_count // 2
        pack_len = deal.shape[1]
        blocks = n_c * 2
        rows_bf = jax.ShapeDtypeStruct((blocks, half, width), BF)
        own_f32 = jax.ShapeDtypeStruct((half, width), F32)

        att_cols, ff_cols = att_proj.shape[2] // n_c, ff_proj.shape[2] // n_c
        att_shape, ff_shape = (4, *att_proj.shape[1:]), (3, *ff_proj.shape[1:])
        att_full = jax.ShapeDtypeStruct((2, 4, width, att_cols), BF)
        ff_full = jax.ShapeDtypeStruct((2, 3, width, ff_cols), BF)
        places = lax.dynamic_index_in_dim(deal, pack_at, 0, keepdims=False)
        length_row = lax.dynamic_index_in_dim(lengths, pack_at, 0, keepdims=False)
        seqs = lengths.shape[1]
        before = jnp.arange(seqs)[:, None] > jnp.arange(seqs)[None, :]
        starts = jnp.sum(jnp.where(before, length_row[None, :], 0), axis=1)
        inside = (places[:, None] >= starts[None, :]) & (
            places[:, None] < (starts + length_row)[None, :]
        )
        firsts = jnp.sum(jnp.where(inside, starts[None, :], 0), axis=1)
        freq_steps = jnp.arange(HEAD_DIM // 2, dtype=F32)
        inverse = jnp.power(10000.0, -2.0 * freq_steps / HEAD_DIM)
        angles = (places - firsts).astype(F32)[:, None] * inverse[None, :]
        cos_table, sine_table = jnp.cos(angles), jnp.sin(angles)
        tables = (
            places[:, None],
            places[None, :],
            firsts[:, None],
            jnp.concatenate([cos_table, cos_table], axis=1),
            jnp.concatenate([-sine_table, sine_table], axis=1),
        )
        rank_width = 2 * att_cols
        act_one, att_w, ff_w, act_two, cot_rows, qkv, attended, mass, resid_mid = call(
            front_kernel,
            "front",
            0,
            (
                rows_bf,
                att_full,
                ff_full,
                rows_bf,
                rows_bf,
                jax.ShapeDtypeStruct((3, pack_len, rank_width), BF),
                jax.ShapeDtypeStruct((pack_len, rank_width), BF),
                jax.ShapeDtypeStruct((pack_len, 2), F32),
                own_f32,
            ),
            [ANY, ANY] + [VMEM] * 5 + [ANY] * 4,
            (ANY,) * 5 + (VMEM,) * 4,
            [
                pltpu.VMEM((half, width), BF),
                pltpu.VMEM((half, width), BF),
                pltpu.VMEM(att_shape, F32),
                pltpu.VMEM(ff_shape, F32),
                pltpu.VMEM(att_shape, BF),
                pltpu.VMEM(ff_shape, BF),
                pltpu.VMEM((half, width), BF),
                pltpu.VMEM((pack_len, width), BF),
                pltpu.VMEM((width, 4 * rank_width), BF),
                dma(6),
                dma(2 * n_c + 8),
            ]
            + scatter_scratch(n_c, half, width)
            + gather_sems(n_c) * 3
            + [dma(n_c), dma(n_c), pltpu.SemaphoreType.DMA] * 2
            + [dma(5 * n_f)] * 4,
            vmem=56,
        )(tokens, cotangent, *tables, att_proj, attn_out, ff_proj, ff_out)
        act_two = act_two.reshape(pack_len, width)
        cot_rows = cot_rows.reshape(pack_len, width)

        tile = 256
        tiles = ff_cols // tile
        kept = pl.BlockSpec((pack_len, width), lambda i: (0, 0), pipeline_mode=pl.Buffered(1))
        moved = pl.BlockSpec((1, 3, width, tile), lambda i: (i // tiles, 0, 0, i % tiles))
        rows_flat = jax.ShapeDtypeStruct((pack_len, width), BF)
        act_two_part, branch_part, joined = pl.pallas_call(
            hidden_kernel,
            grid=(2 * tiles,),
            out_shape=(rows_flat, rows_flat, jax.ShapeDtypeStruct((3, pack_len, 2 * ff_cols), BF)),
            in_specs=[kept, kept, moved],
            out_specs=(
                kept,
                kept,
                pl.BlockSpec((3, pack_len, 2 * ff_cols), lambda i: (0, 0, 0), pipeline_mode=pl.Buffered(1)),
            ),
            scratch_shapes=[pltpu.VMEM((3, width, 2 * ff_cols), BF)],
            compiler_params=pltpu.CompilerParams(vmem_limit_bytes=60 << 20),
            name="hidden",
        )(act_two, cot_rows, ff_w)
        height = width // n_f
        count = n_f + n_c + n_t
        input_grad, block_out, att_total, ff_total, norm_value, *_ = call(
            back_kernel,
            "back",
            1,
            (
                jax.ShapeDtypeStruct((n_t, half, width), BF),
                jax.ShapeDtypeStruct((n_t, half, width), BF),
                jax.ShapeDtypeStruct(att_shape, BF),
                jax.ShapeDtypeStruct(ff_shape, BF),
                jax.ShapeDtypeStruct((8, 128), F32),
                ff_full,
                rows_bf,
            ),
            [ANY] * 5 + [VMEM] + [ANY] * 4 + [VMEM] * 8,
            (ANY,) * 4 + (VMEM,) + (ANY,) * 2,
            [
                pltpu.VMEM((pack_len, width), BF),
                pltpu.VMEM((pack_len, width), BF),
                pltpu.VMEM((2, width, 4 * rank_width), BF),
                pltpu.VMEM((2, 1, width, 4 * att_cols), BF),
                pltpu.VMEM((pack_len, HEAD_DIM), F32),
                pltpu.VMEM((pack_len, HEAD_DIM), F32),
                pltpu.VMEM((half, width), F32),
                pltpu.VMEM((half, width), BF),
                pltpu.VMEM((half, width), BF),
                pltpu.VMEM((half, width), BF),
                pltpu.VMEM((half, width), BF),
                dma(2 * n_c + 8),
                dma(2),
                pltpu.SemaphoreType.REGULAR((2, 3)),
            ]
            + scatter_scratch(n_c, half, width)
            + gather_sems(n_c)
            + [dma(3)]
            + [dma(4 * n_c), dma(4 * n_c), dma(4), dma(3 * n_c), dma(3 * n_c), dma(3)]
            + [
                pltpu.SemaphoreType.DMA((2, 3)),
                pltpu.SemaphoreType.DMA((2, 3)),
                dma(2),
            ]
            + [pltpu.VMEM((k, 8, 128), F32) for k in (4, n_t, n_c, n_f)]
            + [dma(count), dma(count)]
            + collect_scratch(n_f, 3, height, ff_cols)
            + collect_scratch(n_f, 1, height, 4 * att_cols),
            vmem=62,
        )(
            act_two, cot_rows, joined, act_two_part.reshape(rows_bf.shape), branch_part.reshape(rows_bf.shape),
            resid_mid, tokens, cotangent, act_one, att_w, *tables, qkv, attended, mass,
        )
        weights = (att_proj, attn_out, ff_proj, ff_out)
        firsts_old = (att_proj_first, attn_out_first, ff_proj_first, ff_out_first)
        seconds_old = (att_proj_second, attn_out_second, ff_proj_second, ff_out_second)
        results = pl.pallas_call(
            finish_kernel,
            out_shape=(
                *(jax.ShapeDtypeStruct(w.shape, F32) for w in weights * 4),
                *(jax.ShapeDtypeStruct(w.shape, BF) for w in weights),
                jax.ShapeDtypeStruct(block_out.shape, BF),
                jax.ShapeDtypeStruct(input_grad.shape, F32),
            ),
            in_specs=[VMEM] + [ANY] * 16,
            out_specs=(ANY,) * 22,
            scratch_shapes=[
                pltpu.VMEM(att_shape, BF),
                pltpu.VMEM(ff_shape, BF),
                pltpu.VMEM(att_shape, F32),
                pltpu.VMEM(ff_shape, F32),
                pltpu.VMEM((3, *att_shape), F32),
                pltpu.VMEM((3, *ff_shape), F32),
                pltpu.VMEM(block_out.shape, BF),
                pltpu.VMEM(input_grad.shape, BF),
                pltpu.VMEM(input_grad.shape, F32),
                pltpu.SemaphoreType.DMA((17, 2, 5)),
            ],
            compiler_params=pltpu.CompilerParams(vmem_limit_bytes=56 << 20),
            name="finish",
        )(norm_value, block_out, input_grad, att_total, ff_total, *weights, *firsts_old, *seconds_old)
        return (
            results[20].reshape(tokens.shape),
            results[21].reshape(tokens.shape),
            norm_value[0, :1],
            *results[:20],
        )

    return shards


def solution(mesh):
    act = P("fsdp", "ctx", None)
    table = P("fsdp", None)
    cube = P(None, ("fsdp", "ctx"), "tp")
    flat = P(("fsdp", "ctx"), "tp")
    group = (cube, flat, cube, flat)
    in_specs = (act, act, table, table) + group * 3
    out_specs = (act, act, P()) + group * 5
    return jax.shard_map(
        make_shards(mesh), mesh=mesh, in_specs=in_specs, out_specs=out_specs, check_vma=False
    )
```

```python
import functools

import jax
import jax.numpy as jnp
from jax import lax
from jax.experimental import pallas as pl
from jax.experimental.pallas import tpu as pltpu
from jax.sharding import PartitionSpec as P

HEAD_DIM = 128
STEP = 10
EPS_NORM = 1e-05
BETA_ONE = 0.9
BETA_TWO = 0.95
EPS_ADAM = 1e-08
DECAY = 0.1
MAX_NORM = 1.0
NEG_FILL = -1e30
BF = jnp.bfloat16
F32 = jnp.float32
MESH = pl.DeviceIdType.MESH
ANY = pl.BlockSpec(memory_space=pl.ANY)
VMEM = pl.BlockSpec(memory_space=pltpu.VMEM)
ROWS = 16
STEP_ROWS = 32
QUERIES = 256
SCORE_SCALE = HEAD_DIM ** (-0.5)


def mean_spread(values):
    centre = values - jnp.mean(values, axis=-1, keepdims=True)
    spread = jnp.mean(centre * centre, axis=-1, keepdims=True)
    scale = lax.rsqrt(spread + EPS_NORM)
    return centre * scale, scale


def norm_back(grad, normed, scale):
    return scale * (
        grad
        - jnp.mean(grad, axis=-1, keepdims=True)
        - normed * jnp.mean(grad * normed, axis=-1, keepdims=True)
    )


def dot(left, right, dims):
    return lax.dot_general(left, right, (dims, ((), ())), preferred_element_type=F32)


def adam_step(weight, grad_sum, first, second, clip_factor, learn_rate):
    clipped = grad_sum * clip_factor
    first_new = BETA_ONE * first + (1.0 - BETA_ONE) * clipped
    second_new = BETA_TWO * second + (1.0 - BETA_TWO) * clipped * clipped
    first_hat = first_new / (1.0 - BETA_ONE**STEP)
    second_hat = second_new / (1.0 - BETA_TWO**STEP)
    weight_new = weight - learn_rate * (
        first_hat / (jnp.sqrt(second_hat) + EPS_ADAM) + DECAY * weight
    )
    return (first_new, second_new, weight_new)


class Place:
    def __init__(self, sizes):
        self.n_f, self.n_c, self.n_t = sizes
        self.f, self.c, self.t = (lax.axis_index(a) for a in ("fsdp", "ctx", "tp"))
        self.hi, self.lo = self.t // 2, lax.rem(self.t, 2)
        self.core = (self.f, self.c, self.t + 1 - 2 * self.lo)
        self.block = self.c * 2 + self.lo
        self.pairs = [(s, o) for o in range(2) for s in range(self.n_f) if s or o]

    def ctx(self, shift):
        return lax.rem(self.c + shift + self.n_c, self.n_c)

    def fsdp(self, shift):
        return lax.rem(self.f + shift + self.n_f, self.n_f)

    def other(self, o):
        return self.hi + o * (1 - 2 * self.hi)

    def z(self, shift):
        return (self.f, self.ctx(shift), self.t)

    def xy(self, shift, o):
        return (self.fsdp(shift), self.c, self.t + o * (2 - 4 * self.hi))

    def greet(self, peers):
        barrier = pltpu.get_barrier_semaphore()
        for peer in peers:
            pl.semaphore_signal(barrier, inc=1, device_id=peer, device_id_type=MESH)
        pl.semaphore_wait(barrier, len(peers))

    def all_z(self):
        return [self.z(s) for s in range(1, self.n_c)]

    def all_xy(self):
        return [self.xy(s, o) for s, o in self.pairs]


def remote(src, dst, send, recv, peer):
    return pltpu.make_async_remote_copy(
        src_ref=src, dst_ref=dst, send_sem=send, recv_sem=recv, device_id=peer, device_id_type=MESH
    )


def by_rows(count, step):
    @pl.loop(0, count // ROWS)
    def _(i):
        step(pl.ds(pl.multiple_of(i * ROWS, ROWS), ROWS))


class Gather:
    def __init__(self, at, src, out, send, recv, local):
        self.at, self.src, self.out, self.send, self.recv = at, src, out, send, recv
        self.local = pltpu.make_async_copy(src, out.at[at.block], local)

    def far(self, way, hop, src=None):
        at = self.at
        block = self.out.at[jnp.clip(at.c - way * (hop - 1), 0, at.n_c - 1) * 2 + at.lo]
        k = hop + (0 if way > 0 else at.n_c)
        return remote(
            block if src is None else src, block, self.send.at[k], self.recv.at[k], at.z(way)
        )

    def near(self, distance, src=None):
        at = self.at
        block = self.out.at[jnp.clip(at.c - distance, 0, at.n_c - 1) * 2 + at.lo]
        k = 2 * at.n_c + distance + at.n_c
        return remote(
            block if src is None else src, block, self.send.at[k], self.recv.at[k], at.core
        )

    def there(self, way, hop):
        return self.at.c + hop < self.at.n_c if way > 0 else self.at.c >= hop

    def start(self):
        for way in (1, -1):

            @pl.when(self.there(way, 1))
            def _(way=way):
                self.far(way, 1, self.src).start()

        self.near(0, self.src).start()
        self.local.start()

    def forward(self, hops=None):
        at = self.at
        for hop in hops or range(1, at.n_c):
            for way in (1, -1):

                @pl.when(self.there(-way, hop))
                def _(way=way, hop=hop):
                    self.far(way, hop).wait_recv()
                    if hop < at.n_c - 1:

                        @pl.when(self.there(way, 1))
                        def _():
                            self.far(way, hop + 1).start()

                    self.near(way * hop).start()

    def finish(self):
        at = self.at
        for hop in range(1, at.n_c):
            for way in (1, -1):

                @pl.when(self.there(way, 1) & self.there(-way, hop - 1))
                def _(way=way, hop=hop):
                    self.far(way, hop).wait_send()

                @pl.when(self.there(-way, hop))
                def _(way=way, hop=hop):
                    self.near(way * hop).wait()

        self.near(0, self.src).wait()
        self.local.wait()


def gather_sems(n_c):
    return [
        pltpu.SemaphoreType.DMA((4 * n_c,)),
        pltpu.SemaphoreType.DMA((4 * n_c,)),
        pltpu.SemaphoreType.DMA,
    ]


class Scatter:
    def __init__(self, at, part, near, sent, got, send, recv):
        self.at, self.part, self.near = at, part, near
        self.sent, self.got, self.send, self.recv = sent, got, send, recv

    def core(self, c):
        at = self.at
        return remote(
            self.part.at[c * 2 + 1 - at.lo], self.near.at[c], self.send.at[c], self.recv.at[c], at.core
        )

    def far(self, way, hop, slot):
        at = self.at
        k = at.n_c + hop + (0 if way > 0 else at.n_c)
        sent = self.sent.at[jnp.clip(at.c + way * hop, 0, at.n_c - 1)]
        return remote(sent, self.got.at[slot], self.send.at[k], self.recv.at[k], at.z(way))

    def end(self, way):
        return self.at.n_c + (0 if way > 0 else 1)

    there = Gather.there

    def start(self):
        at = self.at
        for i in range(at.n_c):
            self.core(jnp.where(at.c * 2 < at.n_c, at.n_c - 1 - i, i)).start()

    def pass_on(self, hops=None):
        at = self.at
        for hop in hops or range(at.n_c - 1, 0, -1):
            for way in (1, -1):

                @pl.when(self.there(way, hop))
                def _(way=way, hop=hop):
                    c = at.c + way * hop
                    self.core(c).wait_recv()
                    if hop < at.n_c - 1:
                        more = self.there(-way, 1)

                        @pl.when(more)
                        def _():
                            self.far(way, hop + 1, c).wait_recv()
                            self.add(c, True)

                        @pl.when(jnp.logical_not(more))
                        def _():
                            self.add(c, False)

                    else:
                        self.add(c, False)
                    self.far(way, hop, self.end(way) if hop == 1 else c).start()

    def add(self, c, more):
        at = self.at

        def rows_of(rows):
            value = self.part[c * 2 + at.lo, rows].astype(F32) + self.near[c, rows].astype(F32)
            if more:
                value = value + self.got[c, rows].astype(F32)
            self.sent[c, rows] = value.astype(BF)

        by_rows(self.near.shape[1], rows_of)

    def arrive(self):
        self.core(self.at.c).wait_recv()
        for way in (1, -1):

            @pl.when(self.there(-way, 1))
            def _(way=way):
                self.far(way, 1, self.end(way)).wait_recv()

            @pl.when(jnp.logical_not(self.there(-way, 1)))
            def _(way=way):
                self.got[self.end(way)] = jnp.zeros(self.got.shape[1:], BF)

    def total(self, rows):
        c, at = self.at.c, self.at
        return (
            self.part[c * 2 + at.lo, rows].astype(F32)
            + self.near[c, rows].astype(F32)
            + self.got[self.end(1), rows].astype(F32)
            + self.got[self.end(-1), rows].astype(F32)
        )

    def free(self, credit):
        at = self.at

        def tell(k, peer):
            pl.semaphore_signal(credit.at[k], inc=1, device_id=peer, device_id_type=MESH)

        tell(0, at.core)
        for k, way in ((1, 1), (2, -1)):

            @pl.when(self.there(way, 1))
            def _(k=k, way=way):
                tell(k, at.z(way))

        pl.semaphore_wait(credit.at[0], 1)
        for k, way in ((1, 1), (2, -1)):

            @pl.when(self.there(-way, 1))
            def _(k=k):
                pl.semaphore_wait(credit.at[k], 1)

    def finish(self):
        at = self.at
        for c in range(at.n_c):
            self.core(c).wait_send()
        for hop in range(1, at.n_c):
            for way in (1, -1):

                @pl.when(self.there(way, hop))
                def _(way=way, hop=hop):
                    self.far(way, hop, 0).wait_send()


def scatter_scratch(n_c, half, width):
    return [
        pltpu.VMEM((2 * n_c, half, width), BF),
        pltpu.VMEM((n_c, half, width), BF),
        pltpu.VMEM((n_c, half, width), BF),
        pltpu.VMEM((n_c + 2, half, width), BF),
        pltpu.SemaphoreType.DMA((3 * n_c,)),
        pltpu.SemaphoreType.DMA((3 * n_c,)),
    ]


class Swap:
    def __init__(self, at, shard, full, send, recv, local):
        self.at = at
        rows, width = shard.shape[1], full.shape[3]
        here = pl.ds((at.f * at.n_c + at.c) * rows, rows)
        target = full.at[at.hi, :, here, :]

        def columns(c):
            return shard.at[:, :, pl.ds(pl.multiple_of(c * width, 128), width)]

        self.local = pltpu.make_async_copy(columns(at.c), target, local)
        self.far = [
            remote(columns(at.ctx(s)), target, send.at[s], recv.at[s], at.z(s))
            for s in range(1, at.n_c)
        ]

    def start(self):
        self.local.start()
        for copy in self.far:
            copy.start()

    def arrived(self, s):
        if s == 0:
            self.local.wait()
        else:
            self.far[s - 1].wait_recv()
        return self.at.ctx(-s)

    def finish(self):
        for copy in self.far:
            copy.wait_send()


class Spread:
    def __init__(self, at, full, send, recv):
        self.at, self.full, self.send, self.recv = at, full, send, recv
        self.height = full.shape[2] // at.n_f // at.n_c

    def part(self, o, shift, piece):
        at = self.at
        first = (at.fsdp(shift) * at.n_c + piece) * self.height
        return self.full.at[at.other(o), :, pl.ds(first, self.height), :]

    def copy(self, part, k, piece, peer):
        k = k * self.at.n_c + piece
        return remote(part, part, self.send.at[k], self.recv.at[k], peer)

    def own(self, piece):
        at = self.at
        return [
            *(self.copy(self.part(0, 0, piece), s, piece, at.xy(s, 0)) for s in range(1, at.n_f)),
            self.copy(self.part(0, 0, piece), 0, piece, at.xy(0, 1)),
        ]

    def passes(self, piece):
        at = self.at
        n = at.n_f
        if piece < at.n_c // 2:
            return [self.copy(self.part(0, -s, piece), n + s, piece, at.xy(0, 1)) for s in range(1, n)]
        return [self.copy(self.part(1, 0, piece), n + s, piece, at.xy(s, 0)) for s in range(1, n)]

    def start(self, piece):
        for copy in self.own(piece):
            copy.start()

    def forward(self, piece):
        own = self.own(piece)
        for copy in own[:-1] if piece < self.at.n_c // 2 else own[-1:]:
            copy.wait_recv()
        for copy in self.passes(piece):
            copy.start()

    def wait(self):
        for piece in range(self.at.n_c):
            own = self.own(piece)
            for copy in own[-1:] if piece < self.at.n_c // 2 else own[:-1]:
                copy.wait_recv()
            for copy in own:
                copy.wait_send()
            for copy in self.passes(piece):
                copy.wait()


class Collect:
    def __init__(self, at, partial, local, by_x, by_y, pass_x, pass_y, send, recv):
        self.at, self.partial, self.local = at, partial, local
        self.by_x, self.by_y, self.pass_x, self.pass_y = by_x, by_y, pass_x, pass_y
        self.send, self.recv = send, recv
        self.matrices = by_y.shape[0]
        self.height = partial.shape[2] // at.n_f // 2

    def first(self, shift, half):
        return (self.at.fsdp(shift) * 2 + half) * self.height

    def part(self, o, shift, half, m):
        rows = pl.ds(self.first(shift, half), self.height)
        return self.partial.at[self.at.other(o), m, rows, :]

    def half(self, ref, half, m):
        return ref.at[m, pl.ds(half * self.height, self.height), :]

    def copy(self, src, dst, k, m, peer):
        k = k * self.matrices + m
        return remote(src, dst, self.send.at[k], self.recv.at[k], peer)

    def raw(self, group, m):
        at = self.at
        n, shifts = at.n_f, range(1, at.n_f)
        if group == 0:
            return [
                self.copy(self.part(1, s, 0, m), self.pass_x.at[s - 1, m], s, m, at.xy(s, 0)) for s in shifts
            ]
        if group == 1:
            return [
                self.copy(self.part(1, s, 1, m), self.pass_y.at[s - 1, m], n + s, m, at.xy(0, 1))
                for s in shifts
            ]
        return [
            *(
                self.copy(
                    self.part(0, s, 0, m), self.half(self.by_x.at[s - 1], 0, m), 2 * n + s, m, at.xy(s, 0)
                )
                for s in shifts
            ),
            self.copy(self.part(1, 0, 1, m), self.half(self.by_y, 1, m), 0, m, at.xy(0, 1)),
        ]

    def added(self, s, m):
        at = self.at
        if s == 0:
            return self.copy(self.pass_x.at[0, m], self.half(self.by_y, 0, m), at.n_f, m, at.xy(0, 1))
        target = self.half(self.by_x.at[s - 1], 1, m)
        return self.copy(self.pass_y.at[s - 1, m], target, 3 * at.n_f + s, m, at.xy(s, 0))

    def start(self, m):
        for group in range(3):
            for copy in self.raw(group, m):
                copy.start()

    def load(self, o, shift, half, m, stage, k):
        return pltpu.make_async_copy(self.part(o, shift, half, m), stage, self.local.at[k])

    def fetch(self, m, stages):
        self.load(1, 0, 0, m, stages[0], 0).start()
        self.load(0, 1, 1, m, stages[1], 1).start()

    def fetch_own(self, m, stages):
        for half in range(2):
            self.load(0, 0, half, m, stages[half], 2 + 2 * m + half).start()

    def reader(self, o, shift, half, m, stage):
        if stage is None:
            first = self.first(shift, half)
            return lambda rows, start: self.partial[
                self.at.other(o), m, pl.ds(pl.multiple_of(first + start, STEP_ROWS), STEP_ROWS)
            ]
        return lambda rows, start: stage[rows]

    def sweep(self, step):
        @pl.loop(0, self.height // STEP_ROWS)
        def _(i):
            start = pl.multiple_of(i * STEP_ROWS, STEP_ROWS)
            step(pl.ds(start, STEP_ROWS), start)

    def forward(self, m, stages=(None, None)):
        n = self.at.n_f
        for copy in self.raw(0, m):
            copy.wait_recv()
        if stages[0] is not None:
            self.load(1, 0, 0, m, stages[0], 0).wait()
        own = self.reader(1, 0, 0, m, stages[0])

        def add_y(rows, start):
            value = own(rows, start).astype(F32)
            for s in range(n - 1):
                value = value + self.pass_x[s, m, rows].astype(F32)
            self.pass_x[0, m, rows] = value.astype(BF)

        self.sweep(add_y)
        self.added(0, m).start()
        for s in range(1, n):
            if stages[1] is not None:
                load = self.load(0, s, 1, m, stages[1], 1)
                if s > 1:
                    load.start()
                load.wait()
            own_x = self.reader(0, s, 1, m, stages[1])
            self.raw(1, m)[s - 1].wait_recv()

            def add_x(rows, start, s=s, own_x=own_x):
                value = own_x(rows, start).astype(F32) + self.pass_y[s - 1, m, rows].astype(F32)
                self.pass_y[s - 1, m, rows] = value.astype(BF)

            self.sweep(add_x)
            self.added(s, m).start()

    def total(self, m, stages=(None, None)):
        n = self.at.n_f
        for copy in self.raw(2, m):
            copy.wait_recv()
        for s in range(n):
            self.added(s, m).wait_recv()
        for half in range(2):
            if stages[half] is not None:
                self.load(0, 0, half, m, stages[half], 2 + 2 * m + half).wait()
            own = self.reader(0, 0, half, m, stages[half])

            def add(rows, start, half=half, own=own):
                here = pl.ds(pl.multiple_of(half * self.height + start, STEP_ROWS), STEP_ROWS)
                value = own(rows, start).astype(F32) + self.by_y[m, here].astype(F32)
                for s in range(n - 1):
                    value = value + self.by_x[s, m, here].astype(F32)
                self.by_y[m, here] = value.astype(BF)

            self.sweep(add)

    def finish(self):
        for m in range(self.matrices):
            for group in range(3):
                for copy in self.raw(group, m):
                    copy.wait_send()
            for s in range(self.at.n_f):
                self.added(s, m).wait_send()


class Share:
    def __init__(self, at, src, out, send, recv, local):
        self.at, self.local = at, pltpu.make_async_copy(src, out.at[at.t], local)
        across = at.t + 2 - 4 * at.hi
        self.first = [
            remote(src, out.at[at.t], send.at[0], recv.at[0], at.xy(0, 1)),
            remote(src, out.at[at.t], send.at[1], recv.at[1], at.core),
        ]
        self.second = remote(out.at[across], out.at[across], send.at[2], recv.at[2], at.core)

    def start(self):
        for copy in (*self.first, self.local):
            copy.start()

    def forward(self):
        self.first[0].wait_recv()
        self.second.start()

    def finish(self):
        self.first[0].wait_send()
        self.first[1].wait()
        self.second.wait()
        self.local.wait()


def collect_scratch(n_f, matrices, height, columns):
    half = (matrices, height // 2, columns)
    return [
        pltpu.VMEM((n_f - 1, matrices, height, columns), BF),
        pltpu.VMEM((matrices, height, columns), BF),
        pltpu.VMEM((n_f - 1, *half), BF),
        pltpu.VMEM((n_f - 1, *half), BF),
        dma(4 * n_f * matrices),
        dma(4 * n_f * matrices),
    ]


class Return:
    def __init__(self, at, summed, shard, send, recv, local):
        rows, sheets = shard.shape[1], summed.shape[0]
        beside = shard.shape[0] // sheets
        width = summed.shape[2] // beside
        self.copies = []
        for m in range(shard.shape[0]):
            target = shard.at[m, :, pl.ds(pl.multiple_of(at.c * width, 128), width)]
            first = m % beside * width

            def part(c, m=m, first=first):
                here = pl.ds(pl.multiple_of(c * rows, rows), rows)
                return summed.at[m // beside, here, first : first + width]

            copies = []
            for s in range(1, at.n_c):
                k = m * at.n_c + s
                copies.append(remote(part(at.ctx(s)), target, send.at[k], recv.at[k], at.z(s)))
            copies.append(pltpu.make_async_copy(part(at.c), target, local.at[m]))
            self.copies.append(copies)

    def start(self, m):
        for copy in self.copies[m]:
            copy.start()

    def wait(self):
        for copies in self.copies:
            for copy in copies:
                copy.wait()


def pack_weights(w, packed):
    heads = w.shape[0]
    for i in range(4):
        for y in range(heads):
            k = (i * heads + y) * HEAD_DIM
            packed[:, k : k + HEAD_DIM] = w[y, i]


def turn(values, cos, sine):
    return values * cos + pltpu.roll(values, HEAD_DIM // 2, 1) * sine


def recast(wide, low):
    for m in range(wide.shape[0]):

        def step(rows, m=m):
            low[m, rows] = wide[m, rows].astype(low.dtype)

        by_rows(wide.shape[1], step)


def dma(count):
    return pltpu.SemaphoreType.DMA((count,))


def make_shards(mesh):
    sizes = tuple(mesh.shape[a] for a in ("fsdp", "ctx", "tp"))
    n_f, n_c, n_t = sizes

    def call(kernel, name, collective, outs, ins, out_specs, scratch, aliases=None, vmem=40):
        return pl.pallas_call(
            kernel,
            out_shape=outs,
            in_specs=ins,
            out_specs=out_specs,
            scratch_shapes=scratch,
            input_output_aliases=aliases or {},
            compiler_params=pltpu.CompilerParams(
                collective_id=collective, has_side_effects=True, vmem_limit_bytes=vmem << 20
            ),
            name=name,
        )

    def local(kernel, name, outs, scratch):
        return pl.pallas_call(
            kernel,
            out_shape=outs,
            scratch_shapes=scratch,
            compiler_params=pltpu.CompilerParams(vmem_limit_bytes=60 << 20),
            name=name,
        )

    def front_kernel(
        tok_ref, cot_ref, place, key_place, first, cos, sine, att_ref, out_ref, ffp_ref, ffo_ref,
        rows_ref, attw_ref, ffw_ref, a2_ref, cots_ref, qkv, attended, mass, mid_ref,
        x_ref, own_cot, att_wide, ff_wide, att_low, ff_low, low, a1, packed, lk, lp,
        part, near, sent, got, ss, sr, g1, h1, l1, g2, h2, l2, g3, h3, l3, s4, r4, l4, s5, r5, l5, s6, r6, s7, r7,
    ):
        at = Place(sizes)
        half = x_ref.shape[0]
        mine = pl.ds(pl.multiple_of(at.lo * half, half), half)
        loads = [
            pltpu.make_async_copy(tok_ref.at[at.hi, mine], x_ref, lk.at[0]),
            pltpu.make_async_copy(att_ref, att_wide.at[pl.ds(0, 3)], lk.at[1]),
            pltpu.make_async_copy(out_ref, att_wide.at[3], lk.at[2]),
            pltpu.make_async_copy(ffp_ref, ff_wide.at[pl.ds(0, 2)], lk.at[3]),
            pltpu.make_async_copy(ffo_ref, ff_wide.at[2], lk.at[4]),
            pltpu.make_async_copy(cot_ref.at[at.hi, mine], own_cot, lk.at[5]),
        ]
        for copy in loads:
            copy.start()
        scatter = Scatter(at, part, near, sent, got, ss, sr)
        gather = Gather(at, low, rows_ref, g1, h1, l1)
        cots = Gather(at, own_cot, cots_ref, g2, h2, l2)
        a2 = Gather(at, low, a2_ref, g3, h3, l3)
        swap_att = Swap(at, att_low, attw_ref, s4, r4, l4)
        swap_ff = Swap(at, ff_low, ffw_ref, s5, r5, l5)
        spread_att = Spread(at, attw_ref, s6, r6)
        spread_ff = Spread(at, ffw_ref, s7, r7)
        loads[0].wait()

        def norm_one(rows):
            low[rows] = mean_spread(x_ref[rows].astype(F32))[0].astype(BF)

        by_rows(half, norm_one)
        loads[1].wait()
        loads[2].wait()
        recast(att_wide, att_low)
        at.greet([at.core, *at.all_z(), *at.all_xy()])
        gather.start()
        swap_att.start()
        spread_att.start(swap_att.arrived(0))
        for copy in loads[3:]:
            copy.wait()
        recast(ff_wide, ff_low)
        gather.forward(range(1, 2))
        behind = [s for pair in zip(range(1, n_c), range(n_c - 1, 0, -1)) for s in pair][: n_c - 1]
        spread_att.start(swap_att.arrived(behind[0]))
        spread_att.start(swap_att.arrived(behind[1]))
        gather.forward(range(2, n_c - 1))
        swap_ff.start()
        for s in behind[2:]:
            spread_att.start(swap_att.arrived(s))
        gather.forward(range(n_c - 1, n_c))
        for piece in range(n_c):
            spread_att.forward(piece)
        spread_ff.start(swap_ff.arrived(0))
        gather.finish()
        take = [pltpu.make_async_copy(rows_ref.at[b], a1.at[pl.ds(b * half, half)], lp.at[b]) for b in range(2 * n_c)]
        for copy in take:
            copy.start()
        spread_att.wait()
        heads = attw_ref.shape[0]
        packs = [
            pltpu.make_async_copy(
                attw_ref.at[y, i],
                packed.at[:, pl.ds((i * heads + y) * HEAD_DIM, HEAD_DIM)],
                lp.at[2 * n_c + i * heads + y],
            )
            for i in range(4)
            for y in range(heads)
        ]
        for copy in packs:
            copy.start()
        for copy in (*take, *packs):
            copy.wait()
        attend(a1, packed, place, key_place, first, cos, sine, qkv, attended, mass, part)
        scatter.start()
        cots.start()
        scatter.pass_on(range(n_c - 1, n_c - 2, -1))
        spread_ff.start(swap_ff.arrived(behind[0]))
        spread_ff.start(swap_ff.arrived(behind[1]))
        cots.forward(range(1, 2))
        scatter.pass_on(range(n_c - 2, 1, -1))
        for s in behind[2:]:
            spread_ff.start(swap_ff.arrived(s))
        cots.forward(range(2, 3))
        scatter.pass_on(range(1, 2))
        spread_ff.forward(0)
        scatter.arrive()

        def norm_two(rows):
            mid = x_ref[rows].astype(F32) + scatter.total(rows)
            mid_ref[rows] = mid
            low[rows] = mean_spread(mid)[0].astype(BF)

        by_rows(half, norm_two)
        a2.start()
        a2.forward(range(1, 2))
        spread_ff.forward(n_c - 1)
        a2.forward(range(2, 3))
        for piece in range(1, n_c - 1):
            spread_ff.forward(piece)
        a2.forward(range(3, n_c))
        cots.forward(range(3, n_c))
        cots.finish()
        a2.finish()
        scatter.finish()
        swap_att.finish()
        swap_ff.finish()
        spread_ff.wait()

    def back_kernel(
        a2_ref, cots_ref, joined_ref, d_a2_ref, ffw_ref, mid_ref, tok_ref, cot_ref, a1_ref, attw_ref,
        place, key_place, first, cos, sine, qkv, attended, mass,
        input_ref, out_ref, attg_ref, ffg_ref, norm_ref, grad_ref, rows_ref,
        rows_one, rows_two, wide, sheets, d_v, d_k, own, block, low, x_ref, own_cot, lk, lg, credit,
        part, near, sent, got, ss, sr, g1, h1, l1, lf, s4, r4, l4, s5, r5, l5, s6, r6, l6,
        total, got_p, got_c, s7, r7, *collected,
    ):
        at = Place(sizes)
        half = own.shape[0]
        length, tall = rows_one.shape[0], wide.shape[1]
        mine = pl.ds(pl.multiple_of(at.lo * half, half), half)

        def load(*pairs):
            copies = [pltpu.make_async_copy(src, dst, lk.at[i]) for i, (src, dst) in enumerate(pairs)]
            for copy in copies:
                copy.start()
            for copy in copies:
                copy.wait()

        def in_blocks(src, dst):
            return [(src.at[b], dst.at[pl.ds(b * half, half)]) for b in range(2 * n_c)]

        scatter = Scatter(at, part, near, sent, got, ss, sr)
        gather = Gather(at, low, rows_ref, g1, h1, l1)
        columns = sheets.shape[3]
        high = tall // n_f // 2
        early = [wide.at[1, pl.ds(length, high), pl.ds(i * columns, columns)] for i in range(2)]
        late = [
            [sheets.at[m % 2, 0, pl.ds((m // 2 * 2 + i) * high, high)] for i in range(2)] for m in range(3)
        ]
        collect_ff = Collect(at, grad_ref, lf, *collected[:6])
        collect_att = Collect(at, sheets, None, *collected[6:])
        give_ff = Return(at, collected[1], ffg_ref, s5, r5, l5)
        give_att = Return(at, collected[7], attg_ref, s4, r4, l4)
        load((d_a2_ref, part))
        at.greet([*plane(at), *at.all_z()])
        scatter.start()
        load(
            (a2_ref, rows_one),
            (cots_ref, rows_two),
            (joined_ref.at[0], wide.at[0, pl.ds(0, length)]),
            (joined_ref.at[1], wide.at[0, pl.ds(length, length)]),
            (joined_ref.at[2], wide.at[1, pl.ds(0, length)]),
            (tok_ref.at[at.hi, mine], x_ref),
            (cot_ref.at[at.hi, mine], own_cot),
        )

        def keep(k):
            y, m = k % 2, k // 2
            return pltpu.make_async_copy(sheets.at[y, 0], grad_ref.at[y, m], lg.at[y])

        for k in range(6):
            y, m = k % 2, k // 2
            if k >= 2 and y == 0:
                keep(k - 2).wait()
                keep(k - 1).wait()
            rows = rows_two if m == 2 else rows_one
            slot, start = ((0, 0), (0, length), (1, 0))[m]

            @pl.loop(0, 2)
            def _(i, y=y, rows=rows, slot=slot, start=start):
                cols = pl.ds(pl.multiple_of(i * (tall // 2), tall // 2), tall // 2)
                side = wide[slot, start : start + length, y * columns : (y + 1) * columns]
                sheets[y, 0, cols] = dot(rows[:, cols], side, ((0,), (0,))).astype(BF)

            keep(k).start()
            if k == 0:
                scatter.pass_on(range(n_c - 1, n_c - 2, -1))
            if k == 2:
                collect_ff.start(0)
            if k == 3:
                scatter.pass_on(range(n_c - 2, 1, -1))
            if k == 4:
                collect_ff.start(1)
        keep(4).wait()
        keep(5).wait()
        collect_ff.start(2)
        collect_ff.fetch(0, early)
        scatter.pass_on(range(1, 2))
        scatter.arrive()

        def norm_two(rows):
            normed, scale = mean_spread(mid_ref[rows])
            grad = own_cot[rows].astype(F32) + norm_back(scatter.total(rows), normed, scale)
            own[rows] = grad
            low[rows] = grad.astype(BF)

        by_rows(half, norm_two)
        gather.start()
        heads = attw_ref.shape[0]
        load(*((ffw_ref.at[y, 2], wide.at[0, :, pl.ds(y * columns, columns)]) for y in range(heads)))
        scatter.finish()
        scatter.free(credit.at[0])
        width = part.shape[2] // 4

        @pl.loop(0, 4)
        def _(c):
            cols = pl.ds(pl.multiple_of(c * width, width), width)
            value = dot(wide[1, :length], wide[0, cols], ((1,), (1,))).astype(BF)
            part[:, :, cols] = value.reshape(part.shape[0], part.shape[1], width)

        gather.forward(range(1, 2))
        collect_ff.forward(0, early)
        collect_ff.fetch(1, early)
        gather.forward(range(2, n_c - 1))
        scatter.start()
        collect_ff.forward(1, early)
        collect_ff.fetch(2, early)
        for m in range(3):
            collect_ff.fetch_own(m, late[m])
        collect_ff.forward(2, early)
        gather.forward(range(n_c - 1, n_c))
        load(
            *in_blocks(a1_ref, rows_two),
            *(
                (attw_ref.at[y, i], wide.at[0, :, pl.ds((i * heads + y) * HEAD_DIM, HEAD_DIM)])
                for i in range(4)
                for y in range(heads)
            ),
        )
        scatter.pass_on(range(n_c - 1, n_c - 2, -1))
        gather.finish()
        load(*in_blocks(rows_ref, rows_one))
        packed, joint = wide.at[0], wide.at[1, pl.ds(length, length)]
        wide_heads = heads * HEAD_DIM
        joint[:, :wide_heads] = dot(rows_one[...], packed[:, 3 * wide_heads :], ((1,), (0,))).astype(BF)
        for y in range(heads):
            attend_back(y, packed, joint, place, key_place, first, cos, sine, qkv, mass, d_v, d_k, heads)
            if y == 0:
                scatter.pass_on(range(n_c - 2, 1, -1))
                collect_ff.total(0, late[0])
        scatter.pass_on(range(1, 2))
        give_ff.start(0)
        collect_ff.total(1, late[1])
        scatter.arrive()
        give_ff.start(1)
        collect_ff.total(2, late[2])
        give_ff.start(2)

        def add(rows):
            block[rows] = (mid_ref[rows] + scatter.total(rows)).astype(BF)

        by_rows(half, add)
        scatter.finish()
        scatter.free(credit.at[1])

        @pl.loop(0, 4)
        def _(c):
            cols = pl.ds(pl.multiple_of(c * width, width), width)
            value = dot(joint[:, : 3 * wide_heads], packed[cols, : 3 * wide_heads], ((1,), (1,))).astype(BF)
            part[:, :, cols] = value.reshape(part.shape[0], part.shape[1], width)

        scatter.start()

        @pl.loop(0, 2)
        def _(c):
            cols = pl.ds(pl.multiple_of(c * 2 * width, width), 2 * width)
            for i in range(4):
                if i < 3:
                    value = dot(
                        rows_two[:, cols], joint[:, i * wide_heads : (i + 1) * wide_heads], ((0,), (0,))
                    )
                else:
                    value = dot(rows_one[:, cols], attended[...], ((0,), (0,)))
                for y in range(heads):
                    sheets[y, 0, cols, i * HEAD_DIM : (i + 1) * HEAD_DIM] = value[
                        :, y * HEAD_DIM : (y + 1) * HEAD_DIM
                    ].astype(BF)

        collect_att.start(0)
        scatter.pass_on(range(n_c - 1, n_c - 2, -1))
        share_block = Share(at, block, out_ref, s6.at[0], r6.at[0], l6.at[0])
        share_input = Share(at, low, input_ref, s6.at[1], r6.at[1], l6.at[1])
        share_block.start()
        collect_att.forward(0)
        scatter.pass_on(range(n_c - 2, 1, -1))
        share_block.forward()
        collect_att.total(0)
        for m in range(4):
            give_att.start(m)
        scatter.pass_on(range(1, 2))
        scatter.arrive()

        def norm_one(rows):
            normed, scale = mean_spread(x_ref[rows].astype(F32))
            low[rows] = (own[rows] + norm_back(scatter.total(rows), normed, scale)).astype(BF)

        by_rows(half, norm_one)
        share_input.start()
        scatter.finish()
        collect_ff.finish()
        collect_att.finish()
        share_input.forward()
        give_ff.wait()
        give_att.wait()
        own_rows, own_cols = ffg_ref.shape[1], attg_ref.shape[2]
        ff_low = [rows_one.at[pl.ds(m * own_rows, own_rows)] for m in range(3)]
        att_low = [
            rows_two.at[pl.ds(0, own_rows), pl.ds(m * own_cols, own_cols)] for m in range(4)
        ]
        load(
            *((ffg_ref.at[m], ff_low[m]) for m in range(3)),
            *((attg_ref.at[m], att_low[m]) for m in range(4)),
        )
        sum_norm(at, (*ff_low, *att_low), norm_ref, total, got_p, got_c, s7, r7)
        share_block.finish()
        share_input.finish()

    def plane(at):
        count = n_f * n_t
        here = at.f * n_t + at.t
        others = [lax.rem(here + i, count) for i in range(1, count)]
        return [(i // n_t, at.c, lax.rem(i, n_t)) for i in others]

    def sum_norm(at, grads, norm_ref, total, got_p, got_c, send, recv):
        total[0] = jnp.zeros(total.shape[1:], F32)
        for low in grads:

            def square(rows, low=low):
                value = low[rows].astype(F32)
                value = value * value
                value = value[: ROWS // 2] + value[ROWS // 2 :]
                lanes = value[:, :128]
                for c in range(1, value.shape[1] // 128):
                    lanes = lanes + value[:, c * 128 : (c + 1) * 128]
                total[0] += lanes

            by_rows(low.shape[0], square)
        base = 0
        stages = ((plane(at), got_p, at.f * n_t + at.t), (at.all_z(), got_c, at.c))
        for stage, (peers, got, place) in enumerate(stages):
            copies = [
                remote(total.at[stage], got.at[place], send.at[base + i], recv.at[base + i], peer)
                for i, peer in enumerate(peers)
            ]
            base += len(peers)
            for copy in copies:
                copy.start()
            got[place] = total[stage]
            for copy in copies:
                copy.wait()
            value = got[0]
            for i in range(1, got.shape[0]):
                value = value + got[i]
            total[stage + 1] = value
        norm = jnp.sqrt(jnp.sum(total[2], axis=(0, 1), keepdims=True))
        norm_ref[...] = jnp.broadcast_to(norm, norm_ref.shape)

    def finish_kernel(norm_ref, block_in, input_in, attg_ref, ffg_ref, *refs):
        olds, outs, scratch = refs[:12], refs[12:34], refs[34:]
        low_att, low_ff, wide_att, wide_ff, old_att, old_ff, block_keep, input_low, input_keep, ls = scratch
        groups = (
            (attg_ref, low_att, wide_att, old_att, 0, attg_ref.shape[1]),
            (ffg_ref, low_ff, wide_ff, old_ff, 2, attg_ref.shape[1] // 4),
        )
        chunks = [
            (group, m, r)
            for group in groups
            for m in range(group[0].shape[0])
            for r in range(group[0].shape[1] // group[5])
        ]

        def sheet(array, first, m, group):
            last = group[0].shape[0] - 1
            return array[first + 1] if m == last else array[first].at[m]

        loads, stores = [], []
        for i, (group, m, r) in enumerate(chunks):
            here = pl.ds(r * group[5], group[5])
            one = [pltpu.make_async_copy(group[0].at[m, here], group[1].at[m, here], ls.at[i, 0, 3])]
            one += [
                pltpu.make_async_copy(
                    sheet(olds, 4 * j + group[4], m, group).at[here], group[3].at[j, m, here], ls.at[i, 0, j]
                )
                for j in range(3)
            ]
            for copy in one:
                copy.start()
            loads.append(one)
        kept = ((block_in, block_keep, block_keep, outs[20]), (input_in, input_low, input_keep, outs[21]))
        through = []
        for i, (src, first, keep, out) in enumerate(kept):
            copy = pltpu.make_async_copy(src, first, ls.at[len(chunks), 0, i])
            copy.start()
            through.append((copy, pltpu.make_async_copy(keep, out, ls.at[len(chunks), 1, i])))
        norm = norm_ref[0:1, 0:1]
        clip = jnp.minimum(1.0, MAX_NORM / (norm + 1e-06))
        width = ffg_ref.shape[1] * n_f * n_c
        for i, (group, m, r) in enumerate(chunks):
            for copy in loads[i]:
                copy.wait()
            low, wide, old = group[1:4]
            rate = (width // 32) ** (-0.5) if group[4] == 0 and m == 3 else width ** (-0.5)

            @pl.loop(0, group[5] // ROWS)
            def _(k, low=low, wide=wide, old=old, m=m, r=r, step=group[5], rate=rate):
                rows = pl.ds(pl.multiple_of(r * step + k * ROWS, ROWS), ROWS)
                grad = low[m, rows].astype(F32)
                wide[m, rows] = grad
                first_new, second_new, weight_new = adam_step(
                    old[0, m, rows], grad, old[1, m, rows], old[2, m, rows], clip, rate
                )
                old[0, m, rows] = weight_new
                old[1, m, rows] = first_new
                old[2, m, rows] = second_new
                low[m, rows] = weight_new.astype(BF)

            here = pl.ds(r * group[5], group[5])
            for k, (src, out) in enumerate(
                ((wide, 0), (old.at[1], 4), (old.at[2], 8), (old.at[0], 12), (low, 16))
            ):
                store = pltpu.make_async_copy(
                    src.at[m, here], sheet(outs, out + group[4], m, group).at[here], ls.at[i, 1, k]
                )
                store.start()
                stores.append(store)
        for load, store in through:
            load.wait()
            if load is through[1][0]:
                recast(input_low, input_keep)
            store.start()
            stores.append(store)
        for store in stores:
            store.wait()

    def attend(a1, packed, place, key_place, first, cos, sine, qkv, attended, mass, part):
        wide = attended.shape[1]
        heads = wide // HEAD_DIM
        for i in range(3):
            joint = dot(a1[...], packed[:, i * wide : (i + 1) * wide], ((1,), (0,)))
            for y in range(heads):
                cols = slice(y * HEAD_DIM, (y + 1) * HEAD_DIM)
                head = joint[:, cols]
                if i < 2:
                    head = turn(head, cos[...], sine[...])
                qkv[i, :, cols] = head.astype(BF)
        for y in range(heads):
            cols = slice(y * HEAD_DIM, (y + 1) * HEAD_DIM)

            @pl.loop(0, a1.shape[0] // QUERIES)
            def _(c, y=y, cols=cols):
                rows = pl.ds(pl.multiple_of(c * QUERIES, QUERIES), QUERIES)
                scores = dot(qkv[0, rows, cols], qkv[1, :, cols], ((1,), (1,))) * SCORE_SCALE
                allowed = (key_place[...] <= place[rows]) & (key_place[...] >= first[rows])
                scores = jnp.where(allowed, scores, NEG_FILL)
                peak = jnp.max(scores, axis=1, keepdims=True)
                exp_scores = jnp.exp(scores - peak)
                total = jnp.sum(exp_scores, axis=1, keepdims=True)
                probs = (exp_scores * (1.0 / total)).astype(BF)
                attended[rows, cols] = dot(probs, qkv[2, :, cols], ((1,), (0,))).astype(BF)
                mass[rows, y : y + 1] = peak + jnp.log(total)

        width = part.shape[2] // 4

        @pl.loop(0, 4)
        def _(c):
            cols = pl.ds(pl.multiple_of(c * width, width), width)
            value = dot(attended[...], packed[cols, 3 * wide :], ((1,), (1,))).astype(BF)
            part[:, :, cols] = value.reshape(part.shape[0], part.shape[1], width)

    def attend_back(y, packed, joint, place, key_place, first, cos, sine, qkv, mass, d_v, d_k, heads):
        wide = heads * HEAD_DIM
        cols = slice(y * HEAD_DIM, (y + 1) * HEAD_DIM)

        @pl.loop(0, qkv.shape[1] // QUERIES)
        def _(c):
            rows = pl.ds(pl.multiple_of(c * QUERIES, QUERIES), QUERIES)
            query, key, value = qkv[0, rows, cols], qkv[1, :, cols], qkv[2, :, cols]
            d_att = joint[rows, cols]
            scores = dot(query, key, ((1,), (1,))) * SCORE_SCALE
            allowed = (key_place[...] <= place[rows]) & (key_place[...] >= first[rows])
            probs = jnp.exp(jnp.where(allowed, scores, NEG_FILL) - mass[rows, y : y + 1])
            d_prob = dot(d_att, value, ((1,), (1,)))
            delta = jnp.sum(probs * d_prob, axis=1, keepdims=True)
            d_score = (probs * (d_prob - delta)).astype(BF)
            v_part = dot(probs.astype(BF), d_att, ((0,), (0,)))
            k_part = dot(d_score, query, ((0,), (0,)))

            @pl.when(c == 0)
            def _():
                d_v[...] = v_part
                d_k[...] = k_part

            @pl.when(c > 0)
            def _():
                d_v[...] += v_part
                d_k[...] += k_part

            d_query = dot(d_score, key, ((1,), (0,))) * SCORE_SCALE
            joint[rows, cols] = turn(d_query, cos[rows], -sine[rows]).astype(BF)

        joint[:, wide + y * HEAD_DIM : wide + (y + 1) * HEAD_DIM] = turn(
            d_k[...] * SCORE_SCALE, cos[...], -sine[...]
        ).astype(BF)
        joint[:, 2 * wide + y * HEAD_DIM : 2 * wide + (y + 1) * HEAD_DIM] = d_v[...].astype(BF)

    def hidden_kernel(a2, cot, w, d_a2, joined, kept):
        d_up, d_gate, hidden = joined.at[0], joined.at[1], joined.at[2]
        step, steps = pl.program_id(0), pl.num_programs(0)
        tile = w.shape[3]
        here = pl.ds(pl.multiple_of(step * tile, tile), tile)
        length, width = a2.shape
        chunk = length // 2

        @pl.loop(0, 2)
        def _(i):
            rows = pl.ds(pl.multiple_of(i * chunk, chunk), chunk)
            up = dot(a2[rows], w[0, 0], ((1,), (0,)))
            gate = dot(a2[rows], w[0, 1], ((1,), (0,)))
            d_hid = dot(cot[rows], w[0, 2], ((1,), (0,)))
            sigma = jax.nn.sigmoid(gate)
            act = gate * sigma
            hidden[rows, here] = (act * up).astype(BF)
            d_up[rows, here] = (d_hid * act).astype(BF)
            d_gate[rows, here] = (d_hid * up * sigma * (1.0 + gate * (1.0 - sigma))).astype(BF)

        for m in range(2):
            kept[m, :, here] = w[0, m]

        @pl.when(step == steps - 1)
        def _():
            @pl.loop(0, 8)
            def _(i):
                cols = pl.ds(pl.multiple_of(i * (width // 8), width // 8), width // 8)
                d_a2[:, cols] = (
                    dot(d_up[...], kept[0, cols], ((1,), (1,)))
                    + dot(d_gate[...], kept[1, cols], ((1,), (1,)))
                ).astype(BF)

    def shards(
        tokens,
        cotangent,
        lengths,
        deal,
        att_proj,
        attn_out,
        ff_proj,
        ff_out,
        att_proj_first,
        attn_out_first,
        ff_proj_first,
        ff_out_first,
        att_proj_second,
        attn_out_second,
        ff_proj_second,
        ff_out_second,
    ):
        t_at = lax.axis_index("tp")
        pack_at = t_at // 2
        packs, row_count, width = tokens.shape
        half = row_count // 2
        pack_len = deal.shape[1]
        blocks = n_c * 2
        rows_bf = jax.ShapeDtypeStruct((blocks, half, width), BF)
        own_f32 = jax.ShapeDtypeStruct((half, width), F32)

        att_cols, ff_cols = att_proj.shape[2] // n_c, ff_proj.shape[2] // n_c
        att_shape, ff_shape = (4, *att_proj.shape[1:]), (3, *ff_proj.shape[1:])
        att_full = jax.ShapeDtypeStruct((2, 4, width, att_cols), BF)
        ff_full = jax.ShapeDtypeStruct((2, 3, width, ff_cols), BF)
        places = lax.dynamic_index_in_dim(deal, pack_at, 0, keepdims=False)
        length_row = lax.dynamic_index_in_dim(lengths, pack_at, 0, keepdims=False)
        seqs = lengths.shape[1]
        before = jnp.arange(seqs)[:, None] > jnp.arange(seqs)[None, :]
        starts = jnp.sum(jnp.where(before, length_row[None, :], 0), axis=1)
        inside = (places[:, None] >= starts[None, :]) & (
            places[:, None] < (starts + length_row)[None, :]
        )
        firsts = jnp.sum(jnp.where(inside, starts[None, :], 0), axis=1)
        freq_steps = jnp.arange(HEAD_DIM // 2, dtype=F32)
        inverse = jnp.power(10000.0, -2.0 * freq_steps / HEAD_DIM)
        angles = (places - firsts).astype(F32)[:, None] * inverse[None, :]
        cos_table, sine_table = jnp.cos(angles), jnp.sin(angles)
        tables = (
            places[:, None],
            places[None, :],
            firsts[:, None],
            jnp.concatenate([cos_table, cos_table], axis=1),
            jnp.concatenate([-sine_table, sine_table], axis=1),
        )
        rank_width = 2 * att_cols
        act_one, att_w, ff_w, act_two, cot_rows, qkv, attended, mass, resid_mid = call(
            front_kernel,
            "front",
            0,
            (
                rows_bf,
                att_full,
                ff_full,
                rows_bf,
                rows_bf,
                jax.ShapeDtypeStruct((3, pack_len, rank_width), BF),
                jax.ShapeDtypeStruct((pack_len, rank_width), BF),
                jax.ShapeDtypeStruct((pack_len, 2), F32),
                own_f32,
            ),
            [ANY, ANY] + [VMEM] * 5 + [ANY] * 4,
            (ANY,) * 5 + (VMEM,) * 4,
            [
                pltpu.VMEM((half, width), BF),
                pltpu.VMEM((half, width), BF),
                pltpu.VMEM(att_shape, F32),
                pltpu.VMEM(ff_shape, F32),
                pltpu.VMEM(att_shape, BF),
                pltpu.VMEM(ff_shape, BF),
                pltpu.VMEM((half, width), BF),
                pltpu.VMEM((pack_len, width), BF),
                pltpu.VMEM((width, 4 * rank_width), BF),
                dma(6),
                dma(2 * n_c + 8),
            ]
            + scatter_scratch(n_c, half, width)
            + gather_sems(n_c) * 3
            + [dma(n_c), dma(n_c), pltpu.SemaphoreType.DMA] * 2
            + [dma(2 * n_f * n_c)] * 4,
            vmem=56,
        )(tokens, cotangent, *tables, att_proj, attn_out, ff_proj, ff_out)
        act_two = act_two.reshape(pack_len, width)
        cot_rows = cot_rows.reshape(pack_len, width)

        tile = 256
        tiles = ff_cols // tile
        kept = pl.BlockSpec((pack_len, width), lambda i: (0, 0), pipeline_mode=pl.Buffered(1))
        moved = pl.BlockSpec((1, 3, width, tile), lambda i: (i // tiles, 0, 0, i % tiles))
        rows_flat = jax.ShapeDtypeStruct((pack_len, width), BF)
        act_two_part, joined = pl.pallas_call(
            hidden_kernel,
            grid=(2 * tiles,),
            out_shape=(rows_flat, jax.ShapeDtypeStruct((3, pack_len, 2 * ff_cols), BF)),
            in_specs=[kept, kept, moved],
            out_specs=(
                kept,
                pl.BlockSpec((3, pack_len, 2 * ff_cols), lambda i: (0, 0, 0), pipeline_mode=pl.Buffered(1)),
            ),
            scratch_shapes=[pltpu.VMEM((2, width, 2 * ff_cols), BF)],
            compiler_params=pltpu.CompilerParams(vmem_limit_bytes=60 << 20),
            name="hidden",
        )(act_two, cot_rows, ff_w)
        height = width // n_f
        count = n_f * n_t + n_c
        input_grad, block_out, att_total, ff_total, norm_value, *_ = call(
            back_kernel,
            "back",
            1,
            (
                jax.ShapeDtypeStruct((n_t, half, width), BF),
                jax.ShapeDtypeStruct((n_t, half, width), BF),
                jax.ShapeDtypeStruct(att_shape, BF),
                jax.ShapeDtypeStruct(ff_shape, BF),
                jax.ShapeDtypeStruct((8, 128), F32),
                ff_full,
                rows_bf,
            ),
            [ANY] * 5 + [VMEM] + [ANY] * 4 + [VMEM] * 8,
            (ANY,) * 4 + (VMEM,) + (ANY,) * 2,
            [
                pltpu.VMEM((pack_len, width), BF),
                pltpu.VMEM((pack_len, width), BF),
                pltpu.VMEM((2, width, 4 * rank_width), BF),
                pltpu.VMEM((2, 1, width, 4 * att_cols), BF),
                pltpu.VMEM((pack_len, HEAD_DIM), F32),
                pltpu.VMEM((pack_len, HEAD_DIM), F32),
                pltpu.VMEM((half, width), F32),
                pltpu.VMEM((half, width), BF),
                pltpu.VMEM((half, width), BF),
                pltpu.VMEM((half, width), BF),
                pltpu.VMEM((half, width), BF),
                dma(2 * n_c + 8),
                dma(2),
                pltpu.SemaphoreType.REGULAR((2, 3)),
            ]
            + scatter_scratch(n_c, half, width)
            + gather_sems(n_c)
            + [dma(8)]
            + [dma(4 * n_c), dma(4 * n_c), dma(4), dma(3 * n_c), dma(3 * n_c), dma(3)]
            + [
                pltpu.SemaphoreType.DMA((2, 3)),
                pltpu.SemaphoreType.DMA((2, 3)),
                dma(2),
            ]
            + [pltpu.VMEM((k, 8, 128), F32) for k in (3, n_f * n_t, n_c)]
            + [dma(count), dma(count)]
            + collect_scratch(n_f, 3, height, ff_cols)
            + collect_scratch(n_f, 1, height, 4 * att_cols),
            vmem=62,
        )(
            act_two, cot_rows, joined, act_two_part.reshape(rows_bf.shape), ff_w,
            resid_mid, tokens, cotangent, act_one, att_w, *tables, qkv, attended, mass,
        )
        weights = (att_proj, attn_out, ff_proj, ff_out)
        firsts_old = (att_proj_first, attn_out_first, ff_proj_first, ff_out_first)
        seconds_old = (att_proj_second, attn_out_second, ff_proj_second, ff_out_second)
        results = pl.pallas_call(
            finish_kernel,
            out_shape=(
                *(jax.ShapeDtypeStruct(w.shape, F32) for w in weights * 4),
                *(jax.ShapeDtypeStruct(w.shape, BF) for w in weights),
                jax.ShapeDtypeStruct(block_out.shape, BF),
                jax.ShapeDtypeStruct(input_grad.shape, F32),
            ),
            in_specs=[VMEM] + [ANY] * 16,
            out_specs=(ANY,) * 22,
            scratch_shapes=[
                pltpu.VMEM(att_shape, BF),
                pltpu.VMEM(ff_shape, BF),
                pltpu.VMEM(att_shape, F32),
                pltpu.VMEM(ff_shape, F32),
                pltpu.VMEM((3, *att_shape), F32),
                pltpu.VMEM((3, *ff_shape), F32),
                pltpu.VMEM(block_out.shape, BF),
                pltpu.VMEM(input_grad.shape, BF),
                pltpu.VMEM(input_grad.shape, F32),
                pltpu.SemaphoreType.DMA((17, 2, 5)),
            ],
            compiler_params=pltpu.CompilerParams(vmem_limit_bytes=56 << 20),
            name="finish",
        )(norm_value, block_out, input_grad, att_total, ff_total, *weights, *firsts_old, *seconds_old)
        return (
            results[20].reshape(tokens.shape),
            results[21].reshape(tokens.shape),
            norm_value[0, :1],
            *results[:20],
        )

    return shards


def solution(mesh):
    act = P("fsdp", "ctx", None)
    table = P("fsdp", None)
    cube = P(None, ("fsdp", "ctx"), "tp")
    flat = P(("fsdp", "ctx"), "tp")
    group = (cube, flat, cube, flat)
    in_specs = (act, act, table, table) + group * 3
    out_specs = (act, act, P()) + group * 5
    return jax.shard_map(
        make_shards(mesh), mesh=mesh, in_specs=in_specs, out_specs=out_specs, check_vma=False
    )
```

```python
import functools

import jax
import jax.numpy as jnp
from jax import lax
from jax.experimental import pallas as pl
from jax.experimental.pallas import tpu as pltpu
from jax.sharding import PartitionSpec as P

HEAD_DIM = 128
STEP = 10
EPS_NORM = 1e-05
BETA_ONE = 0.9
BETA_TWO = 0.95
EPS_ADAM = 1e-08
DECAY = 0.1
MAX_NORM = 1.0
NEG_FILL = -1e30
BF = jnp.bfloat16
F32 = jnp.float32
MESH = pl.DeviceIdType.MESH
ANY = pl.BlockSpec(memory_space=pl.ANY)
VMEM = pl.BlockSpec(memory_space=pltpu.VMEM)
ROWS = 16
STEP_ROWS = 32
QUERIES = 256
SCORE_SCALE = HEAD_DIM ** (-0.5)


def mean_spread(values):
    centre = values - jnp.mean(values, axis=-1, keepdims=True)
    spread = jnp.mean(centre * centre, axis=-1, keepdims=True)
    scale = lax.rsqrt(spread + EPS_NORM)
    return centre * scale, scale


def norm_back(grad, normed, scale):
    return scale * (
        grad
        - jnp.mean(grad, axis=-1, keepdims=True)
        - normed * jnp.mean(grad * normed, axis=-1, keepdims=True)
    )


def dot(left, right, dims):
    return lax.dot_general(left, right, (dims, ((), ())), preferred_element_type=F32)


def adam_step(weight, grad_sum, first, second, clip_factor, learn_rate):
    clipped = grad_sum * clip_factor
    first_new = BETA_ONE * first + (1.0 - BETA_ONE) * clipped
    second_new = BETA_TWO * second + (1.0 - BETA_TWO) * clipped * clipped
    first_hat = first_new / (1.0 - BETA_ONE**STEP)
    second_hat = second_new / (1.0 - BETA_TWO**STEP)
    weight_new = weight - learn_rate * (
        first_hat / (jnp.sqrt(second_hat) + EPS_ADAM) + DECAY * weight
    )
    return (first_new, second_new, weight_new)


class Place:
    def __init__(self, sizes):
        self.n_f, self.n_c, self.n_t = sizes
        self.f, self.c, self.t = (lax.axis_index(a) for a in ("fsdp", "ctx", "tp"))
        self.hi, self.lo = self.t // 2, lax.rem(self.t, 2)
        self.core = (self.f, self.c, self.t + 1 - 2 * self.lo)
        self.block = self.c * 2 + self.lo
        self.pairs = [(s, o) for o in range(2) for s in range(self.n_f) if s or o]

    def ctx(self, shift):
        return lax.rem(self.c + shift + self.n_c, self.n_c)

    def fsdp(self, shift):
        return lax.rem(self.f + shift + self.n_f, self.n_f)

    def other(self, o):
        return self.hi + o * (1 - 2 * self.hi)

    def z(self, shift):
        return (self.f, self.ctx(shift), self.t)

    def xy(self, shift, o):
        return (self.fsdp(shift), self.c, self.t + o * (2 - 4 * self.hi))

    def greet(self, peers):
        barrier = pltpu.get_barrier_semaphore()
        for peer in peers:
            pl.semaphore_signal(barrier, inc=1, device_id=peer, device_id_type=MESH)
        pl.semaphore_wait(barrier, len(peers))

    def all_z(self):
        return [self.z(s) for s in range(1, self.n_c)]

    def all_xy(self):
        return [self.xy(s, o) for s, o in self.pairs]


def remote(src, dst, send, recv, peer):
    return pltpu.make_async_remote_copy(
        src_ref=src, dst_ref=dst, send_sem=send, recv_sem=recv, device_id=peer, device_id_type=MESH
    )


def by_rows(count, step):
    @pl.loop(0, count // ROWS)
    def _(i):
        step(pl.ds(pl.multiple_of(i * ROWS, ROWS), ROWS))


class Gather:
    def __init__(self, at, src, out, send, recv, local):
        self.at, self.src, self.out, self.send, self.recv = at, src, out, send, recv
        self.local = pltpu.make_async_copy(src, out.at[at.block], local)

    def far(self, way, hop, src=None):
        at = self.at
        block = self.out.at[jnp.clip(at.c - way * (hop - 1), 0, at.n_c - 1) * 2 + at.lo]
        k = hop + (0 if way > 0 else at.n_c)
        return remote(
            block if src is None else src, block, self.send.at[k], self.recv.at[k], at.z(way)
        )

    def near(self, distance, src=None):
        at = self.at
        block = self.out.at[jnp.clip(at.c - distance, 0, at.n_c - 1) * 2 + at.lo]
        k = 2 * at.n_c + distance + at.n_c
        return remote(
            block if src is None else src, block, self.send.at[k], self.recv.at[k], at.core
        )

    def there(self, way, hop):
        return self.at.c + hop < self.at.n_c if way > 0 else self.at.c >= hop

    def start(self):
        for way in (1, -1):

            @pl.when(self.there(way, 1))
            def _(way=way):
                self.far(way, 1, self.src).start()

        self.near(0, self.src).start()
        self.local.start()

    def forward(self, hops=None):
        at = self.at
        for hop in hops or range(1, at.n_c):
            for way in (1, -1):

                @pl.when(self.there(-way, hop))
                def _(way=way, hop=hop):
                    self.far(way, hop).wait_recv()
                    if hop < at.n_c - 1:

                        @pl.when(self.there(way, 1))
                        def _():
                            self.far(way, hop + 1).start()

                    self.near(way * hop).start()

    def finish(self):
        at = self.at
        for hop in range(1, at.n_c):
            for way in (1, -1):

                @pl.when(self.there(way, 1) & self.there(-way, hop - 1))
                def _(way=way, hop=hop):
                    self.far(way, hop).wait_send()

                @pl.when(self.there(-way, hop))
                def _(way=way, hop=hop):
                    self.near(way * hop).wait()

        self.near(0, self.src).wait()
        self.local.wait()


def gather_sems(n_c):
    return [
        pltpu.SemaphoreType.DMA((4 * n_c,)),
        pltpu.SemaphoreType.DMA((4 * n_c,)),
        pltpu.SemaphoreType.DMA,
    ]


class Scatter:
    def __init__(self, at, part, near, sent, got, send, recv):
        self.at, self.part, self.near = at, part, near
        self.sent, self.got, self.send, self.recv = sent, got, send, recv

    def core(self, c):
        at = self.at
        return remote(
            self.part.at[c * 2 + 1 - at.lo], self.near.at[c], self.send.at[c], self.recv.at[c], at.core
        )

    def far(self, way, hop, slot):
        at = self.at
        k = at.n_c + hop + (0 if way > 0 else at.n_c)
        sent = self.sent.at[self.slot(jnp.clip(at.c + way * hop, 0, at.n_c - 1))]
        return remote(sent, self.got.at[slot], self.send.at[k], self.recv.at[k], at.z(way))

    def slot(self, c):
        return jnp.minimum(jnp.where(c > self.at.c, c - 1, c), self.at.n_c - 2)

    def end(self, way):
        return self.at.c if way > 0 else self.at.n_c

    there = Gather.there

    def start(self):
        at = self.at
        for i in range(at.n_c):
            self.core(jnp.where(at.c * 2 < at.n_c, at.n_c - 1 - i, i)).start()

    def pass_on(self, hops=None):
        at = self.at
        for hop in hops or range(at.n_c - 1, 0, -1):
            for way in (1, -1):

                @pl.when(self.there(way, hop))
                def _(way=way, hop=hop):
                    c = at.c + way * hop
                    self.core(c).wait_recv()
                    if hop < at.n_c - 1:
                        more = self.there(-way, 1)

                        @pl.when(more)
                        def _():
                            self.far(way, hop + 1, c).wait_recv()
                            self.add(c, True)

                        @pl.when(jnp.logical_not(more))
                        def _():
                            self.add(c, False)

                    else:
                        self.add(c, False)
                    self.far(way, hop, at.n_c if hop == 1 and way < 0 else c).start()

    def add(self, c, more):
        at, slot = self.at, self.slot(c)

        def rows_of(rows):
            value = self.part[c * 2 + at.lo, rows].astype(F32) + self.near[c, rows].astype(F32)
            if more:
                value = value + self.got[c, rows].astype(F32)
            self.sent[slot, rows] = value.astype(BF)

        by_rows(self.near.shape[1], rows_of)

    def arrive(self):
        self.core(self.at.c).wait_recv()
        for way in (1, -1):

            @pl.when(self.there(-way, 1))
            def _(way=way):
                self.far(way, 1, self.end(way)).wait_recv()

            @pl.when(jnp.logical_not(self.there(-way, 1)))
            def _(way=way):
                self.got[self.end(way)] = jnp.zeros(self.got.shape[1:], BF)

    def total(self, rows):
        c, at = self.at.c, self.at
        return (
            self.part[c * 2 + at.lo, rows].astype(F32)
            + self.near[c, rows].astype(F32)
            + self.got[self.end(1), rows].astype(F32)
            + self.got[self.end(-1), rows].astype(F32)
        )

    def free(self, credit):
        at = self.at

        def tell(k, peer):
            pl.semaphore_signal(credit.at[k], inc=1, device_id=peer, device_id_type=MESH)

        tell(0, at.core)
        for k, way in ((1, 1), (2, -1)):

            @pl.when(self.there(way, 1))
            def _(k=k, way=way):
                tell(k, at.z(way))

        pl.semaphore_wait(credit.at[0], 1)
        for k, way in ((1, 1), (2, -1)):

            @pl.when(self.there(-way, 1))
            def _(k=k):
                pl.semaphore_wait(credit.at[k], 1)

    def finish(self):
        at = self.at
        for c in range(at.n_c):
            self.core(c).wait_send()
        for hop in range(1, at.n_c):
            for way in (1, -1):

                @pl.when(self.there(way, hop))
                def _(way=way, hop=hop):
                    self.far(way, hop, 0).wait_send()


def scatter_scratch(n_c, half, width):
    return [
        pltpu.VMEM((2 * n_c, half, width), BF),
        pltpu.VMEM((n_c, half, width), BF),
        pltpu.VMEM((n_c - 1, half, width), BF),
        pltpu.VMEM((n_c + 1, half, width), BF),
        pltpu.SemaphoreType.DMA((3 * n_c,)),
        pltpu.SemaphoreType.DMA((3 * n_c,)),
    ]


class Swap:
    def __init__(self, at, shard, full, send, recv, local):
        self.at = at
        rows, width = shard.shape[1], full.shape[3]
        here = pl.ds((at.f * at.n_c + at.c) * rows, rows)
        target = full.at[at.hi, :, here, :]

        def columns(c):
            return shard.at[:, :, pl.ds(pl.multiple_of(c * width, 128), width)]

        self.local = pltpu.make_async_copy(columns(at.c), target, local)
        self.far = [
            remote(columns(at.ctx(s)), target, send.at[s], recv.at[s], at.z(s))
            for s in range(1, at.n_c)
        ]

    def start(self):
        self.local.start()
        for copy in self.far:
            copy.start()

    def arrived(self, s):
        if s == 0:
            self.local.wait()
        else:
            self.far[s - 1].wait_recv()
        return self.at.ctx(-s)

    def finish(self):
        for copy in self.far:
            copy.wait_send()


class Spread:
    def __init__(self, at, full, send, recv):
        self.at, self.full, self.send, self.recv = at, full, send, recv
        self.height = full.shape[2] // at.n_f // at.n_c

    def part(self, o, shift, piece):
        at = self.at
        first = (at.fsdp(shift) * at.n_c + piece) * self.height
        return self.full.at[at.other(o), :, pl.ds(first, self.height), :]

    def copy(self, part, k, piece, peer):
        k = k * self.at.n_c + piece
        return remote(part, part, self.send.at[k], self.recv.at[k], peer)

    def own(self, piece):
        at = self.at
        return [
            *(self.copy(self.part(0, 0, piece), s, piece, at.xy(s, 0)) for s in range(1, at.n_f)),
            self.copy(self.part(0, 0, piece), 0, piece, at.xy(0, 1)),
        ]

    def passes(self, piece):
        at = self.at
        n = at.n_f
        if piece < at.n_c // 2:
            return [self.copy(self.part(0, -s, piece), n + s, piece, at.xy(0, 1)) for s in range(1, n)]
        return [self.copy(self.part(1, 0, piece), n + s, piece, at.xy(s, 0)) for s in range(1, n)]

    def start(self, piece):
        for copy in self.own(piece):
            copy.start()

    def forward(self, piece):
        own = self.own(piece)
        for copy in own[:-1] if piece < self.at.n_c // 2 else own[-1:]:
            copy.wait_recv()
        for copy in self.passes(piece):
            copy.start()

    def wait(self):
        for piece in range(self.at.n_c):
            own = self.own(piece)
            for copy in own[-1:] if piece < self.at.n_c // 2 else own[:-1]:
                copy.wait_recv()
            for copy in own:
                copy.wait_send()
            for copy in self.passes(piece):
                copy.wait()


class Collect:
    def __init__(self, at, partial, local, by_x, by_y, pass_x, pass_y, send, recv):
        self.at, self.partial, self.local = at, partial, local
        self.by_x, self.by_y, self.pass_x, self.pass_y = by_x, by_y, pass_x, pass_y
        self.send, self.recv = send, recv
        self.matrices = by_y.shape[0]
        self.height = partial.shape[2] // at.n_f // 2

    def first(self, shift, half):
        return (self.at.fsdp(shift) * 2 + half) * self.height

    def part(self, o, shift, half, m):
        rows = pl.ds(self.first(shift, half), self.height)
        return self.partial.at[self.at.other(o), m, rows, :]

    def half(self, ref, half, m):
        return ref.at[m, pl.ds(half * self.height, self.height), :]

    def copy(self, src, dst, k, m, peer):
        k = k * self.matrices + m
        return remote(src, dst, self.send.at[k], self.recv.at[k], peer)

    def raw(self, group, m):
        at = self.at
        n, shifts = at.n_f, range(1, at.n_f)
        if group == 0:
            return [
                self.copy(self.part(1, s, 0, m), self.pass_x.at[s - 1, m], s, m, at.xy(s, 0)) for s in shifts
            ]
        if group == 1:
            return [
                self.copy(self.part(1, s, 1, m), self.pass_y.at[s - 1, m], n + s, m, at.xy(0, 1))
                for s in shifts
            ]
        return [
            *(
                self.copy(
                    self.part(0, s, 0, m), self.half(self.by_x.at[s - 1], 0, m), 2 * n + s, m, at.xy(s, 0)
                )
                for s in shifts
            ),
            self.copy(self.part(1, 0, 1, m), self.half(self.by_y, 1, m), 0, m, at.xy(0, 1)),
        ]

    def added(self, s, m):
        at = self.at
        if s == 0:
            return self.copy(self.pass_x.at[0, m], self.half(self.by_y, 0, m), at.n_f, m, at.xy(0, 1))
        target = self.half(self.by_x.at[s - 1], 1, m)
        return self.copy(self.pass_y.at[s - 1, m], target, 3 * at.n_f + s, m, at.xy(s, 0))

    def start(self, m):
        for group in range(3):
            for copy in self.raw(group, m):
                copy.start()

    def load(self, o, shift, half, m, stage, k):
        return pltpu.make_async_copy(self.part(o, shift, half, m), stage, self.local.at[k])

    def fetch(self, m, stages):
        self.load(1, 0, 0, m, stages[0], 0).start()
        self.load(0, 1, 1, m, stages[1], 1).start()

    def fetch_own(self, m, stages):
        for half in range(2):
            self.load(0, 0, half, m, stages[half], 2 + 2 * m + half).start()

    def reader(self, o, shift, half, m, stage):
        if stage is None:
            first = self.first(shift, half)
            return lambda rows, start: self.partial[
                self.at.other(o), m, pl.ds(pl.multiple_of(first + start, STEP_ROWS), STEP_ROWS)
            ]
        return lambda rows, start: stage[rows]

    def sweep(self, step):
        @pl.loop(0, self.height // STEP_ROWS)
        def _(i):
            start = pl.multiple_of(i * STEP_ROWS, STEP_ROWS)
            step(pl.ds(start, STEP_ROWS), start)

    def forward(self, m, stages=(None, None)):
        n = self.at.n_f
        for copy in self.raw(0, m):
            copy.wait_recv()
        if stages[0] is not None:
            self.load(1, 0, 0, m, stages[0], 0).wait()
        own = self.reader(1, 0, 0, m, stages[0])

        def add_y(rows, start):
            value = own(rows, start).astype(F32)
            for s in range(n - 1):
                value = value + self.pass_x[s, m, rows].astype(F32)
            self.pass_x[0, m, rows] = value.astype(BF)

        self.sweep(add_y)
        self.added(0, m).start()
        for s in range(1, n):
            if stages[1] is not None:
                load = self.load(0, s, 1, m, stages[1], 1)
                if s > 1:
                    load.start()
                load.wait()
            own_x = self.reader(0, s, 1, m, stages[1])
            self.raw(1, m)[s - 1].wait_recv()

            def add_x(rows, start, s=s, own_x=own_x):
                value = own_x(rows, start).astype(F32) + self.pass_y[s - 1, m, rows].astype(F32)
                self.pass_y[s - 1, m, rows] = value.astype(BF)

            self.sweep(add_x)
            self.added(s, m).start()

    def total(self, m, squares, stages=(None, None)):
        n = self.at.n_f
        for copy in self.raw(2, m):
            copy.wait_recv()
        for s in range(n):
            self.added(s, m).wait_recv()
        for half in range(2):
            if stages[half] is not None:
                self.load(0, 0, half, m, stages[half], 2 + 2 * m + half).wait()
            own = self.reader(0, 0, half, m, stages[half])

            def add(rows, start, half=half, own=own):
                here = pl.ds(pl.multiple_of(half * self.height + start, STEP_ROWS), STEP_ROWS)
                value = own(rows, start).astype(F32) + self.by_y[m, here].astype(F32)
                for s in range(n - 1):
                    value = value + self.by_x[s, m, here].astype(F32)
                rounded = value.astype(BF)
                self.by_y[m, here] = rounded
                value = rounded.astype(F32)
                value = value * value
                tall = squares.shape[1]
                rows = value[:tall]
                for r in range(tall, value.shape[0], tall):
                    rows = rows + value[r : r + tall]
                wide = squares.shape[2]
                lanes = rows[:, :wide]
                for c in range(wide, value.shape[1], wide):
                    lanes = lanes + rows[:, c : c + wide]
                squares[0] += lanes

            self.sweep(add)

    def finish(self):
        for m in range(self.matrices):
            for group in range(3):
                for copy in self.raw(group, m):
                    copy.wait_send()
            for s in range(self.at.n_f):
                self.added(s, m).wait_send()


class Share:
    def __init__(self, at, src, out, send, recv, local):
        self.at, self.local = at, pltpu.make_async_copy(src, out.at[at.t], local)
        across = at.t + 2 - 4 * at.hi
        self.first = [
            remote(src, out.at[at.t], send.at[0], recv.at[0], at.xy(0, 1)),
            remote(src, out.at[at.t], send.at[1], recv.at[1], at.core),
        ]
        self.second = remote(out.at[across], out.at[across], send.at[2], recv.at[2], at.core)

    def start(self):
        for copy in (*self.first, self.local):
            copy.start()

    def forward(self):
        self.first[0].wait_recv()
        self.second.start()

    def finish(self):
        self.first[0].wait_send()
        self.first[1].wait()
        self.second.wait()
        self.local.wait()


def collect_scratch(n_f, matrices, height, columns):
    half = (matrices, height // 2, columns)
    return [
        pltpu.VMEM((n_f - 1, matrices, height, columns), BF),
        pltpu.VMEM((matrices, height, columns), BF),
        pltpu.VMEM((n_f - 1, *half), BF),
        pltpu.VMEM((n_f - 1, *half), BF),
        dma(4 * n_f * matrices),
        dma(4 * n_f * matrices),
    ]


class Return:
    def __init__(self, at, summed, shard, send, recv, local):
        rows, sheets = shard.shape[1], summed.shape[0]
        beside = shard.shape[0] // sheets
        width = summed.shape[2] // beside
        self.copies = []
        for m in range(shard.shape[0]):
            target = shard.at[m, :, pl.ds(pl.multiple_of(at.c * width, 128), width)]
            first = m % beside * width

            def part(c, m=m, first=first):
                here = pl.ds(pl.multiple_of(c * rows, rows), rows)
                return summed.at[m // beside, here, first : first + width]

            copies = []
            for s in range(1, at.n_c):
                k = m * at.n_c + s
                copies.append(remote(part(at.ctx(s)), target, send.at[k], recv.at[k], at.z(s)))
            copies.append(pltpu.make_async_copy(part(at.c), target, local.at[m]))
            self.copies.append(copies)

    def start(self, m):
        for copy in self.copies[m]:
            copy.start()

    def wait(self):
        for copies in self.copies:
            for copy in copies:
                copy.wait()


def pack_weights(w, packed):
    heads = w.shape[0]
    for i in range(4):
        for y in range(heads):
            k = (i * heads + y) * HEAD_DIM
            packed[:, k : k + HEAD_DIM] = w[y, i]


def turn(values, cos, sine):
    return values * cos + pltpu.roll(values, HEAD_DIM // 2, 1) * sine


def recast(wide, low):
    for m in range(wide.shape[0]):

        def step(rows, m=m):
            low[m, rows] = wide[m, rows].astype(low.dtype)

        by_rows(wide.shape[1], step)


def dma(count):
    return pltpu.SemaphoreType.DMA((count,))


def make_shards(mesh):
    sizes = tuple(mesh.shape[a] for a in ("fsdp", "ctx", "tp"))
    n_f, n_c, n_t = sizes

    def call(kernel, name, collective, outs, ins, out_specs, scratch, aliases=None, vmem=40):
        return pl.pallas_call(
            kernel,
            out_shape=outs,
            in_specs=ins,
            out_specs=out_specs,
            scratch_shapes=scratch,
            input_output_aliases=aliases or {},
            compiler_params=pltpu.CompilerParams(
                collective_id=collective, has_side_effects=True, vmem_limit_bytes=vmem << 20
            ),
            name=name,
        )

    def local(kernel, name, outs, scratch):
        return pl.pallas_call(
            kernel,
            out_shape=outs,
            scratch_shapes=scratch,
            compiler_params=pltpu.CompilerParams(vmem_limit_bytes=60 << 20),
            name=name,
        )

    def front_kernel(
        tok_ref, cot_ref, spots, key_place, cos, sine, att_ref, out_ref, ffp_ref, ffo_ref,
        rows_ref, attw_ref, ffw_ref, a2_ref, cots_ref, qkv, attended, mass, mid_ref,
        x_ref, own_cot, att_wide, ff_wide, att_low, ff_low, low, a1, packed, lk, lp,
        part, near, sent, got, ss, sr, g1, h1, l1, g2, h2, l2, g3, h3, l3, s4, r4, l4, s5, r5, l5, s6, r6, s7, r7,
    ):
        at = Place(sizes)
        half = x_ref.shape[0]
        mine = pl.ds(pl.multiple_of(at.lo * half, half), half)
        loads = [
            pltpu.make_async_copy(tok_ref.at[at.hi, mine], x_ref, lk.at[0]),
            pltpu.make_async_copy(att_ref, att_wide.at[pl.ds(0, 3)], lk.at[1]),
            pltpu.make_async_copy(out_ref, att_wide.at[3], lk.at[2]),
            pltpu.make_async_copy(ffp_ref, ff_wide.at[pl.ds(0, 2)], lk.at[3]),
            pltpu.make_async_copy(ffo_ref, ff_wide.at[2], lk.at[4]),
            pltpu.make_async_copy(cot_ref.at[at.hi, mine], own_cot, lk.at[5]),
        ]
        for copy in loads:
            copy.start()
        scatter = Scatter(at, part, near, sent, got, ss, sr)
        gather = Gather(at, low, rows_ref, g1, h1, l1)
        cots = Gather(at, own_cot, cots_ref, g2, h2, l2)
        a2 = Gather(at, low, a2_ref, g3, h3, l3)
        swap_att = Swap(at, att_low, attw_ref, s4, r4, l4)
        swap_ff = Swap(at, ff_low, ffw_ref, s5, r5, l5)
        spread_att = Spread(at, attw_ref, s6, r6)
        spread_ff = Spread(at, ffw_ref, s7, r7)
        loads[0].wait()

        def norm_one(rows):
            low[rows] = mean_spread(x_ref[rows].astype(F32))[0].astype(BF)

        by_rows(half, norm_one)
        loads[1].wait()
        loads[2].wait()
        recast(att_wide, att_low)
        at.greet([at.core, *at.all_z(), *at.all_xy()])
        swap_att.start()
        gather.start()
        spread_att.start(swap_att.arrived(0))
        for copy in loads[3:]:
            copy.wait()
        recast(ff_wide, ff_low)
        gather.forward(range(1, 2))
        behind = [s for pair in zip(range(1, n_c), range(n_c - 1, 0, -1)) for s in pair][: n_c - 1]
        spread_att.start(swap_att.arrived(behind[0]))
        spread_att.start(swap_att.arrived(behind[1]))
        gather.forward(range(2, n_c - 1))
        swap_ff.start()
        for s in behind[2:]:
            spread_att.start(swap_att.arrived(s))
        gather.forward(range(n_c - 1, n_c))
        for piece in range(n_c):
            spread_att.forward(piece)
        spread_ff.start(swap_ff.arrived(0))
        gather.finish()
        take = [pltpu.make_async_copy(rows_ref.at[b], a1.at[pl.ds(b * half, half)], lp.at[b]) for b in range(2 * n_c)]
        for copy in take:
            copy.start()
        spread_att.wait()
        heads = attw_ref.shape[0]
        packs = [
            pltpu.make_async_copy(
                attw_ref.at[y, i],
                packed.at[:, pl.ds((i * heads + y) * HEAD_DIM, HEAD_DIM)],
                lp.at[2 * n_c + i * heads + y],
            )
            for i in range(4)
            for y in range(heads)
        ]
        for copy in packs:
            copy.start()
        for copy in (*take, *packs):
            copy.wait()
        attend(a1, packed, spots, key_place, cos, sine, qkv, attended, mass, part)
        scatter.start()
        cots.start()
        scatter.pass_on(range(n_c - 1, n_c - 2, -1))
        spread_ff.start(swap_ff.arrived(behind[0]))
        spread_ff.start(swap_ff.arrived(behind[1]))
        cots.forward(range(1, 2))
        scatter.pass_on(range(n_c - 2, 1, -1))
        for s in behind[2:]:
            spread_ff.start(swap_ff.arrived(s))
        cots.forward(range(2, 3))
        scatter.pass_on(range(1, 2))
        spread_ff.forward(0)
        scatter.arrive()

        def norm_two(rows):
            mid = x_ref[rows].astype(F32) + scatter.total(rows)
            mid_ref[rows] = mid
            low[rows] = mean_spread(mid)[0].astype(BF)

        by_rows(half, norm_two)
        a2.start()
        a2.forward(range(1, 2))
        spread_ff.forward(n_c - 1)
        a2.forward(range(2, 3))
        for piece in range(1, n_c - 1):
            spread_ff.forward(piece)
        a2.forward(range(3, n_c))
        cots.forward(range(3, n_c))
        cots.finish()
        a2.finish()
        scatter.finish()
        swap_att.finish()
        swap_ff.finish()
        spread_ff.wait()

    def back_kernel(
        a2_ref, cots_ref, joined_ref, d_a2_ref, ffw_ref, mid_ref, tok_ref, cot_ref, a1_ref, attw_ref,
        spots, key_place, cos, sine, qkv, attended, mass,
        input_ref, out_ref, attg_ref, ffg_ref, norm_ref, grad_ref, rows_ref,
        rows_one, rows_two, wide, sheets, d_v, d_k, own, block, low, lk, lg, credit,
        part, near, sent, got, ss, sr, near2, sent2, got2, ss2, sr2, g1, h1, l1, lf, s4, r4, l4, s5, r5, l5, s6, r6, l6,
        total, got_p, got_c, s7, r7, *collected,
    ):
        at = Place(sizes)
        half = own.shape[0]
        length, tall = 2 * n_c * half, wide.shape[1]
        mine = pl.ds(pl.multiple_of(at.lo * half, half), half)

        def load(*pairs):
            copies = [pltpu.make_async_copy(src, dst, lk.at[i]) for i, (src, dst) in enumerate(pairs)]
            for copy in copies:
                copy.start()
            for copy in copies:
                copy.wait()

        def flat(ref, cols=slice(None)):
            value = ref[:, :, cols]
            return value.reshape(length, value.shape[2])

        scatter = Scatter(at, part, near, sent, got, ss, sr)
        branch = Scatter(at, rows_one, near2, sent2, got2, ss2, sr2)
        gather = Gather(at, low, rows_ref, g1, h1, l1)
        columns = sheets.shape[3]
        high = tall // n_f // 2
        early = [wide.at[1, pl.ds(length, high), pl.ds(i * columns, columns)] for i in range(2)]
        late = [
            [sheets.at[m % 2, 0, pl.ds((m // 2 * 2 + i) * high, high)] for i in range(2)] for m in range(3)
        ]
        collect_ff = Collect(at, grad_ref, lf, *collected[:6])
        collect_att = Collect(at, sheets, None, *collected[6:])
        give_ff = Return(at, collected[1], ffg_ref, s5, r5, l5)
        give_att = Return(at, collected[7], attg_ref, s4, r4, l4)
        total[0] = jnp.zeros(total.shape[1:], F32)
        at.greet([*plane(at), *at.all_z()])
        load((d_a2_ref, part))
        scatter.start()
        load(
            (a2_ref, rows_one),
            (cots_ref, rows_two),
            (joined_ref.at[0], wide.at[0, pl.ds(0, length)]),
            (joined_ref.at[1], wide.at[0, pl.ds(length, length)]),
            (joined_ref.at[2], wide.at[1, pl.ds(0, length)]),
            (cot_ref.at[at.hi, mine], block),
        )

        def keep(k):
            y, m = k % 2, k // 2
            return pltpu.make_async_copy(sheets.at[y, 0], grad_ref.at[y, m], lg.at[y])

        for k in range(6):
            y, m = k % 2, k // 2
            if k >= 2 and y == 0:
                keep(k - 2).wait()
                keep(k - 1).wait()
            rows = rows_two if m == 2 else rows_one
            slot, start = ((0, 0), (0, length), (1, 0))[m]

            @pl.loop(0, 2)
            def _(i, y=y, rows=rows, slot=slot, start=start):
                cols = pl.ds(pl.multiple_of(i * (tall // 2), tall // 2), tall // 2)
                side = wide[slot, start : start + length, y * columns : (y + 1) * columns]
                sheets[y, 0, cols] = dot(flat(rows, cols), side, ((0,), (0,))).astype(BF)

            keep(k).start()
            if k == 0:
                scatter.pass_on(range(n_c - 1, n_c - 2, -1))
            if k == 2:
                collect_ff.start(0)
            if k == 3:
                scatter.pass_on(range(n_c - 2, 1, -1))
            if k == 4:
                collect_ff.start(1)
        keep(4).wait()
        keep(5).wait()
        collect_ff.start(2)
        collect_ff.fetch(0, early)
        scatter.pass_on(range(1, 2))
        scatter.arrive()

        def norm_two(rows):
            normed, scale = mean_spread(mid_ref[rows])
            grad = block[rows].astype(F32) + norm_back(scatter.total(rows), normed, scale)
            own[rows] = grad
            low[rows] = grad.astype(BF)

        by_rows(half, norm_two)
        gather.start()
        heads = attw_ref.shape[0]
        scatter.finish()
        scatter.free(credit.at[0])
        width = part.shape[2] // 4
        gather.forward(range(1, 2))
        collect_ff.forward(0, early)
        collect_ff.fetch(1, early)
        gather.forward(range(2, n_c - 1))
        collect_ff.forward(1, early)
        collect_ff.fetch(2, early)
        for m in range(3):
            collect_ff.fetch_own(m, late[m])
        collect_ff.forward(2, early)
        gather.forward(range(n_c - 1, n_c))
        load(
            (a1_ref, rows_two),
            *(
                (attw_ref.at[y, i], wide.at[0, :, pl.ds((i * heads + y) * HEAD_DIM, HEAD_DIM)])
                for i in range(4)
                for y in range(heads)
            ),
        )
        gather.finish()
        load((rows_ref, rows_one), (tok_ref.at[at.hi, mine], low))
        packed, joint = wide.at[0], wide.at[1, pl.ds(length, length)]
        wide_heads = heads * HEAD_DIM
        joint[:, :wide_heads] = dot(flat(rows_one), packed[:, 3 * wide_heads :], ((1,), (0,))).astype(BF)
        collect_ff.total(0, total, late[0])
        give_ff.start(0)
        for y in range(heads):
            attend_back(y, packed, joint, spots, key_place, cos, sine, qkv, mass, d_v, d_k, heads)
            if y == 0:
                collect_ff.total(1, total, late[1])
                give_ff.start(1)

        @pl.loop(0, 4)
        def _(c):
            cols = pl.ds(pl.multiple_of(c * width, width), width)
            value = dot(joint[:, : 3 * wide_heads], packed[cols, : 3 * wide_heads], ((1,), (1,))).astype(BF)
            part[:, :, cols] = value.reshape(part.shape[0], part.shape[1], width)

        scatter.start()
        collect_ff.total(2, total, late[2])

        @pl.loop(0, 2)
        def _(c):
            cols = pl.ds(pl.multiple_of(c * 2 * width, width), 2 * width)
            for i in range(4):
                if i < 3:
                    value = dot(
                        flat(rows_two, cols), joint[:, i * wide_heads : (i + 1) * wide_heads], ((0,), (0,))
                    )
                else:
                    value = dot(flat(rows_one, cols), attended[...], ((0,), (0,)))
                for y in range(heads):
                    sheets[y, 0, cols, i * HEAD_DIM : (i + 1) * HEAD_DIM] = value[
                        :, y * HEAD_DIM : (y + 1) * HEAD_DIM
                    ].astype(BF)

        collect_att.start(0)
        scatter.pass_on(range(n_c - 1, n_c - 2, -1))
        give_ff.start(2)
        load(*((ffw_ref.at[y, 2], wide.at[0, :, pl.ds(y * columns, columns)]) for y in range(heads)))

        @pl.loop(0, 4)
        def _(c):
            cols = pl.ds(pl.multiple_of(c * width, width), width)
            value = dot(wide[1, :length], wide[0, cols], ((1,), (1,))).astype(BF)
            rows_one[:, :, cols] = value.reshape(rows_one.shape[0], rows_one.shape[1], width)

        branch.start()
        share_block = Share(at, block, out_ref, s6.at[0], r6.at[0], l6.at[0])
        share_input = Share(at, low, input_ref, s6.at[1], r6.at[1], l6.at[1])
        scatter.pass_on(range(n_c - 2, 1, -1))
        branch.pass_on(range(n_c - 1, n_c - 2, -1))
        collect_att.forward(0)
        scatter.pass_on(range(1, 2))
        branch.pass_on(range(n_c - 2, 1, -1))
        collect_att.total(0, total)
        for m in range(4):
            give_att.start(m)
        branch.pass_on(range(1, 2))
        scatter.arrive()

        def norm_one(rows):
            normed, scale = mean_spread(low[rows].astype(F32))
            low[rows] = (own[rows] + norm_back(scatter.total(rows), normed, scale)).astype(BF)

        by_rows(half, norm_one)
        share_input.start()
        branch.arrive()

        def add(rows):
            block[rows] = (mid_ref[rows] + branch.total(rows)).astype(BF)

        by_rows(half, add)
        share_block.start()
        scatter.finish()
        branch.finish()
        collect_ff.finish()
        collect_att.finish()
        share_input.forward()
        share_block.forward()
        sum_norm(at, norm_ref, total, got_p, got_c, s7, r7)
        give_ff.wait()
        give_att.wait()
        share_block.finish()
        share_input.finish()

    def plane(at):
        count = n_f * n_t
        here = at.f * n_t + at.t
        others = [lax.rem(here + i, count) for i in range(1, count)]
        return [(i // n_t, at.c, lax.rem(i, n_t)) for i in others]

    def sum_norm(at, norm_ref, total, got_p, got_c, send, recv):
        base = 0
        stages = ((plane(at), got_p, at.f * n_t + at.t), (at.all_z(), got_c, at.c))
        for stage, (peers, got, place) in enumerate(stages):
            copies = [
                remote(total.at[stage], got.at[place], send.at[base + i], recv.at[base + i], peer)
                for i, peer in enumerate(peers)
            ]
            base += len(peers)
            for copy in copies:
                copy.start()
            got[place] = total[stage]
            for copy in copies:
                copy.wait()
            value = got[0]
            for i in range(1, got.shape[0]):
                value = value + got[i]
            total[stage + 1] = value
        norm = jnp.sqrt(jnp.sum(total[2], axis=(0, 1), keepdims=True))
        norm_ref[...] = jnp.broadcast_to(norm, norm_ref.shape)

    def finish_kernel(norm_ref, block_in, input_in, attg_ref, ffg_ref, *refs):
        olds, outs, scratch = refs[:12], refs[12:34], refs[34:]
        low_att, low_ff, wide_att, wide_ff, old_att, old_ff, block_keep, input_low, input_keep, ls = scratch
        groups = (
            (attg_ref, low_att, wide_att, old_att, 0, attg_ref.shape[1]),
            (ffg_ref, low_ff, wide_ff, old_ff, 2, attg_ref.shape[1] // 4),
        )
        chunks = [
            (group, m, r)
            for group in groups
            for m in range(group[0].shape[0])
            for r in range(group[0].shape[1] // group[5])
        ]

        def sheet(array, first, m, group):
            last = group[0].shape[0] - 1
            return array[first + 1] if m == last else array[first].at[m]

        loads, stores = [], []
        for i, (group, m, r) in enumerate(chunks):
            here = pl.ds(r * group[5], group[5])
            one = [pltpu.make_async_copy(group[0].at[m, here], group[1].at[m, here], ls.at[i, 0, 3])]
            one += [
                pltpu.make_async_copy(
                    sheet(olds, 4 * j + group[4], m, group).at[here], group[3].at[j, m, here], ls.at[i, 0, j]
                )
                for j in range(3)
            ]
            for copy in one:
                copy.start()
            loads.append(one)
        kept = ((block_in, block_keep, block_keep, outs[20]), (input_in, input_low, input_keep, outs[21]))
        through = []
        for i, (src, first, keep, out) in enumerate(kept):
            copy = pltpu.make_async_copy(src, first, ls.at[len(chunks), 0, i])
            copy.start()
            through.append((copy, pltpu.make_async_copy(keep, out, ls.at[len(chunks), 1, i])))
        norm = norm_ref[0:1, 0:1]
        clip = jnp.minimum(1.0, MAX_NORM / (norm + 1e-06))
        width = ffg_ref.shape[1] * n_f * n_c
        for i, (group, m, r) in enumerate(chunks):
            for copy in loads[i]:
                copy.wait()
            low, wide, old = group[1:4]
            rate = (width // 32) ** (-0.5) if group[4] == 0 and m == 3 else width ** (-0.5)

            @pl.loop(0, group[5] // ROWS)
            def _(k, low=low, wide=wide, old=old, m=m, r=r, step=group[5], rate=rate):
                rows = pl.ds(pl.multiple_of(r * step + k * ROWS, ROWS), ROWS)
                grad = low[m, rows].astype(F32)
                wide[m, rows] = grad
                first_new, second_new, weight_new = adam_step(
                    old[0, m, rows], grad, old[1, m, rows], old[2, m, rows], clip, rate
                )
                old[0, m, rows] = weight_new
                old[1, m, rows] = first_new
                old[2, m, rows] = second_new
                low[m, rows] = weight_new.astype(BF)

            here = pl.ds(r * group[5], group[5])
            for k, (src, out) in enumerate(
                ((wide, 0), (old.at[1], 4), (old.at[2], 8), (old.at[0], 12), (low, 16))
            ):
                store = pltpu.make_async_copy(
                    src.at[m, here], sheet(outs, out + group[4], m, group).at[here], ls.at[i, 1, k]
                )
                store.start()
                stores.append(store)
        for load, store in through:
            load.wait()
            if load is through[1][0]:
                recast(input_low, input_keep)
            store.start()
            stores.append(store)
        for store in stores:
            store.wait()

    def attend(a1, packed, spots, key_place, cos, sine, qkv, attended, mass, part):
        wide = attended.shape[1]
        heads = wide // HEAD_DIM
        for i in range(3):
            joint = dot(a1[...], packed[:, i * wide : (i + 1) * wide], ((1,), (0,)))
            for y in range(heads):
                cols = slice(y * HEAD_DIM, (y + 1) * HEAD_DIM)
                head = joint[:, cols]
                if i < 2:
                    head = turn(head, cos[...], sine[...])
                qkv[i, :, cols] = head.astype(BF)
        for y in range(heads):
            cols = slice(y * HEAD_DIM, (y + 1) * HEAD_DIM)

            @pl.loop(0, a1.shape[0] // QUERIES)
            def _(c, y=y, cols=cols):
                rows = pl.ds(pl.multiple_of(c * QUERIES, QUERIES), QUERIES)
                scores = dot(qkv[0, rows, cols], qkv[1, :, cols], ((1,), (1,))) * SCORE_SCALE
                allowed = (key_place[...] <= spots[rows, 0:1]) & (key_place[...] >= spots[rows, 1:2])
                scores = jnp.where(allowed, scores, NEG_FILL)
                peak = jnp.max(scores, axis=1, keepdims=True)
                exp_scores = jnp.exp(scores - peak)
                total = jnp.sum(exp_scores, axis=1, keepdims=True)
                probs = (exp_scores * (1.0 / total)).astype(BF)
                attended[rows, cols] = dot(probs, qkv[2, :, cols], ((1,), (0,))).astype(BF)
                mass[rows, y : y + 1] = peak + jnp.log(total)

        width = part.shape[2] // 4

        @pl.loop(0, 4)
        def _(c):
            cols = pl.ds(pl.multiple_of(c * width, width), width)
            value = dot(attended[...], packed[cols, 3 * wide :], ((1,), (1,))).astype(BF)
            part[:, :, cols] = value.reshape(part.shape[0], part.shape[1], width)

    def attend_back(y, packed, joint, spots, key_place, cos, sine, qkv, mass, d_v, d_k, heads):
        wide = heads * HEAD_DIM
        cols = slice(y * HEAD_DIM, (y + 1) * HEAD_DIM)

        @pl.loop(0, qkv.shape[1] // QUERIES)
        def _(c):
            rows = pl.ds(pl.multiple_of(c * QUERIES, QUERIES), QUERIES)
            query, key, value = qkv[0, rows, cols], qkv[1, :, cols], qkv[2, :, cols]
            d_att = joint[rows, cols]
            scores = dot(query, key, ((1,), (1,))) * SCORE_SCALE
            allowed = (key_place[...] <= spots[rows, 0:1]) & (key_place[...] >= spots[rows, 1:2])
            probs = jnp.exp(jnp.where(allowed, scores, NEG_FILL) - mass[rows, y : y + 1])
            d_prob = dot(d_att, value, ((1,), (1,)))
            delta = jnp.sum(probs * d_prob, axis=1, keepdims=True)
            d_score = (probs * (d_prob - delta)).astype(BF)
            v_part = dot(probs.astype(BF), d_att, ((0,), (0,)))
            k_part = dot(d_score, query, ((0,), (0,)))

            @pl.when(c == 0)
            def _():
                d_v[...] = v_part
                d_k[...] = k_part

            @pl.when(c > 0)
            def _():
                d_v[...] += v_part
                d_k[...] += k_part

            d_query = dot(d_score, key, ((1,), (0,))) * SCORE_SCALE
            joint[rows, cols] = turn(d_query, cos[rows], -sine[rows]).astype(BF)

        joint[:, wide + y * HEAD_DIM : wide + (y + 1) * HEAD_DIM] = turn(
            d_k[...] * SCORE_SCALE, cos[...], -sine[...]
        ).astype(BF)
        joint[:, 2 * wide + y * HEAD_DIM : 2 * wide + (y + 1) * HEAD_DIM] = d_v[...].astype(BF)

    def hidden_kernel(a2, cot, w, d_a2, joined, kept):
        d_up, d_gate, hidden = joined.at[0], joined.at[1], joined.at[2]
        step, steps = pl.program_id(0), pl.num_programs(0)
        tile = w.shape[3]
        here = pl.ds(pl.multiple_of(step * tile, tile), tile)
        length, width = a2.shape
        chunk = length // 2

        @pl.loop(0, 2)
        def _(i):
            rows = pl.ds(pl.multiple_of(i * chunk, chunk), chunk)
            up = dot(a2[rows], w[0, 0], ((1,), (0,)))
            gate = dot(a2[rows], w[0, 1], ((1,), (0,)))
            d_hid = dot(cot[rows], w[0, 2], ((1,), (0,)))
            sigma = jax.nn.sigmoid(gate)
            act = gate * sigma
            hidden[rows, here] = (act * up).astype(BF)
            d_up[rows, here] = (d_hid * act).astype(BF)
            d_gate[rows, here] = (d_hid * up * sigma * (1.0 + gate * (1.0 - sigma))).astype(BF)

        for m in range(2):
            kept[m, :, here] = w[0, m]

        @pl.when(step == steps - 1)
        def _():
            @pl.loop(0, 8)
            def _(i):
                cols = pl.ds(pl.multiple_of(i * (width // 8), width // 8), width // 8)
                d_a2[:, cols] = (
                    dot(d_up[...], kept[0, cols], ((1,), (1,)))
                    + dot(d_gate[...], kept[1, cols], ((1,), (1,)))
                ).astype(BF)

    def shards(
        tokens,
        cotangent,
        lengths,
        deal,
        att_proj,
        attn_out,
        ff_proj,
        ff_out,
        att_proj_first,
        attn_out_first,
        ff_proj_first,
        ff_out_first,
        att_proj_second,
        attn_out_second,
        ff_proj_second,
        ff_out_second,
    ):
        t_at = lax.axis_index("tp")
        pack_at = t_at // 2
        packs, row_count, width = tokens.shape
        half = row_count // 2
        pack_len = deal.shape[1]
        blocks = n_c * 2
        rows_bf = jax.ShapeDtypeStruct((blocks, half, width), BF)
        own_f32 = jax.ShapeDtypeStruct((half, width), F32)

        att_cols, ff_cols = att_proj.shape[2] // n_c, ff_proj.shape[2] // n_c
        att_shape, ff_shape = (4, *att_proj.shape[1:]), (3, *ff_proj.shape[1:])
        att_full = jax.ShapeDtypeStruct((2, 4, width, att_cols), BF)
        ff_full = jax.ShapeDtypeStruct((2, 3, width, ff_cols), BF)
        places = lax.dynamic_index_in_dim(deal, pack_at, 0, keepdims=False)
        length_row = lax.dynamic_index_in_dim(lengths, pack_at, 0, keepdims=False)
        seqs = lengths.shape[1]
        before = jnp.arange(seqs)[:, None] > jnp.arange(seqs)[None, :]
        starts = jnp.sum(jnp.where(before, length_row[None, :], 0), axis=1)
        inside = (places[:, None] >= starts[None, :]) & (
            places[:, None] < (starts + length_row)[None, :]
        )
        firsts = jnp.sum(jnp.where(inside, starts[None, :], 0), axis=1)
        freq_steps = jnp.arange(HEAD_DIM // 2, dtype=F32)
        inverse = jnp.power(10000.0, -2.0 * freq_steps / HEAD_DIM)
        angles = (places - firsts).astype(F32)[:, None] * inverse[None, :]
        cos_table, sine_table = jnp.cos(angles), jnp.sin(angles)
        tables = (
            jnp.stack([places, firsts], axis=1),
            places[None, :],
            jnp.concatenate([cos_table, cos_table], axis=1),
            jnp.concatenate([-sine_table, sine_table], axis=1),
        )
        rank_width = 2 * att_cols
        act_one, att_w, ff_w, act_two, cot_rows, qkv, attended, mass, resid_mid = call(
            front_kernel,
            "front",
            0,
            (
                rows_bf,
                att_full,
                ff_full,
                rows_bf,
                rows_bf,
                jax.ShapeDtypeStruct((3, pack_len, rank_width), BF),
                jax.ShapeDtypeStruct((pack_len, rank_width), BF),
                jax.ShapeDtypeStruct((pack_len, 2), F32),
                own_f32,
            ),
            [ANY, ANY] + [VMEM] * 4 + [ANY] * 4,
            (ANY,) * 5 + (VMEM,) * 4,
            [
                pltpu.VMEM((half, width), BF),
                pltpu.VMEM((half, width), BF),
                pltpu.VMEM(att_shape, F32),
                pltpu.VMEM(ff_shape, F32),
                pltpu.VMEM(att_shape, BF),
                pltpu.VMEM(ff_shape, BF),
                pltpu.VMEM((half, width), BF),
                pltpu.VMEM((pack_len, width), BF),
                pltpu.VMEM((width, 4 * rank_width), BF),
                dma(6),
                dma(2 * n_c + 8),
            ]
            + scatter_scratch(n_c, half, width)
            + gather_sems(n_c) * 3
            + [dma(n_c), dma(n_c), pltpu.SemaphoreType.DMA] * 2
            + [dma(2 * n_f * n_c)] * 4,
            vmem=56,
        )(tokens, cotangent, *tables, att_proj, attn_out, ff_proj, ff_out)
        act_two = act_two.reshape(pack_len, width)
        cot_rows = cot_rows.reshape(pack_len, width)

        tile = 256
        tiles = ff_cols // tile
        kept = pl.BlockSpec((pack_len, width), lambda i: (0, 0), pipeline_mode=pl.Buffered(1))
        moved = pl.BlockSpec((1, 3, width, tile), lambda i: (i // tiles, 0, 0, i % tiles))
        rows_flat = jax.ShapeDtypeStruct((pack_len, width), BF)
        act_two_part, joined = pl.pallas_call(
            hidden_kernel,
            grid=(2 * tiles,),
            out_shape=(rows_flat, jax.ShapeDtypeStruct((3, pack_len, 2 * ff_cols), BF)),
            in_specs=[kept, kept, moved],
            out_specs=(
                kept,
                pl.BlockSpec((3, pack_len, 2 * ff_cols), lambda i: (0, 0, 0), pipeline_mode=pl.Buffered(1)),
            ),
            scratch_shapes=[pltpu.VMEM((2, width, 2 * ff_cols), BF)],
            compiler_params=pltpu.CompilerParams(vmem_limit_bytes=60 << 20),
            name="hidden",
        )(act_two, cot_rows, ff_w)
        height = width // n_f
        count = n_f * n_t + n_c
        input_grad, block_out, att_total, ff_total, norm_value, *_ = call(
            back_kernel,
            "back",
            1,
            (
                jax.ShapeDtypeStruct((n_t, half, width), BF),
                jax.ShapeDtypeStruct((n_t, half, width), BF),
                jax.ShapeDtypeStruct(att_shape, BF),
                jax.ShapeDtypeStruct(ff_shape, BF),
                jax.ShapeDtypeStruct((8, 128), F32),
                ff_full,
                rows_bf,
            ),
            [ANY] * 5 + [VMEM] + [ANY] * 4 + [VMEM] * 7,
            (ANY,) * 4 + (VMEM,) + (ANY,) * 2,
            [
                pltpu.VMEM((2 * n_c, half, width), BF),
                pltpu.VMEM((2 * n_c, half, width), BF),
                pltpu.VMEM((2, width, 4 * rank_width), BF),
                pltpu.VMEM((2, 1, width, 4 * att_cols), BF),
                pltpu.VMEM((pack_len, HEAD_DIM), F32),
                pltpu.VMEM((pack_len, HEAD_DIM), F32),
                pltpu.VMEM((half, width), F32),
                pltpu.VMEM((half, width), BF),
                pltpu.VMEM((half, width), BF),
                dma(12),
                dma(2),
                pltpu.SemaphoreType.REGULAR((1, 3)),
            ]
            + scatter_scratch(n_c, half, width)
            + scatter_scratch(n_c, half, width)[1:]
            + gather_sems(n_c)
            + [dma(8)]
            + [dma(4 * n_c), dma(4 * n_c), dma(4), dma(3 * n_c), dma(3 * n_c), dma(3)]
            + [
                pltpu.SemaphoreType.DMA((2, 3)),
                pltpu.SemaphoreType.DMA((2, 3)),
                dma(2),
            ]
            + [pltpu.VMEM((k, 8, 128), F32) for k in (3, n_f * n_t, n_c)]
            + [dma(count), dma(count)]
            + collect_scratch(n_f, 3, height, ff_cols)
            + collect_scratch(n_f, 1, height, 4 * att_cols),
            vmem=62,
        )(
            act_two.reshape(rows_bf.shape), cot_rows.reshape(rows_bf.shape), joined, act_two_part.reshape(rows_bf.shape), ff_w,
            resid_mid, tokens, cotangent, act_one, att_w, *tables, qkv, attended, mass,
        )
        weights = (att_proj, attn_out, ff_proj, ff_out)
        firsts_old = (att_proj_first, attn_out_first, ff_proj_first, ff_out_first)
        seconds_old = (att_proj_second, attn_out_second, ff_proj_second, ff_out_second)
        results = pl.pallas_call(
            finish_kernel,
            out_shape=(
                *(jax.ShapeDtypeStruct(w.shape, F32) for w in weights * 4),
                *(jax.ShapeDtypeStruct(w.shape, BF) for w in weights),
                jax.ShapeDtypeStruct(block_out.shape, BF),
                jax.ShapeDtypeStruct(input_grad.shape, F32),
            ),
            in_specs=[VMEM] + [ANY] * 16,
            out_specs=(ANY,) * 22,
            scratch_shapes=[
                pltpu.VMEM(att_shape, BF),
                pltpu.VMEM(ff_shape, BF),
                pltpu.VMEM(att_shape, F32),
                pltpu.VMEM(ff_shape, F32),
                pltpu.VMEM((3, *att_shape), F32),
                pltpu.VMEM((3, *ff_shape), F32),
                pltpu.VMEM(block_out.shape, BF),
                pltpu.VMEM(input_grad.shape, BF),
                pltpu.VMEM(input_grad.shape, F32),
                pltpu.SemaphoreType.DMA((17, 2, 5)),
            ],
            compiler_params=pltpu.CompilerParams(vmem_limit_bytes=56 << 20),
            name="finish",
        )(norm_value, block_out, input_grad, att_total, ff_total, *weights, *firsts_old, *seconds_old)
        return (
            results[20].reshape(tokens.shape),
            results[21].reshape(tokens.shape),
            norm_value[0, :1],
            *results[:20],
        )

    return shards


def solution(mesh):
    act = P("fsdp", "ctx", None)
    table = P("fsdp", None)
    cube = P(None, ("fsdp", "ctx"), "tp")
    flat = P(("fsdp", "ctx"), "tp")
    group = (cube, flat, cube, flat)
    in_specs = (act, act, table, table) + group * 3
    out_specs = (act, act, P()) + group * 5
    return jax.shard_map(
        make_shards(mesh), mesh=mesh, in_specs=in_specs, out_specs=out_specs, check_vma=False
    )
```

```python
import functools

import jax
import jax.numpy as jnp
from jax import lax
from jax.experimental import pallas as pl
from jax.experimental.pallas import tpu as pltpu
from jax.sharding import PartitionSpec as P

HEAD_DIM = 128
STEP = 10
EPS_NORM = 1e-05
BETA_ONE = 0.9
BETA_TWO = 0.95
EPS_ADAM = 1e-08
DECAY = 0.1
MAX_NORM = 1.0
NEG_FILL = -1e30
BF = jnp.bfloat16
F32 = jnp.float32
MESH = pl.DeviceIdType.MESH
ANY = pl.BlockSpec(memory_space=pl.ANY)
VMEM = pl.BlockSpec(memory_space=pltpu.VMEM)
ROWS = 16
STEP_ROWS = 32
QUERIES = 256
SCORE_SCALE = HEAD_DIM ** (-0.5)


def mean_spread(values):
    centre = values - jnp.mean(values, axis=-1, keepdims=True)
    spread = jnp.mean(centre * centre, axis=-1, keepdims=True)
    scale = lax.rsqrt(spread + EPS_NORM)
    return centre * scale, scale


def norm_back(grad, normed, scale):
    return scale * (
        grad
        - jnp.mean(grad, axis=-1, keepdims=True)
        - normed * jnp.mean(grad * normed, axis=-1, keepdims=True)
    )


def dot(left, right, dims):
    return lax.dot_general(left, right, (dims, ((), ())), preferred_element_type=F32)


def adam_step(weight, grad_sum, first, second, clip_factor, learn_rate):
    clipped = grad_sum * clip_factor
    first_new = BETA_ONE * first + (1.0 - BETA_ONE) * clipped
    second_new = BETA_TWO * second + (1.0 - BETA_TWO) * clipped * clipped
    first_hat = first_new / (1.0 - BETA_ONE**STEP)
    second_hat = second_new / (1.0 - BETA_TWO**STEP)
    weight_new = weight - learn_rate * (
        first_hat / (jnp.sqrt(second_hat) + EPS_ADAM) + DECAY * weight
    )
    return (first_new, second_new, weight_new)


class Place:
    def __init__(self, sizes):
        self.n_f, self.n_c, self.n_t = sizes
        self.f, self.c, self.t = (lax.axis_index(a) for a in ("fsdp", "ctx", "tp"))
        self.hi, self.lo = self.t // 2, lax.rem(self.t, 2)
        self.core = (self.f, self.c, self.t + 1 - 2 * self.lo)
        self.block = self.c * 2 + self.lo
        self.pairs = [(s, o) for o in range(2) for s in range(self.n_f) if s or o]

    def ctx(self, shift):
        return lax.rem(self.c + shift + self.n_c, self.n_c)

    def fsdp(self, shift):
        return lax.rem(self.f + shift + self.n_f, self.n_f)

    def other(self, o):
        return self.hi + o * (1 - 2 * self.hi)

    def z(self, shift):
        return (self.f, self.ctx(shift), self.t)

    def xy(self, shift, o):
        return (self.fsdp(shift), self.c, self.t + o * (2 - 4 * self.hi))

    def greet(self, peers):
        barrier = pltpu.get_barrier_semaphore()
        for peer in peers:
            pl.semaphore_signal(barrier, inc=1, device_id=peer, device_id_type=MESH)
        pl.semaphore_wait(barrier, len(peers))

    def all_z(self):
        return [self.z(s) for s in range(1, self.n_c)]

    def all_xy(self):
        return [self.xy(s, o) for s, o in self.pairs]


def remote(src, dst, send, recv, peer):
    return pltpu.make_async_remote_copy(
        src_ref=src, dst_ref=dst, send_sem=send, recv_sem=recv, device_id=peer, device_id_type=MESH
    )


def by_rows(count, step):
    @pl.loop(0, count // ROWS)
    def _(i):
        step(pl.ds(pl.multiple_of(i * ROWS, ROWS), ROWS))


class Gather:
    def __init__(self, at, src, out, send, recv, local):
        self.at, self.src, self.out, self.send, self.recv = at, src, out, send, recv
        self.local = pltpu.make_async_copy(src, out.at[at.block], local)

    def far(self, way, hop, src=None):
        at = self.at
        block = self.out.at[jnp.clip(at.c - way * (hop - 1), 0, at.n_c - 1) * 2 + at.lo]
        k = hop + (0 if way > 0 else at.n_c)
        return remote(
            block if src is None else src, block, self.send.at[k], self.recv.at[k], at.z(way)
        )

    def near(self, distance, src=None):
        at = self.at
        block = self.out.at[jnp.clip(at.c - distance, 0, at.n_c - 1) * 2 + at.lo]
        k = 2 * at.n_c + distance + at.n_c
        return remote(
            block if src is None else src, block, self.send.at[k], self.recv.at[k], at.core
        )

    def there(self, way, hop):
        return self.at.c + hop < self.at.n_c if way > 0 else self.at.c >= hop

    def start(self):
        for way in (1, -1):

            @pl.when(self.there(way, 1))
            def _(way=way):
                self.far(way, 1, self.src).start()

        self.near(0, self.src).start()
        self.local.start()

    def forward(self, hops=None):
        at = self.at
        for hop in hops or range(1, at.n_c):
            for way in (1, -1):

                @pl.when(self.there(-way, hop))
                def _(way=way, hop=hop):
                    self.far(way, hop).wait_recv()
                    if hop < at.n_c - 1:

                        @pl.when(self.there(way, 1))
                        def _():
                            self.far(way, hop + 1).start()

                    self.near(way * hop).start()

    def finish(self):
        at = self.at
        for hop in range(1, at.n_c):
            for way in (1, -1):

                @pl.when(self.there(way, 1) & self.there(-way, hop - 1))
                def _(way=way, hop=hop):
                    self.far(way, hop).wait_send()

                @pl.when(self.there(-way, hop))
                def _(way=way, hop=hop):
                    self.near(way * hop).wait()

        self.near(0, self.src).wait()
        self.local.wait()


def gather_sems(n_c):
    return [
        pltpu.SemaphoreType.DMA((4 * n_c,)),
        pltpu.SemaphoreType.DMA((4 * n_c,)),
        pltpu.SemaphoreType.DMA,
    ]


class Scatter:
    def __init__(self, at, part, near, sent, got, send, recv):
        self.at, self.part, self.near = at, part, near
        self.sent, self.got, self.send, self.recv = sent, got, send, recv

    def core(self, c):
        at = self.at
        return remote(
            self.part.at[c * 2 + 1 - at.lo], self.near.at[c], self.send.at[c], self.recv.at[c], at.core
        )

    def far(self, way, hop, slot):
        at = self.at
        k = at.n_c + hop + (0 if way > 0 else at.n_c)
        sent = self.sent.at[self.slot(jnp.clip(at.c + way * hop, 0, at.n_c - 1))]
        return remote(sent, self.got.at[slot], self.send.at[k], self.recv.at[k], at.z(way))

    def slot(self, c):
        return jnp.minimum(jnp.where(c > self.at.c, c - 1, c), self.at.n_c - 2)

    def end(self, way):
        return self.at.c if way > 0 else self.at.n_c

    there = Gather.there

    def start(self):
        at = self.at
        for i in range(at.n_c):
            self.core(jnp.where(at.c * 2 < at.n_c, at.n_c - 1 - i, i)).start()

    def pass_on(self, hops=None):
        at = self.at
        for hop in hops or range(at.n_c - 1, 0, -1):
            for way in (1, -1):

                @pl.when(self.there(way, hop))
                def _(way=way, hop=hop):
                    c = at.c + way * hop
                    self.core(c).wait_recv()
                    if hop < at.n_c - 1:
                        more = self.there(-way, 1)

                        @pl.when(more)
                        def _():
                            self.far(way, hop + 1, c).wait_recv()
                            self.add(c, True)

                        @pl.when(jnp.logical_not(more))
                        def _():
                            self.add(c, False)

                    else:
                        self.add(c, False)
                    self.far(way, hop, at.n_c if hop == 1 and way < 0 else c).start()

    def add(self, c, more):
        at, slot = self.at, self.slot(c)

        def rows_of(rows):
            value = self.part[c * 2 + at.lo, rows].astype(F32) + self.near[c, rows].astype(F32)
            if more:
                value = value + self.got[c, rows].astype(F32)
            self.sent[slot, rows] = value.astype(BF)

        by_rows(self.near.shape[1], rows_of)

    def arrive(self):
        self.core(self.at.c).wait_recv()
        for way in (1, -1):

            @pl.when(self.there(-way, 1))
            def _(way=way):
                self.far(way, 1, self.end(way)).wait_recv()

            @pl.when(jnp.logical_not(self.there(-way, 1)))
            def _(way=way):
                self.got[self.end(way)] = jnp.zeros(self.got.shape[1:], BF)

    def total(self, rows):
        c, at = self.at.c, self.at
        return (
            self.part[c * 2 + at.lo, rows].astype(F32)
            + self.near[c, rows].astype(F32)
            + self.got[self.end(1), rows].astype(F32)
            + self.got[self.end(-1), rows].astype(F32)
        )

    def free(self, credit):
        at = self.at

        def tell(k, peer):
            pl.semaphore_signal(credit.at[k], inc=1, device_id=peer, device_id_type=MESH)

        tell(0, at.core)
        for k, way in ((1, 1), (2, -1)):

            @pl.when(self.there(way, 1))
            def _(k=k, way=way):
                tell(k, at.z(way))

        pl.semaphore_wait(credit.at[0], 1)
        for k, way in ((1, 1), (2, -1)):

            @pl.when(self.there(-way, 1))
            def _(k=k):
                pl.semaphore_wait(credit.at[k], 1)

    def finish(self):
        at = self.at
        for c in range(at.n_c):
            self.core(c).wait_send()
        for hop in range(1, at.n_c):
            for way in (1, -1):

                @pl.when(self.there(way, hop))
                def _(way=way, hop=hop):
                    self.far(way, hop, 0).wait_send()


def scatter_scratch(n_c, half, width):
    return [
        pltpu.VMEM((2 * n_c, half, width), BF),
        pltpu.VMEM((n_c, half, width), BF),
        pltpu.VMEM((n_c - 1, half, width), BF),
        pltpu.VMEM((n_c + 1, half, width), BF),
        pltpu.SemaphoreType.DMA((3 * n_c,)),
        pltpu.SemaphoreType.DMA((3 * n_c,)),
    ]


class Swap:
    def __init__(self, at, shard, full, send, recv, local):
        self.at = at
        rows, width = shard.shape[1], full.shape[3]
        here = pl.ds((at.f * at.n_c + at.c) * rows, rows)
        target = full.at[at.hi, :, here, :]

        def columns(c):
            return shard.at[:, :, pl.ds(pl.multiple_of(c * width, 128), width)]

        self.local = pltpu.make_async_copy(columns(at.c), target, local)
        self.far = [
            remote(columns(at.ctx(s)), target, send.at[s], recv.at[s], at.z(s))
            for s in range(1, at.n_c)
        ]

    def start(self):
        self.local.start()
        for copy in self.far:
            copy.start()

    def arrived(self, s):
        if s == 0:
            self.local.wait()
        else:
            self.far[s - 1].wait_recv()
        return self.at.ctx(-s)

    def finish(self):
        for copy in self.far:
            copy.wait_send()


class Spread:
    def __init__(self, at, full, send, recv):
        self.at, self.full, self.send, self.recv = at, full, send, recv
        self.height = full.shape[2] // at.n_f // at.n_c

    def part(self, o, shift, piece):
        at = self.at
        first = (at.fsdp(shift) * at.n_c + piece) * self.height
        return self.full.at[at.other(o), :, pl.ds(first, self.height), :]

    def copy(self, part, k, piece, peer):
        k = k * self.at.n_c + piece
        return remote(part, part, self.send.at[k], self.recv.at[k], peer)

    def own(self, piece):
        at = self.at
        return [
            *(self.copy(self.part(0, 0, piece), s, piece, at.xy(s, 0)) for s in range(1, at.n_f)),
            self.copy(self.part(0, 0, piece), 0, piece, at.xy(0, 1)),
        ]

    def passes(self, piece):
        at = self.at
        n = at.n_f
        if piece < at.n_c // 2:
            return [self.copy(self.part(0, -s, piece), n + s, piece, at.xy(0, 1)) for s in range(1, n)]
        return [self.copy(self.part(1, 0, piece), n + s, piece, at.xy(s, 0)) for s in range(1, n)]

    def start(self, piece):
        for copy in self.own(piece):
            copy.start()

    def forward(self, piece):
        own = self.own(piece)
        for copy in own[:-1] if piece < self.at.n_c // 2 else own[-1:]:
            copy.wait_recv()
        for copy in self.passes(piece):
            copy.start()

    def wait(self):
        for piece in range(self.at.n_c):
            own = self.own(piece)
            for copy in own[-1:] if piece < self.at.n_c // 2 else own[:-1]:
                copy.wait_recv()
            for copy in own:
                copy.wait_send()
            for copy in self.passes(piece):
                copy.wait()


class Collect:
    def __init__(self, at, partial, local, by_x, by_y, pass_x, pass_y, send, recv):
        self.at, self.partial, self.local = at, partial, local
        self.by_x, self.by_y, self.pass_x, self.pass_y = by_x, by_y, pass_x, pass_y
        self.send, self.recv = send, recv
        self.matrices = by_y.shape[0]
        self.height = partial.shape[2] // at.n_f // 2

    def first(self, shift, half):
        return (self.at.fsdp(shift) * 2 + half) * self.height

    def part(self, o, shift, half, m):
        rows = pl.ds(self.first(shift, half), self.height)
        return self.partial.at[self.at.other(o), m, rows, :]

    def half(self, ref, half, m):
        return ref.at[m, pl.ds(half * self.height, self.height), :]

    def copy(self, src, dst, k, m, peer):
        k = k * self.matrices + m
        return remote(src, dst, self.send.at[k], self.recv.at[k], peer)

    def raw(self, group, m):
        at = self.at
        n, shifts = at.n_f, range(1, at.n_f)
        if group == 0:
            return [
                self.copy(self.part(1, s, 0, m), self.pass_x.at[s - 1, m], s, m, at.xy(s, 0)) for s in shifts
            ]
        if group == 1:
            return [
                self.copy(self.part(1, s, 1, m), self.pass_y.at[s - 1, m], n + s, m, at.xy(0, 1))
                for s in shifts
            ]
        return [
            *(
                self.copy(
                    self.part(0, s, 0, m), self.half(self.by_x.at[s - 1], 0, m), 2 * n + s, m, at.xy(s, 0)
                )
                for s in shifts
            ),
            self.copy(self.part(1, 0, 1, m), self.half(self.by_y, 1, m), 0, m, at.xy(0, 1)),
        ]

    def added(self, s, m):
        at = self.at
        if s == 0:
            return self.copy(self.pass_x.at[0, m], self.half(self.by_y, 0, m), at.n_f, m, at.xy(0, 1))
        target = self.half(self.by_x.at[s - 1], 1, m)
        return self.copy(self.pass_y.at[s - 1, m], target, 3 * at.n_f + s, m, at.xy(s, 0))

    def start(self, m):
        for group in range(3):
            for copy in self.raw(group, m):
                copy.start()

    def load(self, o, shift, half, m, stage, k):
        return pltpu.make_async_copy(self.part(o, shift, half, m), stage, self.local.at[k])

    def fetch(self, m, stages):
        self.load(1, 0, 0, m, stages[0], 0).start()
        self.load(0, 1, 1, m, stages[1], 1).start()

    def fetch_own(self, m, stages):
        for half in range(2):
            self.load(0, 0, half, m, stages[half], 2 + 2 * m + half).start()

    def reader(self, o, shift, half, m, stage):
        if stage is None:
            first = self.first(shift, half)
            return lambda rows, start: self.partial[
                self.at.other(o), m, pl.ds(pl.multiple_of(first + start, STEP_ROWS), STEP_ROWS)
            ]
        return lambda rows, start: stage[rows]

    def sweep(self, step):
        @pl.loop(0, self.height // STEP_ROWS)
        def _(i):
            start = pl.multiple_of(i * STEP_ROWS, STEP_ROWS)
            step(pl.ds(start, STEP_ROWS), start)

    def forward(self, m, stages=(None, None)):
        n = self.at.n_f
        for copy in self.raw(0, m):
            copy.wait_recv()
        if stages[0] is not None:
            self.load(1, 0, 0, m, stages[0], 0).wait()
        own = self.reader(1, 0, 0, m, stages[0])

        def add_y(rows, start):
            value = own(rows, start).astype(F32)
            for s in range(n - 1):
                value = value + self.pass_x[s, m, rows].astype(F32)
            self.pass_x[0, m, rows] = value.astype(BF)

        self.sweep(add_y)
        self.added(0, m).start()
        for s in range(1, n):
            if stages[1] is not None:
                load = self.load(0, s, 1, m, stages[1], 1)
                if s > 1:
                    load.start()
                load.wait()
            own_x = self.reader(0, s, 1, m, stages[1])
            self.raw(1, m)[s - 1].wait_recv()

            def add_x(rows, start, s=s, own_x=own_x):
                value = own_x(rows, start).astype(F32) + self.pass_y[s - 1, m, rows].astype(F32)
                self.pass_y[s - 1, m, rows] = value.astype(BF)

            self.sweep(add_x)
            self.added(s, m).start()

    def total(self, m, squares, stages=(None, None)):
        n = self.at.n_f
        for copy in self.raw(2, m):
            copy.wait_recv()
        for s in range(n):
            self.added(s, m).wait_recv()
        for half in range(2):
            if stages[half] is not None:
                self.load(0, 0, half, m, stages[half], 2 + 2 * m + half).wait()
            own = self.reader(0, 0, half, m, stages[half])

            def add(rows, start, half=half, own=own):
                here = pl.ds(pl.multiple_of(half * self.height + start, STEP_ROWS), STEP_ROWS)
                value = own(rows, start).astype(F32) + self.by_y[m, here].astype(F32)
                for s in range(n - 1):
                    value = value + self.by_x[s, m, here].astype(F32)
                rounded = value.astype(BF)
                self.by_y[m, here] = rounded
                value = rounded.astype(F32)
                value = value * value
                tall = squares.shape[1]
                rows = value[:tall]
                for r in range(tall, value.shape[0], tall):
                    rows = rows + value[r : r + tall]
                wide = squares.shape[2]
                lanes = rows[:, :wide]
                for c in range(wide, value.shape[1], wide):
                    lanes = lanes + rows[:, c : c + wide]
                squares[0] += lanes

            self.sweep(add)

    def finish(self):
        for m in range(self.matrices):
            for group in range(3):
                for copy in self.raw(group, m):
                    copy.wait_send()
            for s in range(self.at.n_f):
                self.added(s, m).wait_send()


class Share:
    def __init__(self, at, src, out, send, recv, local):
        self.at, self.local = at, pltpu.make_async_copy(src, out.at[at.t], local)
        across = at.t + 2 - 4 * at.hi
        self.first = [
            remote(src, out.at[at.t], send.at[0], recv.at[0], at.xy(0, 1)),
            remote(src, out.at[at.t], send.at[1], recv.at[1], at.core),
        ]
        self.second = remote(out.at[across], out.at[across], send.at[2], recv.at[2], at.core)

    def start(self):
        for copy in (*self.first, self.local):
            copy.start()

    def forward(self):
        self.first[0].wait_recv()
        self.second.start()

    def finish(self):
        self.first[0].wait_send()
        self.first[1].wait()
        self.second.wait()
        self.local.wait()


def collect_scratch(n_f, matrices, height, columns):
    half = (matrices, height // 2, columns)
    return [
        pltpu.VMEM((n_f - 1, matrices, height, columns), BF),
        pltpu.VMEM((matrices, height, columns), BF),
        pltpu.VMEM((n_f - 1, *half), BF),
        pltpu.VMEM((n_f - 1, *half), BF),
        dma(4 * n_f * matrices),
        dma(4 * n_f * matrices),
    ]


class Return:
    def __init__(self, at, summed, shard, send, recv, local):
        rows, sheets = shard.shape[1], summed.shape[0]
        beside = shard.shape[0] // sheets
        width = summed.shape[2] // beside
        self.copies = []
        for m in range(shard.shape[0]):
            target = shard.at[m, :, pl.ds(pl.multiple_of(at.c * width, 128), width)]
            first = m % beside * width

            def part(c, m=m, first=first):
                here = pl.ds(pl.multiple_of(c * rows, rows), rows)
                return summed.at[m // beside, here, first : first + width]

            copies = []
            for s in range(1, at.n_c):
                k = m * at.n_c + s
                copies.append(remote(part(at.ctx(s)), target, send.at[k], recv.at[k], at.z(s)))
            copies.append(pltpu.make_async_copy(part(at.c), target, local.at[m]))
            self.copies.append(copies)

    def start(self, m):
        for copy in self.copies[m]:
            copy.start()

    def wait(self):
        for copies in self.copies:
            for copy in copies:
                copy.wait()


def pack_weights(w, packed):
    heads = w.shape[0]
    for i in range(4):
        for y in range(heads):
            k = (i * heads + y) * HEAD_DIM
            packed[:, k : k + HEAD_DIM] = w[y, i]


def turn(values, cos, sine):
    return values * cos + pltpu.roll(values, HEAD_DIM // 2, 1) * sine


def recast(wide, low):
    for m in range(wide.shape[0]):

        def step(rows, m=m):
            low[m, rows] = wide[m, rows].astype(low.dtype)

        by_rows(wide.shape[1], step)


def dma(count):
    return pltpu.SemaphoreType.DMA((count,))


def make_shards(mesh):
    sizes = tuple(mesh.shape[a] for a in ("fsdp", "ctx", "tp"))
    n_f, n_c, n_t = sizes

    def call(kernel, name, collective, outs, ins, out_specs, scratch, aliases=None, vmem=40):
        return pl.pallas_call(
            kernel,
            out_shape=outs,
            in_specs=ins,
            out_specs=out_specs,
            scratch_shapes=scratch,
            input_output_aliases=aliases or {},
            compiler_params=pltpu.CompilerParams(
                collective_id=collective, has_side_effects=True, vmem_limit_bytes=vmem << 20
            ),
            name=name,
        )

    def local(kernel, name, outs, scratch):
        return pl.pallas_call(
            kernel,
            out_shape=outs,
            scratch_shapes=scratch,
            compiler_params=pltpu.CompilerParams(vmem_limit_bytes=60 << 20),
            name=name,
        )

    def front_kernel(
        tok_ref, cot_ref, spots, key_place, cos, sine, att_ref, out_ref, ffp_ref, ffo_ref,
        rows_ref, attw_ref, ffw_ref, a2_ref, cots_ref, qkv, attended, mass, mid_ref,
        x_ref, own_cot, att_wide, ff_wide, att_low, ff_low, low, a1, packed, lk, lp,
        part, near, sent, got, ss, sr, g1, h1, l1, g2, h2, l2, g3, h3, l3, s4, r4, l4, s5, r5, l5, s6, r6, s7, r7,
    ):
        at = Place(sizes)
        half = x_ref.shape[0]
        mine = pl.ds(pl.multiple_of(at.lo * half, half), half)
        loads = [
            pltpu.make_async_copy(tok_ref.at[at.hi, mine], x_ref, lk.at[0]),
            pltpu.make_async_copy(att_ref, att_wide.at[pl.ds(0, 3)], lk.at[1]),
            pltpu.make_async_copy(out_ref, att_wide.at[3], lk.at[2]),
            pltpu.make_async_copy(ffp_ref, ff_wide.at[pl.ds(0, 2)], lk.at[3]),
            pltpu.make_async_copy(ffo_ref, ff_wide.at[2], lk.at[4]),
            pltpu.make_async_copy(cot_ref.at[at.hi, mine], own_cot, lk.at[5]),
        ]
        for copy in loads:
            copy.start()
        scatter = Scatter(at, part, near, sent, got, ss, sr)
        gather = Gather(at, low, rows_ref, g1, h1, l1)
        cots = Gather(at, own_cot, cots_ref, g2, h2, l2)
        a2 = Gather(at, low, a2_ref, g3, h3, l3)
        swap_att = Swap(at, att_low, attw_ref, s4, r4, l4)
        swap_ff = Swap(at, ff_low, ffw_ref, s5, r5, l5)
        spread_att = Spread(at, attw_ref, s6, r6)
        spread_ff = Spread(at, ffw_ref, s7, r7)
        at.greet([at.core, *at.all_z(), *at.all_xy()])
        loads[0].wait()

        def norm_one(rows):
            low[rows] = mean_spread(x_ref[rows].astype(F32))[0].astype(BF)

        by_rows(half, norm_one)
        loads[1].wait()
        loads[2].wait()
        recast(att_wide, att_low)
        swap_att.start()
        gather.start()
        spread_att.start(swap_att.arrived(0))
        for copy in loads[3:]:
            copy.wait()
        recast(ff_wide, ff_low)
        gather.forward(range(1, 2))
        behind = [s for pair in zip(range(1, n_c), range(n_c - 1, 0, -1)) for s in pair][: n_c - 1]
        spread_att.start(swap_att.arrived(behind[0]))
        spread_att.start(swap_att.arrived(behind[1]))
        gather.forward(range(2, n_c - 1))
        swap_ff.start()
        for s in behind[2:]:
            spread_att.start(swap_att.arrived(s))
        gather.forward(range(n_c - 1, n_c))
        for piece in range(n_c):
            spread_att.forward(piece)
        spread_ff.start(swap_ff.arrived(0))
        gather.finish()
        take = [pltpu.make_async_copy(rows_ref.at[b], a1.at[pl.ds(b * half, half)], lp.at[b]) for b in range(2 * n_c)]
        for copy in take:
            copy.start()
        spread_att.wait()
        heads = attw_ref.shape[0]
        packs = [
            pltpu.make_async_copy(
                attw_ref.at[y, i],
                packed.at[:, pl.ds((i * heads + y) * HEAD_DIM, HEAD_DIM)],
                lp.at[2 * n_c + i * heads + y],
            )
            for i in range(4)
            for y in range(heads)
        ]
        for copy in packs:
            copy.start()
        for copy in (*take, *packs):
            copy.wait()
        attend(a1, packed, spots, key_place, cos, sine, qkv, attended, mass, part)
        scatter.start()
        cots.start()
        scatter.pass_on(range(n_c - 1, n_c - 2, -1))
        spread_ff.start(swap_ff.arrived(behind[0]))
        spread_ff.start(swap_ff.arrived(behind[1]))
        cots.forward(range(1, 2))
        scatter.pass_on(range(n_c - 2, 1, -1))
        for s in behind[2:]:
            spread_ff.start(swap_ff.arrived(s))
        cots.forward(range(2, 3))
        scatter.pass_on(range(1, 2))
        spread_ff.forward(0)
        scatter.arrive()

        def norm_two(rows):
            mid = x_ref[rows].astype(F32) + scatter.total(rows)
            mid_ref[rows] = mid
            low[rows] = mean_spread(mid)[0].astype(BF)

        by_rows(half, norm_two)
        a2.start()
        a2.forward(range(1, 2))
        spread_ff.forward(n_c - 1)
        a2.forward(range(2, 3))
        for piece in range(1, n_c - 1):
            spread_ff.forward(piece)
        a2.forward(range(3, n_c))
        cots.forward(range(3, n_c))
        cots.finish()
        a2.finish()
        scatter.finish()
        swap_att.finish()
        swap_ff.finish()
        spread_ff.wait()

    def back_kernel(
        a2_ref, cots_ref, joined_ref, d_a2_ref, ffw_ref, mid_ref, tok_ref, cot_ref, a1_ref, attw_ref,
        spots, key_place, cos, sine, qkv, attended, mass,
        input_ref, out_ref, attg_ref, ffg_ref, norm_ref, grad_ref, rows_ref,
        rows_one, rows_two, wide, sheets, d_v, d_k, own, block, low, lk, lg, credit,
        part, near, sent, got, ss, sr, near2, sent2, got2, ss2, sr2, g1, h1, l1, lf, s4, r4, l4, s5, r5, l5, s6, r6, l6,
        total, got_p, got_c, s7, r7, *collected,
    ):
        at = Place(sizes)
        half = own.shape[0]
        length, tall = 2 * n_c * half, wide.shape[1]
        mine = pl.ds(pl.multiple_of(at.lo * half, half), half)

        def load(*pairs):
            copies = [pltpu.make_async_copy(src, dst, lk.at[i]) for i, (src, dst) in enumerate(pairs)]
            for copy in copies:
                copy.start()
            for copy in copies:
                copy.wait()

        def flat(ref, cols=slice(None)):
            value = ref[:, :, cols]
            return value.reshape(length, value.shape[2])

        scatter = Scatter(at, part, near, sent, got, ss, sr)
        branch = Scatter(at, rows_one, near2, sent2, got2, ss2, sr2)
        gather = Gather(at, low, rows_ref, g1, h1, l1)
        columns = sheets.shape[3]
        high = tall // n_f // 2
        early = [wide.at[1, pl.ds(length, high), pl.ds(i * columns, columns)] for i in range(2)]
        late = [
            [sheets.at[m % 2, 0, pl.ds((m // 2 * 2 + i) * high, high)] for i in range(2)] for m in range(3)
        ]
        collect_ff = Collect(at, grad_ref, lf, *collected[:6])
        collect_att = Collect(at, sheets, None, *collected[6:])
        give_ff = Return(at, collected[1], ffg_ref, s5, r5, l5)
        give_att = Return(at, collected[7], attg_ref, s4, r4, l4)
        total[0] = jnp.zeros(total.shape[1:], F32)
        at.greet([*plane(at), *at.all_z()])
        load((d_a2_ref, part))
        scatter.start()
        load(
            (a2_ref, rows_one),
            (cots_ref, rows_two),
            (joined_ref.at[0], wide.at[0, pl.ds(0, length)]),
            (joined_ref.at[1], wide.at[0, pl.ds(length, length)]),
            (joined_ref.at[2], wide.at[1, pl.ds(0, length)]),
            (cot_ref.at[at.hi, mine], block),
        )

        def keep(k):
            y, m = k % 2, k // 2
            return pltpu.make_async_copy(sheets.at[y, 0], grad_ref.at[y, m], lg.at[y])

        for k in range(6):
            y, m = k % 2, k // 2
            if k >= 2 and y == 0:
                keep(k - 2).wait()
                keep(k - 1).wait()
            rows = rows_two if m == 2 else rows_one
            slot, start = ((0, 0), (0, length), (1, 0))[m]

            @pl.loop(0, 2)
            def _(i, y=y, rows=rows, slot=slot, start=start):
                cols = pl.ds(pl.multiple_of(i * (tall // 2), tall // 2), tall // 2)
                side = wide[slot, start : start + length, y * columns : (y + 1) * columns]
                sheets[y, 0, cols] = dot(flat(rows, cols), side, ((0,), (0,))).astype(BF)

            keep(k).start()
            if k == 0:
                scatter.pass_on(range(n_c - 1, n_c - 2, -1))
            if k == 2:
                collect_ff.start(0)
            if k == 3:
                scatter.pass_on(range(n_c - 2, 1, -1))
            if k == 4:
                collect_ff.start(1)
        keep(4).wait()
        keep(5).wait()
        collect_ff.start(2)
        collect_ff.fetch(0, early)
        scatter.pass_on(range(1, 2))
        scatter.arrive()

        def norm_two(rows):
            normed, scale = mean_spread(mid_ref[rows])
            grad = block[rows].astype(F32) + norm_back(scatter.total(rows), normed, scale)
            own[rows] = grad
            low[rows] = grad.astype(BF)

        by_rows(half, norm_two)
        gather.start()
        heads = attw_ref.shape[0]
        scatter.finish()
        scatter.free(credit.at[0])
        width = part.shape[2] // 4
        gather.forward(range(1, 2))
        collect_ff.forward(0, early)
        collect_ff.fetch(1, early)
        gather.forward(range(2, n_c - 1))
        collect_ff.forward(1, early)
        collect_ff.fetch(2, early)
        for m in range(3):
            collect_ff.fetch_own(m, late[m])
        collect_ff.forward(2, early)
        gather.forward(range(n_c - 1, n_c))
        load(
            (a1_ref, rows_two),
            *(
                (attw_ref.at[y, i], wide.at[0, :, pl.ds((i * heads + y) * HEAD_DIM, HEAD_DIM)])
                for i in range(4)
                for y in range(heads)
            ),
        )
        gather.finish()
        load((rows_ref, rows_one), (tok_ref.at[at.hi, mine], low))
        packed, joint = wide.at[0], wide.at[1, pl.ds(length, length)]
        wide_heads = heads * HEAD_DIM
        joint[:, :wide_heads] = dot(flat(rows_one), packed[:, 3 * wide_heads :], ((1,), (0,))).astype(BF)
        collect_ff.total(0, total, late[0])
        give_ff.start(0)
        for y in range(heads):
            attend_back(y, packed, joint, spots, key_place, cos, sine, qkv, mass, d_v, d_k, heads)
            if y == 0:
                collect_ff.total(1, total, late[1])
                give_ff.start(1)

        @pl.loop(0, 4)
        def _(c):
            cols = pl.ds(pl.multiple_of(c * width, width), width)
            value = dot(joint[:, : 3 * wide_heads], packed[cols, : 3 * wide_heads], ((1,), (1,))).astype(BF)
            part[:, :, cols] = value.reshape(part.shape[0], part.shape[1], width)

        scatter.start()
        collect_ff.total(2, total, late[2])

        @pl.loop(0, 2)
        def _(c):
            cols = pl.ds(pl.multiple_of(c * 2 * width, width), 2 * width)
            for i in range(4):
                if i < 3:
                    value = dot(
                        flat(rows_two, cols), joint[:, i * wide_heads : (i + 1) * wide_heads], ((0,), (0,))
                    )
                else:
                    value = dot(flat(rows_one, cols), attended[...], ((0,), (0,)))
                for y in range(heads):
                    sheets[y, 0, cols, i * HEAD_DIM : (i + 1) * HEAD_DIM] = value[
                        :, y * HEAD_DIM : (y + 1) * HEAD_DIM
                    ].astype(BF)

        collect_att.start(0)
        scatter.pass_on(range(n_c - 1, n_c - 2, -1))
        load(*((ffw_ref.at[y, 2], wide.at[0, :, pl.ds(y * columns, columns)]) for y in range(heads)))

        @pl.loop(0, 4)
        def _(c):
            cols = pl.ds(pl.multiple_of(c * width, width), width)
            value = dot(wide[1, :length], wide[0, cols], ((1,), (1,))).astype(BF)
            rows_one[:, :, cols] = value.reshape(rows_one.shape[0], rows_one.shape[1], width)

        branch.start()
        give_ff.start(2)
        share_block = Share(at, block, out_ref, s6.at[0], r6.at[0], l6.at[0])
        share_input = Share(at, low, input_ref, s6.at[1], r6.at[1], l6.at[1])
        scatter.pass_on(range(n_c - 2, 1, -1))
        branch.pass_on(range(n_c - 1, n_c - 2, -1))
        collect_att.forward(0)
        scatter.pass_on(range(1, 2))
        branch.pass_on(range(n_c - 2, 1, -1))
        collect_att.total(0, total)
        for m in range(4):
            give_att.start(m)
        branch.pass_on(range(1, 2))
        scatter.arrive()

        def norm_one(rows):
            normed, scale = mean_spread(low[rows].astype(F32))
            low[rows] = (own[rows] + norm_back(scatter.total(rows), normed, scale)).astype(BF)

        by_rows(half, norm_one)
        share_input.start()
        branch.arrive()

        def add(rows):
            block[rows] = (mid_ref[rows] + branch.total(rows)).astype(BF)

        by_rows(half, add)
        share_block.start()
        scatter.finish()
        branch.finish()
        collect_ff.finish()
        collect_att.finish()
        share_input.forward()
        share_block.forward()
        sum_norm(at, norm_ref, total, got_p, got_c, s7, r7)
        give_ff.wait()
        give_att.wait()
        share_block.finish()
        share_input.finish()

    def plane(at):
        count = n_f * n_t
        here = at.f * n_t + at.t
        others = [lax.rem(here + i, count) for i in range(1, count)]
        return [(i // n_t, at.c, lax.rem(i, n_t)) for i in others]

    def sum_norm(at, norm_ref, total, got_p, got_c, send, recv):
        base = 0
        stages = ((plane(at), got_p, at.f * n_t + at.t), (at.all_z(), got_c, at.c))
        for stage, (peers, got, place) in enumerate(stages):
            copies = [
                remote(total.at[stage], got.at[place], send.at[base + i], recv.at[base + i], peer)
                for i, peer in enumerate(peers)
            ]
            base += len(peers)
            for copy in copies:
                copy.start()
            got[place] = total[stage]
            for copy in copies:
                copy.wait()
            value = got[0]
            for i in range(1, got.shape[0]):
                value = value + got[i]
            total[stage + 1] = value
        norm = jnp.sqrt(jnp.sum(total[2], axis=(0, 1), keepdims=True))
        norm_ref[...] = jnp.broadcast_to(norm, norm_ref.shape)

    def finish_kernel(norm_ref, block_in, input_in, attg_ref, ffg_ref, *refs):
        olds, outs, scratch = refs[:12], refs[12:34], refs[34:]
        low_att, low_ff, wide_att, wide_ff, old_att, old_ff, block_keep, input_low, input_keep, ls = scratch
        groups = (
            (attg_ref, low_att, wide_att, old_att, 0, attg_ref.shape[1]),
            (ffg_ref, low_ff, wide_ff, old_ff, 2, attg_ref.shape[1] // 4),
        )
        chunks = [
            (group, m, r)
            for group in groups
            for m in range(group[0].shape[0])
            for r in range(group[0].shape[1] // group[5])
        ]

        def sheet(array, first, m, group):
            last = group[0].shape[0] - 1
            return array[first + 1] if m == last else array[first].at[m]

        loads, stores = [], []
        for i, (group, m, r) in enumerate(chunks):
            here = pl.ds(r * group[5], group[5])
            one = [pltpu.make_async_copy(group[0].at[m, here], group[1].at[m, here], ls.at[i, 0, 3])]
            one += [
                pltpu.make_async_copy(
                    sheet(olds, 4 * j + group[4], m, group).at[here], group[3].at[j, m, here], ls.at[i, 0, j]
                )
                for j in range(3)
            ]
            for copy in one:
                copy.start()
            loads.append(one)
        kept = ((block_in, block_keep, block_keep, outs[20]), (input_in, input_low, input_keep, outs[21]))
        through = []
        for i, (src, first, keep, out) in enumerate(kept):
            copy = pltpu.make_async_copy(src, first, ls.at[len(chunks), 0, i])
            copy.start()
            through.append((copy, pltpu.make_async_copy(keep, out, ls.at[len(chunks), 1, i])))
        norm = norm_ref[0:1, 0:1]
        clip = jnp.minimum(1.0, MAX_NORM / (norm + 1e-06))
        width = ffg_ref.shape[1] * n_f * n_c
        for i, (group, m, r) in enumerate(chunks):
            for copy in loads[i]:
                copy.wait()
            low, wide, old = group[1:4]
            rate = (width // 32) ** (-0.5) if group[4] == 0 and m == 3 else width ** (-0.5)

            @pl.loop(0, group[5] // ROWS)
            def _(k, low=low, wide=wide, old=old, m=m, r=r, step=group[5], rate=rate):
                rows = pl.ds(pl.multiple_of(r * step + k * ROWS, ROWS), ROWS)
                grad = low[m, rows].astype(F32)
                wide[m, rows] = grad
                first_new, second_new, weight_new = adam_step(
                    old[0, m, rows], grad, old[1, m, rows], old[2, m, rows], clip, rate
                )
                old[0, m, rows] = weight_new
                old[1, m, rows] = first_new
                old[2, m, rows] = second_new
                low[m, rows] = weight_new.astype(BF)

            here = pl.ds(r * group[5], group[5])
            for k, (src, out) in enumerate(
                ((wide, 0), (old.at[1], 4), (old.at[2], 8), (old.at[0], 12), (low, 16))
            ):
                store = pltpu.make_async_copy(
                    src.at[m, here], sheet(outs, out + group[4], m, group).at[here], ls.at[i, 1, k]
                )
                store.start()
                stores.append(store)
        for load, store in through:
            load.wait()
            if load is through[1][0]:
                recast(input_low, input_keep)
            store.start()
            stores.append(store)
        for store in stores:
            store.wait()

    def attend(a1, packed, spots, key_place, cos, sine, qkv, attended, mass, part):
        wide = attended.shape[1]
        heads = wide // HEAD_DIM
        for i in range(3):
            joint = dot(a1[...], packed[:, i * wide : (i + 1) * wide], ((1,), (0,)))
            for y in range(heads):
                cols = slice(y * HEAD_DIM, (y + 1) * HEAD_DIM)
                head = joint[:, cols]
                if i < 2:
                    head = turn(head, cos[...], sine[...])
                qkv[i, :, cols] = head.astype(BF)
        for y in range(heads):
            cols = slice(y * HEAD_DIM, (y + 1) * HEAD_DIM)

            @pl.loop(0, a1.shape[0] // QUERIES)
            def _(c, y=y, cols=cols):
                rows = pl.ds(pl.multiple_of(c * QUERIES, QUERIES), QUERIES)
                scores = dot(qkv[0, rows, cols], qkv[1, :, cols], ((1,), (1,))) * SCORE_SCALE
                allowed = (key_place[...] <= spots[rows, 0:1]) & (key_place[...] >= spots[rows, 1:2])
                scores = jnp.where(allowed, scores, NEG_FILL)
                peak = jnp.max(scores, axis=1, keepdims=True)
                exp_scores = jnp.exp(scores - peak)
                total = jnp.sum(exp_scores, axis=1, keepdims=True)
                probs = (exp_scores * (1.0 / total)).astype(BF)
                attended[rows, cols] = dot(probs, qkv[2, :, cols], ((1,), (0,))).astype(BF)
                mass[rows, y : y + 1] = peak + jnp.log(total)

        width = part.shape[2] // 4

        @pl.loop(0, 4)
        def _(c):
            cols = pl.ds(pl.multiple_of(c * width, width), width)
            value = dot(attended[...], packed[cols, 3 * wide :], ((1,), (1,))).astype(BF)
            part[:, :, cols] = value.reshape(part.shape[0], part.shape[1], width)

    def attend_back(y, packed, joint, spots, key_place, cos, sine, qkv, mass, d_v, d_k, heads):
        wide = heads * HEAD_DIM
        cols = slice(y * HEAD_DIM, (y + 1) * HEAD_DIM)

        @pl.loop(0, qkv.shape[1] // QUERIES)
        def _(c):
            rows = pl.ds(pl.multiple_of(c * QUERIES, QUERIES), QUERIES)
            query, key, value = qkv[0, rows, cols], qkv[1, :, cols], qkv[2, :, cols]
            d_att = joint[rows, cols]
            scores = dot(query, key, ((1,), (1,))) * SCORE_SCALE
            allowed = (key_place[...] <= spots[rows, 0:1]) & (key_place[...] >= spots[rows, 1:2])
            probs = jnp.exp(jnp.where(allowed, scores, NEG_FILL) - mass[rows, y : y + 1])
            d_prob = dot(d_att, value, ((1,), (1,)))
            delta = jnp.sum(probs * d_prob, axis=1, keepdims=True)
            d_score = (probs * (d_prob - delta)).astype(BF)
            v_part = dot(probs.astype(BF), d_att, ((0,), (0,)))
            k_part = dot(d_score, query, ((0,), (0,)))

            @pl.when(c == 0)
            def _():
                d_v[...] = v_part
                d_k[...] = k_part

            @pl.when(c > 0)
            def _():
                d_v[...] += v_part
                d_k[...] += k_part

            d_query = dot(d_score, key, ((1,), (0,))) * SCORE_SCALE
            joint[rows, cols] = turn(d_query, cos[rows], -sine[rows]).astype(BF)

        joint[:, wide + y * HEAD_DIM : wide + (y + 1) * HEAD_DIM] = turn(
            d_k[...] * SCORE_SCALE, cos[...], -sine[...]
        ).astype(BF)
        joint[:, 2 * wide + y * HEAD_DIM : 2 * wide + (y + 1) * HEAD_DIM] = d_v[...].astype(BF)

    def hidden_kernel(a2, cot, w, d_a2, joined, kept):
        d_up, d_gate, hidden = joined.at[0], joined.at[1], joined.at[2]
        step, steps = pl.program_id(0), pl.num_programs(0)
        tile = w.shape[3]
        here = pl.ds(pl.multiple_of(step * tile, tile), tile)
        length, width = a2.shape
        chunk = length // 2

        @pl.loop(0, 2)
        def _(i):
            rows = pl.ds(pl.multiple_of(i * chunk, chunk), chunk)
            up = dot(a2[rows], w[0, 0], ((1,), (0,)))
            gate = dot(a2[rows], w[0, 1], ((1,), (0,)))
            d_hid = dot(cot[rows], w[0, 2], ((1,), (0,)))
            sigma = jax.nn.sigmoid(gate)
            act = gate * sigma
            hidden[rows, here] = (act * up).astype(BF)
            d_up[rows, here] = (d_hid * act).astype(BF)
            d_gate[rows, here] = (d_hid * up * sigma * (1.0 + gate * (1.0 - sigma))).astype(BF)

        for m in range(2):
            kept[m, :, here] = w[0, m]

        @pl.when(step == steps - 1)
        def _():
            @pl.loop(0, 8)
            def _(i):
                cols = pl.ds(pl.multiple_of(i * (width // 8), width // 8), width // 8)
                d_a2[:, cols] = (
                    dot(d_up[...], kept[0, cols], ((1,), (1,)))
                    + dot(d_gate[...], kept[1, cols], ((1,), (1,)))
                ).astype(BF)

    def shards(
        tokens,
        cotangent,
        lengths,
        deal,
        att_proj,
        attn_out,
        ff_proj,
        ff_out,
        att_proj_first,
        attn_out_first,
        ff_proj_first,
        ff_out_first,
        att_proj_second,
        attn_out_second,
        ff_proj_second,
        ff_out_second,
    ):
        t_at = lax.axis_index("tp")
        pack_at = t_at // 2
        packs, row_count, width = tokens.shape
        half = row_count // 2
        pack_len = deal.shape[1]
        blocks = n_c * 2
        rows_bf = jax.ShapeDtypeStruct((blocks, half, width), BF)
        own_f32 = jax.ShapeDtypeStruct((half, width), F32)

        att_cols, ff_cols = att_proj.shape[2] // n_c, ff_proj.shape[2] // n_c
        att_shape, ff_shape = (4, *att_proj.shape[1:]), (3, *ff_proj.shape[1:])
        att_full = jax.ShapeDtypeStruct((2, 4, width, att_cols), BF)
        ff_full = jax.ShapeDtypeStruct((2, 3, width, ff_cols), BF)
        places = lax.dynamic_index_in_dim(deal, pack_at, 0, keepdims=False)
        length_row = lax.dynamic_index_in_dim(lengths, pack_at, 0, keepdims=False)
        seqs = lengths.shape[1]
        before = jnp.arange(seqs)[:, None] > jnp.arange(seqs)[None, :]
        starts = jnp.sum(jnp.where(before, length_row[None, :], 0), axis=1)
        inside = (places[:, None] >= starts[None, :]) & (
            places[:, None] < (starts + length_row)[None, :]
        )
        firsts = jnp.sum(jnp.where(inside, starts[None, :], 0), axis=1)
        freq_steps = jnp.arange(HEAD_DIM // 2, dtype=F32)
        inverse = jnp.power(10000.0, -2.0 * freq_steps / HEAD_DIM)
        angles = (places - firsts).astype(F32)[:, None] * inverse[None, :]
        cos_table, sine_table = jnp.cos(angles), jnp.sin(angles)
        tables = (
            jnp.stack([places, firsts], axis=1),
            places[None, :],
            jnp.concatenate([cos_table, cos_table], axis=1),
            jnp.concatenate([-sine_table, sine_table], axis=1),
        )
        rank_width = 2 * att_cols
        act_one, att_w, ff_w, act_two, cot_rows, qkv, attended, mass, resid_mid = call(
            front_kernel,
            "front",
            0,
            (
                rows_bf,
                att_full,
                ff_full,
                rows_bf,
                rows_bf,
                jax.ShapeDtypeStruct((3, pack_len, rank_width), BF),
                jax.ShapeDtypeStruct((pack_len, rank_width), BF),
                jax.ShapeDtypeStruct((pack_len, 2), F32),
                own_f32,
            ),
            [ANY, ANY] + [VMEM] * 4 + [ANY] * 4,
            (ANY,) * 5 + (VMEM,) * 4,
            [
                pltpu.VMEM((half, width), BF),
                pltpu.VMEM((half, width), BF),
                pltpu.VMEM(att_shape, F32),
                pltpu.VMEM(ff_shape, F32),
                pltpu.VMEM(att_shape, BF),
                pltpu.VMEM(ff_shape, BF),
                pltpu.VMEM((half, width), BF),
                pltpu.VMEM((pack_len, width), BF),
                pltpu.VMEM((width, 4 * rank_width), BF),
                dma(6),
                dma(2 * n_c + 8),
            ]
            + scatter_scratch(n_c, half, width)
            + gather_sems(n_c) * 3
            + [dma(n_c), dma(n_c), pltpu.SemaphoreType.DMA] * 2
            + [dma(2 * n_f * n_c)] * 4,
            vmem=56,
        )(tokens, cotangent, *tables, att_proj, attn_out, ff_proj, ff_out)
        act_two = act_two.reshape(pack_len, width)
        cot_rows = cot_rows.reshape(pack_len, width)

        tile = 256
        tiles = ff_cols // tile
        kept = pl.BlockSpec((pack_len, width), lambda i: (0, 0), pipeline_mode=pl.Buffered(1))
        moved = pl.BlockSpec((1, 3, width, tile), lambda i: (i // tiles, 0, 0, i % tiles))
        rows_flat = jax.ShapeDtypeStruct((pack_len, width), BF)
        act_two_part, joined = pl.pallas_call(
            hidden_kernel,
            grid=(2 * tiles,),
            out_shape=(rows_flat, jax.ShapeDtypeStruct((3, pack_len, 2 * ff_cols), BF)),
            in_specs=[kept, kept, moved],
            out_specs=(
                kept,
                pl.BlockSpec((3, pack_len, 2 * ff_cols), lambda i: (0, 0, 0), pipeline_mode=pl.Buffered(1)),
            ),
            scratch_shapes=[pltpu.VMEM((2, width, 2 * ff_cols), BF)],
            compiler_params=pltpu.CompilerParams(vmem_limit_bytes=60 << 20),
            name="hidden",
        )(act_two, cot_rows, ff_w)
        height = width // n_f
        count = n_f * n_t + n_c
        input_grad, block_out, att_total, ff_total, norm_value, *_ = call(
            back_kernel,
            "back",
            1,
            (
                jax.ShapeDtypeStruct((n_t, half, width), BF),
                jax.ShapeDtypeStruct((n_t, half, width), BF),
                jax.ShapeDtypeStruct(att_shape, BF),
                jax.ShapeDtypeStruct(ff_shape, BF),
                jax.ShapeDtypeStruct((8, 128), F32),
                ff_full,
                rows_bf,
            ),
            [ANY] * 5 + [VMEM] + [ANY] * 4 + [VMEM] * 7,
            (ANY,) * 4 + (VMEM,) + (ANY,) * 2,
            [
                pltpu.VMEM((2 * n_c, half, width), BF),
                pltpu.VMEM((2 * n_c, half, width), BF),
                pltpu.VMEM((2, width, 4 * rank_width), BF),
                pltpu.VMEM((2, 1, width, 4 * att_cols), BF),
                pltpu.VMEM((pack_len, HEAD_DIM), F32),
                pltpu.VMEM((pack_len, HEAD_DIM), F32),
                pltpu.VMEM((half, width), F32),
                pltpu.VMEM((half, width), BF),
                pltpu.VMEM((half, width), BF),
                dma(12),
                dma(2),
                pltpu.SemaphoreType.REGULAR((1, 3)),
            ]
            + scatter_scratch(n_c, half, width)
            + scatter_scratch(n_c, half, width)[1:]
            + gather_sems(n_c)
            + [dma(8)]
            + [dma(4 * n_c), dma(4 * n_c), dma(4), dma(3 * n_c), dma(3 * n_c), dma(3)]
            + [
                pltpu.SemaphoreType.DMA((2, 3)),
                pltpu.SemaphoreType.DMA((2, 3)),
                dma(2),
            ]
            + [pltpu.VMEM((k, 8, 128), F32) for k in (3, n_f * n_t, n_c)]
            + [dma(count), dma(count)]
            + collect_scratch(n_f, 3, height, ff_cols)
            + collect_scratch(n_f, 1, height, 4 * att_cols),
            vmem=62,
        )(
            act_two.reshape(rows_bf.shape), cot_rows.reshape(rows_bf.shape), joined, act_two_part.reshape(rows_bf.shape), ff_w,
            resid_mid, tokens, cotangent, act_one, att_w, *tables, qkv, attended, mass,
        )
        weights = (att_proj, attn_out, ff_proj, ff_out)
        firsts_old = (att_proj_first, attn_out_first, ff_proj_first, ff_out_first)
        seconds_old = (att_proj_second, attn_out_second, ff_proj_second, ff_out_second)
        results = pl.pallas_call(
            finish_kernel,
            out_shape=(
                *(jax.ShapeDtypeStruct(w.shape, F32) for w in weights * 4),
                *(jax.ShapeDtypeStruct(w.shape, BF) for w in weights),
                jax.ShapeDtypeStruct(block_out.shape, BF),
                jax.ShapeDtypeStruct(input_grad.shape, F32),
            ),
            in_specs=[VMEM] + [ANY] * 16,
            out_specs=(ANY,) * 22,
            scratch_shapes=[
                pltpu.VMEM(att_shape, BF),
                pltpu.VMEM(ff_shape, BF),
                pltpu.VMEM(att_shape, F32),
                pltpu.VMEM(ff_shape, F32),
                pltpu.VMEM((3, *att_shape), F32),
                pltpu.VMEM((3, *ff_shape), F32),
                pltpu.VMEM(block_out.shape, BF),
                pltpu.VMEM(input_grad.shape, BF),
                pltpu.VMEM(input_grad.shape, F32),
                pltpu.SemaphoreType.DMA((17, 2, 5)),
            ],
            compiler_params=pltpu.CompilerParams(vmem_limit_bytes=56 << 20),
            name="finish",
        )(norm_value, block_out, input_grad, att_total, ff_total, *weights, *firsts_old, *seconds_old)
        return (
            results[20].reshape(tokens.shape),
            results[21].reshape(tokens.shape),
            norm_value[0, :1],
            *results[:20],
        )

    return shards


def solution(mesh):
    act = P("fsdp", "ctx", None)
    table = P("fsdp", None)
    cube = P(None, ("fsdp", "ctx"), "tp")
    flat = P(("fsdp", "ctx"), "tp")
    group = (cube, flat, cube, flat)
    in_specs = (act, act, table, table) + group * 3
    out_specs = (act, act, P()) + group * 5
    return jax.shard_map(
        make_shards(mesh), mesh=mesh, in_specs=in_specs, out_specs=out_specs, check_vma=False
    )
```
